128 devices in a mesh: sfc: 16 (over y, x), grp: 8 (over z, core).
Axes of the slice: x: 4, y: 4, z: 4, core: 2. Of those that a mesh axis runs over, the one named last changes fastest.
Arguments:
- bin_points: float32 [131072, 5, 256], P(('sfc', 'grp')), may hold values from -1 to 1, as said below
- bin_plan: int32 [131072, 1], P(('sfc', 'grp')), may hold values from 0 to 15; in each aligned block of 1024 rows (0 to 1023, 1024 to 2047, ...) at most 128 rows name the same one
- bin_leaf: int32 [131072], P(('sfc', 'grp')), may hold values from 0 to 255
- leaf_slots: int32 [16, 8, 256], P('sfc', None, 'grp'), may hold values from 0 to 255, each once within a row
- box_slots: int32 [16, 8, 32], P('sfc'), may hold values from 0 to 31, each once within a row
- parent_cone: int32 [16, 256], P('sfc'), may hold values from 0 to 15
- box_cone: int32 [16, 32], P('sfc'), may hold values from 0 to 15
- cone_angles: float32 [16, 2], replicated, may hold values from -3.140625 to 3.140625
Outputs:
- leaf_expansions: float32 [32768, 2, 512], P(('sfc', 'grp'))
- level_one: float32 [4096, 2, 512], P(('sfc', 'grp'))
- level_two: float32 [512, 2, 512], P(('sfc', 'grp'))
The draws below stay inside these ranges and needn't reach their ends.
Inputs may be any that keep to these rules, and one draw needn't show every extreme that they name: `bin_plan`: among the rows of one device no value is named by more than 128 rows, a bound that some block reaches. Each row leaf_slots[s, o, :] names every level-one box of segment s once, so every level-one box has exactly one child of each octant. Each row box_slots[s, o, :] names every level-two box of segment s once. `bin_points`: coordinates lie within -1 to 1 and densities within -0.4 to 0.4.
All inputs are finite; a program needn't handle non-finite values.
Results may differ from the reference program's by a relative error of at most 0.0039.
Values sent between devices are 32-bit elements; how exact they have to be, the bound alone decides.
No kernel may reach another device: no remote copies, remote signals or barrier semaphores. Data moves between devices by JAX's collectives and lax.ppermute only.
A program may use at most 320 MiB of HBM per device.

```python
import math
import jax
import jax.numpy as jnp
import numpy as np
from jax import lax

PTS = 256
CONES = 16
BINS_DEV = 1024
LEAF_DEV = 256
CAP = 128
BINS = 131072
PAR1 = 256
PAR2 = 32
N_SFC = 16
N_GRP = 8


def draw_bin_points(key, part):
    coord_key = jax.random.fold_in(key, 11)
    dens_key = jax.random.fold_in(key, 23)
    coords = jax.random.uniform(coord_key, (BINS, 3, PTS), jnp.float32, -1.0, 1.0)
    density = jnp.clip(0.05 * jax.random.normal(dens_key, (BINS, 2, PTS), jnp.float32), -0.4, 0.4)
    return jnp.concatenate([coords, density], axis=1).astype(jnp.float32)


def set_ends(values, rng, least, top_value):
    dims = values.shape
    spot = [jax.random.randint(jax.random.fold_in(rng, axis), (), 0, dims[axis]) for axis in range(len(dims))]
    values = values.at[tuple(spot)].set(least)
    longest = dims.index(max(dims))
    spot[longest] = (spot[longest] + 1) % dims[longest]
    return values.at[tuple(spot)].set(top_value)


def routed_block(own_key, own, number, rows, amount, top, reach, slope):
    ranking = jax.random.permutation(own_key, amount)
    crowded, ordinary = shares(amount, rows * top, reach, slope, True), shares(amount, rows * top, reach, slope, False)
    places = jnp.arange(amount)

    def named(lengths, offset_by):
        used = int((lengths > 0).sum())
        fixed = max(1, used // 4)
        moved = fixed + (places - fixed + offset_by * (used - fixed)) % max(1, amount - fixed)
        return jnp.zeros((amount,), jnp.int32).at[ranking[jnp.where(places < fixed, places, moved)]].set(jnp.asarray(lengths, jnp.int32))

    lengths = jnp.where(number % 4 == 0, named(crowded, number // 4), named(ordinary, number - number // 4 - 1))
    mixed = jax.random.permutation(jax.random.fold_in(own, 3), amount)
    donor, receiver = mixed[0:amount // 2 * 2:2], mixed[1:amount // 2 * 2:2]
    room = jnp.minimum(lengths[donor] - 1, reach - lengths[receiver]) // 2
    room = jnp.where((donor == ranking[0]) | (receiver == ranking[0]) | (lengths[receiver] == 0), 0, jnp.maximum(room, 0))
    moved = jax.random.randint(jax.random.fold_in(own, 4), (amount // 2,), 0, 1 << 20) % (room + 1)
    lengths = lengths.at[donor].add(-moved).at[receiver].add(moved)
    items = jnp.searchsorted(jnp.cumsum(lengths), jnp.arange(rows * top), side="right").astype(jnp.int32)
    table = items.reshape(top, rows).T
    table = table[jax.random.permutation(jax.random.fold_in(own, 1), rows)]
    offset_by = jax.random.randint(jax.random.fold_in(own, 2), (rows, 1), 0, top)
    return jnp.take_along_axis(table, (jnp.arange(top)[None, :] + offset_by) % top, axis=1)


def shares(amount, total, reach, skew, full):
    portions = [(1 << 20) // math.isqrt(rank ** skew) + 1 for rank in range(1, amount + 1)]
    largest = reach if full else min(reach, max(-(-total // amount), total * portions[0] // sum(portions)))
    least = 1 if total - largest >= amount - 1 else 0
    counts, rest = [largest] + [least] * (amount - 1), total - largest - least * (amount - 1)
    while rest > 0:
        candidates = [i for i in range(1, amount) if counts[i] < largest] or [i for i in range(1, amount) if counts[i] < reach]
        mass, remaining = sum([portions[i] for i in candidates]), rest
        for i in candidates:
            addition = min(reach - counts[i], max(1, remaining * portions[i] // mass), rest)
            counts[i] = counts[i] + addition
            rest = rest - addition
    return np.array(counts)


def setup_inputs(seed: int = 0) -> dict:
    arg_keys = jax.random.split(jax.random.key(seed), 9)
    bin_points = draw_bin_points(jax.random.fold_in(arg_keys[8], 71), 0)
    bin_plan_keys = jax.random.split(jax.random.fold_in(arg_keys[1], 1), BINS // BINS_DEV)
    bin_plan_turns = jax.random.permutation(jax.random.fold_in(arg_keys[1], 3), BINS // BINS_DEV)
    bin_plan = jax.vmap(lambda own, number: routed_block(jax.random.fold_in(arg_keys[1], 2), own, number, BINS_DEV, N_SFC, 1, CAP, 2))(bin_plan_keys, bin_plan_turns).reshape((BINS, 1))
    bin_leaf = set_ends(jax.random.randint(arg_keys[2], (BINS,), 0, LEAF_DEV), jax.random.fold_in(arg_keys[2], 1), 0, LEAF_DEV - 1).astype(jnp.int32)
    leaf_slots = jax.vmap(lambda own: jax.random.permutation(own, PAR1))(jax.random.split(arg_keys[3], N_SFC * 8)).reshape((N_SFC, 8, PAR1)).astype(jnp.int32)
    box_slots = jax.vmap(lambda own: jax.random.permutation(own, PAR2))(jax.random.split(arg_keys[4], N_SFC * 8)).reshape((N_SFC, 8, PAR2)).astype(jnp.int32)
    parent_cone = set_ends(jax.random.randint(arg_keys[5], (N_SFC, PAR1), 0, CONES), jax.random.fold_in(arg_keys[5], 1), 0, CONES - 1).astype(jnp.int32)
    box_cone = set_ends(jax.random.randint(arg_keys[6], (N_SFC, PAR2), 0, CONES), jax.random.fold_in(arg_keys[6], 1), 0, CONES - 1).astype(jnp.int32)
    cone_angles = jnp.clip(jax.random.uniform(arg_keys[7], (CONES, 2), jnp.float32, -3.140625, 3.140625), -3.140625, 3.140625)
    return {"bin_points": bin_points, "bin_plan": bin_plan, "bin_leaf": bin_leaf, "leaf_slots": leaf_slots, "box_slots": box_slots, "parent_cone": parent_cone, "box_cone": box_cone, "cone_angles": cone_angles}


kappa_leaf = 2.0
kappa_box = 4.0


def cheb_nodes():
    return np.cos((2.0 * np.arange(8) + 1.0) * np.pi / 16.0)


def lagrange(values):
    nodes = cheb_nodes()
    rows = []
    for center in range(8):
        weight = jnp.ones_like(values)
        for other in range(8):
            if other != center:
                weight = weight * ((values - float(nodes[other])) / float(nodes[center] - nodes[other]))
        rows.append(weight)
    return jnp.stack(rows, axis=-2)


def bin_expansions(points):
    count = points.shape[0]
    width = points.shape[2]
    basis = lagrange(points[:, 0:3])
    weighted = (points[:, 3:5, None, :] * basis[:, 0][:, None]).astype(jnp.bfloat16).reshape(count, 16, width)
    pair = (basis[:, 1][:, :, None, :] * basis[:, 2][:, None, :, :]).astype(jnp.bfloat16).reshape(count, 64, width)
    result = jnp.einsum("bcp,bqp->bcq", weighted.astype(jnp.float32), pair.astype(jnp.float32))
    return result.reshape(count, 2, 512)


def child_axes(octant):
    bits = [octant // 4, (octant // 2) % 2, octant % 2]
    nodes = cheb_nodes()
    return np.stack([0.5 * (2 * bit - 1) + 0.5 * nodes for bit in bits])


def child_matrix(octant):
    axes = child_axes(octant)
    first = lagrange(jnp.asarray(axes[0]).astype(jnp.float32))
    second = lagrange(jnp.asarray(axes[1]).astype(jnp.float32))
    third = lagrange(jnp.asarray(axes[2]).astype(jnp.float32))
    return jnp.einsum("ad,be,cf->abcdef", first, second, third).reshape(512, 512)


def node_phase(dirs, kappa, axes):
    first = jnp.asarray(axes[0]).astype(jnp.float32)
    second = jnp.asarray(axes[1]).astype(jnp.float32)
    third = jnp.asarray(axes[2]).astype(jnp.float32)
    angle = (dirs[:, 0, None, None, None] * first[None, :, None, None]
             + dirs[:, 1, None, None, None] * second[None, None, :, None]
             + dirs[:, 2, None, None, None] * third[None, None, None, :])
    angle = kappa * angle.reshape(dirs.shape[0], 512)
    return jnp.cos(angle), jnp.sin(angle)


def rotate(field, cosine, sine):
    real_part = field[:, 0]
    imag_part = field[:, 1]
    return jnp.stack([real_part * cosine - imag_part * sine, real_part * sine + imag_part * cosine], axis=1)


def cone_vectors(cone_angles):
    azimuth = cone_angles[:, 0]
    polar = cone_angles[:, 1]
    return jnp.stack([jnp.cos(azimuth) * jnp.sin(polar), jnp.sin(azimuth) * jnp.sin(polar), jnp.cos(polar)], axis=1)


def level_term(children, dirs, octant, kappa):
    cosine, sine = node_phase(dirs, kappa, child_axes(octant))
    turned = rotate(children, cosine, sine)
    matrix = child_matrix(octant)
    moved = jnp.dot(turned.reshape(-1, 512), matrix.T, preferred_element_type=jnp.float32, precision=lax.Precision.HIGHEST)
    return moved.reshape(children.shape[0], 2, 512)


def parent_turn(field, dirs, kappa):
    nodes = cheb_nodes()
    cosine, sine = node_phase(dirs, -kappa, np.stack([nodes, nodes, nodes]))
    return rotate(field, cosine, sine)


def level(children, slots, cones, directions, kappa, count):
    segments = children.shape[0]
    total = jnp.zeros((segments, count, 2, 512), jnp.float32)
    parent_dirs = directions[cones]
    seg_index = jnp.arange(segments, dtype=jnp.int32)[:, None]
    for octant in range(8):
        rows = children[:, octant::8]
        parents = slots[:, octant, :]
        child_dirs = jnp.take_along_axis(parent_dirs, parents[:, :, None], axis=1)
        term = level_term(rows.reshape(-1, 2, 512), child_dirs.reshape(-1, 3), octant, kappa)
        total = total.at[seg_index, parents].add(term.reshape(segments, count, 2, 512))
    turned = parent_turn(total.reshape(-1, 2, 512), parent_dirs.reshape(-1, 3), kappa)
    return turned.reshape(segments, count, 2, 512)


def reference(bin_points, bin_plan, bin_leaf, leaf_slots, box_slots, parent_cone, box_cone, cone_angles):
    total = bin_points.shape[0]
    width = bin_points.shape[2]
    block = math.gcd(total, 128)
    terms = lax.map(bin_expansions, bin_points.reshape(total // block, block, 5, width)).reshape(total, 2, 512)
    device = jnp.arange(total, dtype=jnp.int32) // BINS_DEV
    group = device % N_GRP
    leaf_index = (bin_plan[:, 0] * N_GRP + group) * LEAF_DEV + bin_leaf
    leaves = jax.ops.segment_sum(terms, leaf_index, num_segments=N_SFC * N_GRP * LEAF_DEV)
    directions = cone_vectors(cone_angles)
    children = leaves.reshape(N_SFC, N_GRP * LEAF_DEV, 2, 512)
    first_level = level(children, leaf_slots, parent_cone, directions, kappa_leaf, PAR1)
    second_level = level(first_level, box_slots, box_cone, directions, kappa_box, PAR2)
    return leaves, first_level.reshape(-1, 2, 512), second_level.reshape(-1, 2, 512)
```

```python
import functools

import jax
import jax.numpy as jnp
import numpy as np
from jax import lax
from jax.experimental import pallas as pl
from jax.experimental.pallas import tpu as pltpu
from jax.sharding import PartitionSpec as P

kappa_leaf = 2.0
kappa_box = 4.0
f32 = jnp.float32
i32 = jnp.int32
VMEM = pl.BlockSpec(memory_space=pltpu.VMEM)
SMEM = pl.BlockSpec(memory_space=pltpu.SMEM)


def cheb_nodes():
    return np.cos((2.0 * np.arange(8) + 1.0) * np.pi / 16.0)


def lagrange_np(values):
    nodes = cheb_nodes()
    rows = []
    for center in range(8):
        weight = np.ones_like(values)
        for other in range(8):
            if other != center:
                weight = weight * (values - nodes[other]) / (nodes[center] - nodes[other])
        rows.append(weight)
    return np.stack(rows, axis=0)


def child_axis(bit):
    return 0.5 * (2 * bit - 1) + 0.5 * cheb_nodes()


def axis_maps():
    return np.stack([lagrange_np(child_axis(bit)) for bit in range(2)])


def tile_of_nodes(first, second, third):
    rows = np.arange(8)[:, None]
    lanes = np.arange(128)[None, :]
    a = 2 * (rows // 2) + lanes // 64
    b = lanes % 64 // 8 + 0 * rows
    c = lanes % 8 + 0 * rows
    return np.stack([first[a], second[b], third[c]])


def lane_maps():
    maps = axis_maps()
    out = []
    for pick in range(4):
        both = np.kron(maps[pick // 2], maps[pick % 2])
        out.append(np.kron(np.eye(2), both).T)
    return np.stack(out).astype(np.float32)


def row_maps():
    maps = axis_maps()
    rows = np.arange(8)[:, None]
    half = np.arange(128)[None, :] // 64
    k = rows // 2
    out = np.zeros((2, 8, 8, 128), np.float32)
    for bit in range(2):
        for step in range(4):
            for flip in range(2):
                to = 2 * k + half
                frm = 2 * ((k + step) % 4) + (half ^ flip)
                out[bit, 2 * step + flip] = maps[bit][to, frm]
    return out


def basis(x):
    t = cheb_nodes()[:4]
    sq = t * t
    x2 = x * x
    s = [x2 - float(v) for v in sq]
    p01 = s[0] * s[1]
    p23 = s[2] * s[3]
    rest = [s[1] * p23, s[0] * p23, p01 * s[3], p01 * s[2]]
    out = [None] * 8
    for j in range(4):
        scale = 1.0 / (np.prod([sq[j] - sq[i] for i in range(4) if i != j]) * 2.0 * t[j])
        q = rest[j] * float(scale)
        out[j] = q * (x + float(t[j]))
        out[7 - j] = q * (float(t[j]) - x)
    return out


def lanes_of(shape):
    return lax.broadcasted_iota(i32, shape, len(shape) - 1)


def expand_kernel(plan, leaf, codes, pts, *refs):
    outs = refs[:4]
    held, bx, by, bz, dens, count, sems = refs[4:]
    step = pl.program_id(0)
    block = pts.shape[1]
    dests = held.shape[0]
    cap = held.shape[1] - 1
    row = lax.broadcasted_iota(i32, (8, 128), 0)
    spot = jnp.where(row == 0, lanes_of((8, 128)), -1)

    @pl.when(step == 0)
    def _():
        for d in range(dests):
            count[d] = 0
            held[d, cap] = jnp.full((8, 128), 256.0, f32)

    def group(g, carry):
        base = pl.multiple_of(g * 8, 8)
        for axis, ref in ((0, bx), (1, by), (2, bz)):
            values = basis(pts[axis, pl.ds(base, 8), :])
            for a in range(8):
                for h in range(2):
                    ref[h, pl.ds(8 * a, 8), :] = values[a][:, 128 * h : 128 * h + 128]
        for part in range(2):
            values = pts[3 + part, pl.ds(base, 8), :]
            for h in range(2):
                dens[2 * part + h] = values[:, 128 * h : 128 * h + 128]
        for i in range(8):
            weighted, pair = [], []
            for h in range(2):
                lx = bx[h, pl.ds(i, 8, stride=8), :]
                lz = bz[h, pl.ds(i, 8, stride=8), :]
                re, im = (
                    jnp.broadcast_to(dens[2 * part + h, pl.ds(i, 1), :], lx.shape)
                    for part in range(2)
                )
                weighted.append(jnp.concatenate([re * lx, im * lx], axis=0).astype(jnp.bfloat16))
                pair.append(
                    jnp.concatenate(
                        [
                            jnp.broadcast_to(by[h, pl.ds(8 * b + i, 1), :], lz.shape) * lz
                            for b in range(8)
                        ],
                        axis=0,
                    ).astype(jnp.bfloat16)
                )
            res = lax.dot_general(
                jnp.concatenate(weighted, axis=1),
                jnp.concatenate(pair, axis=1),
                (((1,), (1,)), ((), ())),
                preferred_element_type=f32,
            )
            number = step * block + base + i
            d = codes[plan[number]]
            c = count[d]
            count[d] = c + 1
            held[d, c] = jnp.concatenate([res[:8], res[8:]], axis=1)
            held[d, cap] = jnp.where(spot == c, leaf[number].astype(f32), held[d, cap])
        return carry

    lax.fori_loop(0, block // 8, group, 0)

    @pl.when(step == pl.num_programs(0) - 1)
    def _():
        for d in range(dests):
            held[d, cap] = jnp.where(row == 1, count[d].astype(f32), held[d, cap])
        copies = [
            pltpu.make_async_copy(held.at[pl.ds(4 * k, 4)], outs[k], sems.at[k]) for k in range(4)
        ]
        for copy in copies:
            copy.start()
        for copy in copies:
            copy.wait()


def expand(plan, leaf, codes, pts, dests, cap):
    bins, width = pts.shape[1], pts.shape[2]
    block = 128
    return pl.pallas_call(
        expand_kernel,
        out_shape=[jax.ShapeDtypeStruct((dests // 4, cap + 1, 8, 128), f32)] * 4,
        grid_spec=pltpu.PrefetchScalarGridSpec(
            num_scalar_prefetch=3,
            grid=(bins // block,),
            in_specs=[pl.BlockSpec((5, block, width), lambda i, *_: (0, i, 0))],
            out_specs=[pl.BlockSpec(memory_space=pl.ANY)] * 4,
            scratch_shapes=[
                pltpu.VMEM((dests, cap + 1, 8, 128), f32),
                pltpu.VMEM((2, 64, 128), f32),
                pltpu.VMEM((2, 64, 128), f32),
                pltpu.VMEM((2, 64, 128), f32),
                pltpu.VMEM((4, 8, 128), f32),
                pltpu.SMEM((dests,), i32),
                pltpu.SemaphoreType.DMA((4,)),
            ],
        ),
        compiler_params=pltpu.CompilerParams(dimension_semantics=("arbitrary",)),
        name="expand",
    )(plan, leaf, codes, pts)


def gather_kernel(*refs):
    arrived, outs = refs[:4], refs[4:8]
    labels, names, sem = refs[8:]
    cap = arrived[0].shape[1] - 1
    for k in range(4):
        for m in range(4):
            labels[pl.ds(8 * (4 * k + m), 8), :] = arrived[k][m, cap].astype(i32)
    copy = pltpu.make_async_copy(labels, names, sem)
    copy.start()
    for out in outs:
        out[...] = jnp.zeros(out.shape, f32)
    copy.wait()
    for k in range(4):
        most = names[8 * 4 * k + 1, 0]
        for m in range(1, 4):
            most = jnp.maximum(most, names[8 * (4 * k + m) + 1, 0])

        def rows4(r, carry):
            for u in range(4):
                for m in range(4):
                    slot = r * 4 + u
                    where = names[8 * (4 * k + m), slot]
                    outs[m][where] = outs[m][where] + arrived[k][m, slot]
            return carry

        lax.fori_loop(0, (most + 3) // 4, rows4, 0)


def gather(arrived, leaf_count):
    return pl.pallas_call(
        gather_kernel,
        out_shape=[jax.ShapeDtypeStruct((leaf_count + 1, 8, 128), f32)] * 4,
        in_specs=[VMEM] * 4,
        out_specs=[VMEM] * 4,
        scratch_shapes=[
            pltpu.VMEM((128, 128), i32),
            pltpu.SMEM((128, 128), i32),
            pltpu.SemaphoreType.DMA(()),
        ],
        name="gather",
    )(*arrived)


def rows_of(shape):
    return lax.broadcasted_iota(i32, shape, len(shape) - 2)


def swap_rows(t):
    even = rows_of(t.shape) % 2 == 0
    axis = len(t.shape) - 2
    return jnp.where(even, pltpu.roll(t, 7, axis), pltpu.roll(t, 1, axis))


def spin(t, cosine, sine):
    return t * cosine + swap_rows(t) * sine


def row_mix(t, maps, bit):
    flipped = pltpu.roll(t, 64, 2)
    total = None
    for step in range(4):
        for flip in range(2):
            part = flipped if flip else t
            if step:
                part = pltpu.roll(part, 8 - 2 * step, 1)
            term = part * maps[bit, 2 * step + flip]
            total = term if total is None else total + term
    return total


def levels_kernel(
    slots, boxes, cones, box_cones, a0, a1, a2, a3, e0c, e0s, e1c, e1s, e2c, e2s, lanes, rows,
    leaves, partial, turned,
):
    owned = partial.shape[1] * 8 // 9
    upper = partial.shape[1] - owned
    partial[...] = jnp.zeros(partial.shape, f32)
    step = 32
    shape = (step, 8, 128)
    own = rows_of(shape) % 2 == lanes_of(shape) // 64

    def settle(n, carry):
        base = pl.multiple_of(n * step, step)
        t = (a0[pl.ds(base, step)] + a1[pl.ds(base, step)]) + (
            a2[pl.ds(base, step)] + a3[pl.ds(base, step)]
        )
        leaves[pl.ds(base, step)] = jnp.where(own, t, swap_rows(pltpu.roll(t, 64, 2)))
        return carry

    lax.fori_loop(0, leaves.shape[0] // step, settle, 0)

    for o in range(8):
        count = leaves.shape[0] // 8
        for j in range(count):
            e = cones[slots[o, j]] * 8 + o
            turned[j] = spin(leaves[8 * j + o], e0c[e], e0s[e])
        mixed = jnp.dot(
            turned[...].reshape(count * 8, 128), lanes[o % 4],
            precision=lax.Precision.HIGHEST, preferred_element_type=f32,
        ).reshape(count, 8, 128)
        turned[...] = row_mix(mixed, rows, o // 4)
        for j in range(count):
            p = slots[o, j]
            q, r = p // owned, p % owned
            partial[q, r] = partial[q, r] + turned[j]

    for o in range(8):
        count = boxes.shape[1]
        for j in range(count):
            p = 8 * j + o
            cone = cones[p]
            e = box_cones[boxes[o, j]] * 8 + o
            t = spin(partial[p // owned, p % owned], e1c[cone], e1s[cone])
            turned[j] = spin(t, e2c[e], e2s[e])
        mixed = jnp.dot(
            turned[...].reshape(count * 8, 128), lanes[o % 4],
            precision=lax.Precision.HIGHEST, preferred_element_type=f32,
        ).reshape(count, 8, 128)
        turned[...] = row_mix(mixed, rows, o // 4)
        for j in range(count):
            p = boxes[o, j]
            q, r = p // upper, owned + p % upper
            partial[q, r] = partial[q, r] + turned[j]


def close_kernel(first, second, cones, box_cones, got, e1c, e1s, e3c, e3s, out_one, out_two):
    owned = out_one.shape[0]
    for n in range(got.shape[1]):
        t = got[0, n]
        for s in range(1, got.shape[0]):
            t = t + got[s, n]
        if n < owned:
            e = cones[first[0] + n]
            out_one[n] = spin(t, e1c[e], e1s[e])
        else:
            e = box_cones[second[0] + n - owned]
            out_two[n - owned] = spin(t, e3c[e], e3s[e])


def phase_tables(directions, kappa, places):
    grid = jnp.asarray(places.astype(np.float32))
    angle = (
        directions[:, 0, None, None, None] * grid[None, :, 0]
        + directions[:, 1, None, None, None] * grid[None, :, 1]
        + directions[:, 2, None, None, None] * grid[None, :, 2]
    )
    angle = (kappa * angle).reshape(-1, 8, 128)
    sign = jnp.where(lax.broadcasted_iota(i32, (1, 8, 128), 1) % 2 == 0, -1.0, 1.0).astype(f32)
    return jnp.cos(angle), jnp.sin(angle) * sign


def to_nodes(tiles):
    count = tiles.shape[0]
    return tiles.reshape(count, 4, 2, 128).transpose(0, 2, 1, 3).reshape(count, 2, 512)


def cone_vectors(cone_angles):
    azimuth = cone_angles[:, 0]
    polar = cone_angles[:, 1]
    return jnp.stack(
        [jnp.cos(azimuth) * jnp.sin(polar), jnp.sin(azimuth) * jnp.sin(polar), jnp.cos(polar)],
        axis=1,
    )


def hop(x, shift, leg, groups):
    pairs = []
    for s in range(16):
        for g in range(groups):
            y, x0 = s // 4, s % 4
            if g % 2 == leg:
                x0 = (x0 + shift) % 4
            else:
                y = (y + shift) % 4
            pairs.append((s * groups + g, (4 * y + x0) * groups + g))
    return lax.ppermute(x, ("sfc", "grp"), pairs)


def per_device(
    bin_points, bin_plan, bin_leaf, leaf_slots, box_slots, parent_cone, box_cone, cone_angles
):
    peers = lax.axis_size("sfc")
    groups = lax.axis_size("grp")
    rank = lax.axis_index("grp")
    cap = bin_points.shape[0] // 8
    leaf_count = leaf_slots.shape[2] * 8
    first_owned = parent_cone.shape[1] // groups
    second_owned = box_cone.shape[1] // groups

    here = lax.axis_index("sfc")
    there = jnp.arange(peers, dtype=i32)
    along_x, along_y = (there - here) % 4, (there // 4 - here // 4) % 4
    codes = jnp.where(rank % 2 == 0, 4 * along_x + along_y, 4 * along_y + along_x)
    sent = expand(
        bin_plan[:, 0], bin_leaf, codes, jnp.transpose(bin_points, (1, 0, 2)), peers, cap
    )
    arrived = [sent[0]] + [hop(sent[k], k, 0, groups) for k in range(1, 4)]
    held = gather(arrived, leaf_count)
    held = [held[0]] + [hop(held[m], m, 1, groups) for m in range(1, 4)]

    directions = cone_vectors(cone_angles)
    child = np.stack(
        [
            tile_of_nodes(child_axis(o // 4), child_axis(o // 2 % 2), child_axis(o % 2))
            for o in range(8)
        ]
    )
    nodes = cheb_nodes()
    parent = tile_of_nodes(nodes, nodes, nodes)[None]
    e0c, e0s = phase_tables(directions, kappa_leaf, child)
    e1c, e1s = phase_tables(directions, -kappa_leaf, parent)
    e2c, e2s = phase_tables(directions, kappa_box, child)
    e3c, e3s = phase_tables(directions, -kappa_box, parent)

    leaves, partial = pl.pallas_call(
        levels_kernel,
        out_shape=(
            jax.ShapeDtypeStruct((leaf_count, 8, 128), f32),
            jax.ShapeDtypeStruct((groups, first_owned + second_owned, 8, 128), f32),
        ),
        in_specs=[SMEM] * 4 + [VMEM] * 12,
        out_specs=(VMEM, VMEM),
        scratch_shapes=[
            pltpu.VMEM((leaf_count // 8, 8, 128), f32),
        ],
        name="levels",
    )(
        leaf_slots[0], box_slots[0], parent_cone[0], box_cone[0], *held,
        e0c, e0s, e1c, e1s, e2c, e2s, jnp.asarray(lane_maps()), jnp.asarray(row_maps()),
    )
    got = lax.all_to_all(partial, "grp", split_axis=0, concat_axis=0, tiled=True)
    one, two = pl.pallas_call(
        close_kernel,
        out_shape=(
            jax.ShapeDtypeStruct((first_owned, 8, 128), f32),
            jax.ShapeDtypeStruct((second_owned, 8, 128), f32),
        ),
        in_specs=[SMEM] * 4 + [VMEM] * 5,
        out_specs=(VMEM, VMEM),
        name="close",
    )(
        (rank * first_owned)[None], (rank * second_owned)[None], parent_cone[0], box_cone[0],
        got, e1c, e1s, e3c, e3s,
    )
    return (to_nodes(leaves), to_nodes(one), to_nodes(two))


def solution(mesh):
    placed = (
        P(("sfc", "grp"), None, None),
        P(("sfc", "grp"), None),
        P(("sfc", "grp")),
        P("sfc", None, "grp"),
        P("sfc", None, None),
        P("sfc", None),
        P("sfc", None),
        P(),
    )
    return jax.shard_map(
        per_device,
        mesh=mesh,
        in_specs=placed,
        out_specs=(
            P(("sfc", "grp"), None, None),
            P(("sfc", "grp"), None, None),
            P(("sfc", "grp"), None, None),
        ),
        check_vma=False,
    )
```

```python
import functools

import jax
import jax.numpy as jnp
import numpy as np
from jax import lax
from jax.experimental import pallas as pl
from jax.experimental.pallas import tpu as pltpu
from jax.sharding import PartitionSpec as P

kappa_leaf = 2.0
kappa_box = 4.0
f32 = jnp.float32
i32 = jnp.int32
VMEM = pl.BlockSpec(memory_space=pltpu.VMEM)
SMEM = pl.BlockSpec(memory_space=pltpu.SMEM)


def cheb_nodes():
    return np.cos((2.0 * np.arange(8) + 1.0) * np.pi / 16.0)


def lagrange_np(values):
    nodes = cheb_nodes()
    rows = []
    for center in range(8):
        weight = np.ones_like(values)
        for other in range(8):
            if other != center:
                weight = weight * (values - nodes[other]) / (nodes[center] - nodes[other])
        rows.append(weight)
    return np.stack(rows, axis=0)


def child_axis(bit):
    return 0.5 * (2 * bit - 1) + 0.5 * cheb_nodes()


def axis_maps():
    return np.stack([lagrange_np(child_axis(bit)) for bit in range(2)])


def tile_of_nodes(first, second, third):
    rows = np.arange(8)[:, None]
    lanes = np.arange(128)[None, :]
    a = 2 * (rows // 2) + lanes // 64
    b = lanes % 64 // 8 + 0 * rows
    c = lanes % 8 + 0 * rows
    return np.stack([first[a], second[b], third[c]])


def lane_maps():
    maps = axis_maps()
    out = []
    for pick in range(4):
        both = np.kron(maps[pick // 2], maps[pick % 2])
        out.append(np.kron(np.eye(2), both).T)
    return np.stack(out).astype(np.float32)


def row_maps():
    maps = axis_maps()
    rows = np.arange(8)[:, None]
    half = np.arange(128)[None, :] // 64
    k = rows // 2
    out = np.zeros((2, 8, 8, 128), np.float32)
    for bit in range(2):
        for step in range(4):
            for flip in range(2):
                to = 2 * k + half
                frm = 2 * ((k + step) % 4) + (half ^ flip)
                out[bit, 2 * step + flip] = maps[bit][to, frm]
    return out


def basis(x):
    t = cheb_nodes()[:4]
    sq = t * t
    x2 = x * x
    s = [x2 - float(v) for v in sq]
    p01 = s[0] * s[1]
    p23 = s[2] * s[3]
    rest = [s[1] * p23, s[0] * p23, p01 * s[3], p01 * s[2]]
    out = [None] * 8
    for j in range(4):
        scale = 1.0 / (np.prod([sq[j] - sq[i] for i in range(4) if i != j]) * 2.0 * t[j])
        q = rest[j] * float(scale)
        out[j] = q * (x + float(t[j]))
        out[7 - j] = q * (float(t[j]) - x)
    return out


def lanes_of(shape):
    return lax.broadcasted_iota(i32, shape, len(shape) - 1)


def lanes_of(shape):
    return lax.broadcasted_iota(i32, shape, len(shape) - 1)


CHUNKS = ((2,), (1, 3), (0,))
ORDER = tuple(m for chunk in CHUNKS for m in chunk)


def route_kernel(here, plan, leaf, table, labels, picked, scaled):
    bf16 = jnp.bfloat16
    cap = labels.shape[2]
    target = plan[...]
    names = leaf[...].astype(f32)
    along_x = (target - here[0]) % 4
    along_y = (target // 4 - here[1]) % 4
    first = jnp.where(here[2] == 0, along_x, along_y)
    second = jnp.where(here[2] == 0, along_y, along_x)
    place, lead, width = target * 0, target * 0, target * 0
    for chunk in CHUNKS:
        for n, m in enumerate(chunk):
            hit = second == m
            place = jnp.where(hit, ORDER.index(m), place)
            lead = jnp.where(hit, n, lead)
            width = jnp.where(hit, len(chunk), width)
    code = place * 4 + first
    for d in range(16):
        hit = (code == d).astype(f32)
        picked[pl.ds(8 * d, 8), :] = hit
        scaled[pl.ds(8 * d, 8), :] = hit * names
    square = (128, 128)
    row, lane = rows_of(square), lanes_of(square)
    hits = picked[...].astype(bf16)
    ones = jnp.ones(square, bf16)

    def mul(a, b):
        return jnp.dot(a.astype(bf16), b.astype(bf16), preferred_element_type=f32)

    inside = mul(hits, (row < lane).astype(f32))
    ahead = mul(mul((lane < row).astype(f32), hits), ones)
    same = mul(mul(((lane < row) & (lane // 8 == row // 8)).astype(f32), hits), ones)
    order = jnp.zeros((8, 128), f32)
    slot = jnp.zeros((8, 128), f32)
    for d in range(16):
        part = slice(8 * d, 8 * d + 8)
        hit = picked[pl.ds(8 * d, 8), :]
        order = order + hit * (inside[part] + ahead[part])
        slot = slot + hit * (inside[part] + same[part])
    goal_hi = (first * width + lead).astype(f32)
    count = order.shape[0] * 128
    ranks = lax.broadcasted_iota(i32, (count, 128), 0).astype(f32)
    seats = row.astype(f32)
    sub = lax.broadcasted_iota(i32, (8, 128), 0)
    lane_f = lanes_of((8, 128)).astype(f32)
    found = jnp.zeros((8, count), f32)
    marks = jnp.zeros((32, 128), f32)
    nt = (((1,), (1,)), ((), ()))
    for r in range(8):
        at = jnp.broadcast_to(order[r : r + 1, :], (count, 128)) == ranks
        goal = jnp.broadcast_to(goal_hi[r : r + 1, :], (8, 128))
        seat = jnp.broadcast_to(slot[r : r + 1, :], (8, 128))
        values = jnp.where(
            sub == 0, float(r), jnp.where(sub == 1, lane_f, jnp.where(sub == 2, goal, seat))
        )
        found = found + lax.dot_general(
            values.astype(bf16), at.astype(f32).astype(bf16), nt, preferred_element_type=f32
        )
        both = jnp.concatenate(
            [scaled[pl.ds(r, 16, stride=8), :], picked[pl.ds(r, 16, stride=8), :]], axis=0
        )
        sits = jnp.broadcast_to(slot[r : r + 1, :], square) == seats
        marks = marks + lax.dot_general(
            both.astype(bf16), sits.astype(f32).astype(bf16), nt, preferred_element_type=f32
        )
    table[0:1, :] = (found[0:1] * 128.0 + found[1:2]).astype(i32)
    table[1:2, :] = (found[2:3] * float(cap_rows(cap)) + found[3:4]).astype(i32)
    lane_w = lanes_of((1, count))
    ends = jnp.zeros((1, count), f32)
    for q in range(4):
        upto = jnp.sum((place <= q).astype(f32), keepdims=True)
        ends = jnp.where(lane_w == q, jnp.broadcast_to(upto, (1, count)), ends)
    table[2:3, :] = ends.astype(i32)
    label = marks[:16] + 256.0 * (1.0 - marks[16:])
    for d in range(16):
        total = jnp.sum(marks[16 + d : 17 + d], axis=1, keepdims=True)
        labels[d] = jnp.where(
            sub == 0,
            jnp.broadcast_to(label[d : d + 1], (8, 128)),
            jnp.broadcast_to(total, (8, 128)),
        )


def cap_rows(cap):
    return cap + 1


def route(here, plan, leaf):
    bins = plan.shape[0]
    return pl.pallas_call(
        route_kernel,
        out_shape=(
            jax.ShapeDtypeStruct((3, bins), i32),
            jax.ShapeDtypeStruct((16, 8, 128), f32),
        ),
        in_specs=[SMEM, VMEM, VMEM],
        out_specs=(VMEM, VMEM),
        scratch_shapes=[pltpu.VMEM((128, 128), f32)] * 2,
        name="route",
    )(here, plan.reshape(bins // 128, 128), leaf.reshape(bins // 128, 128))


UNROLL = 16


def expand_kernel(chunk, table, labels, pts, *refs):
    outs = refs[:4]
    held, all_pts, stage, bx, by, bz, sems, load_sems = refs[4:]
    first = sum(len(c) for c in CHUNKS[:chunk])
    wide = len(CHUNKS[chunk])
    rows = outs[0].shape[1]
    cap = rows - 1
    bins = all_pts.shape[2]
    loads = [
        pltpu.make_async_copy(
            pts.at[axis, :, pl.ds(128 * h, 128)], all_pts.at[axis, h], load_sems.at[2 * axis + h]
        )
        for axis in range(5)
        for h in range(2)
    ]
    for load in loads:
        load.start()
    for k in range(4):
        for n in range(wide):
            held[(k * wide + n) * rows + cap] = labels[4 * (first + n) + k]
    begin = table[2, first - 1] if first else 0
    end = table[2, first + wide - 1]
    for load in loads:
        load.wait()

    def group(g, carry):
        base = begin + g * UNROLL
        for u in range(UNROLL):
            number = table[0, jnp.minimum(base + u, bins - 1)]
            for axis in range(5):
                for h in range(2):
                    stage[axis, h, pl.ds(u, 1), :] = all_pts[axis, h, pl.ds(number, 1), :]
        for axis, ref in ((0, bx), (1, by), (2, bz)):
            for h in range(2):
                values = basis(stage[axis, h])
                for a in range(8):
                    ref[h, pl.ds(UNROLL * a, UNROLL), :] = values[a]
        for u in range(UNROLL):
            weighted, pair = [], []
            for h in range(2):
                lx = bx[h, pl.ds(u, 8, stride=UNROLL), :]
                lz = bz[h, pl.ds(u, 8, stride=UNROLL), :]
                re, im = (
                    jnp.broadcast_to(stage[3 + part, h, pl.ds(u, 1), :], lx.shape)
                    for part in range(2)
                )
                weighted.append(jnp.concatenate([re * lx, im * lx], axis=0).astype(jnp.bfloat16))
                pair.append(
                    jnp.concatenate(
                        [
                            jnp.broadcast_to(by[h, pl.ds(UNROLL * b + u, 1), :], lz.shape) * lz
                            for b in range(8)
                        ],
                        axis=0,
                    ).astype(jnp.bfloat16)
                )
            res = lax.dot_general(
                jnp.concatenate(weighted, axis=1),
                jnp.concatenate(pair, axis=1),
                (((1,), (1,)), ((), ())),
                preferred_element_type=f32,
            )
            spot = jnp.minimum(base + u, bins - 1)
            goal = jnp.where(base + u < end, table[1, spot], held.shape[0] - 1)
            held[goal] = jnp.concatenate([res[:8], res[8:]], axis=1)
        return carry

    lax.fori_loop(0, (end - begin + UNROLL - 1) // UNROLL, group, 0)
    copies = []
    for k in range(4):
        for n in range(wide):
            copies.append(
                pltpu.make_async_copy(
                    held.at[pl.ds((k * wide + n) * rows, rows)], outs[k].at[n], sems.at[k, n]
                )
            )
    for copy in copies:
        copy.start()
    for copy in copies:
        copy.wait()


def expand(chunk, table, labels, pts, cap):
    bins = pts.shape[1]
    wide = len(CHUNKS[chunk])
    return pl.pallas_call(
        functools.partial(expand_kernel, chunk),
        out_shape=[jax.ShapeDtypeStruct((wide, cap + 1, 8, 128), f32)] * 4,
        in_specs=[SMEM, VMEM, pl.BlockSpec(memory_space=pl.ANY)],
        out_specs=[pl.BlockSpec(memory_space=pl.ANY)] * 4,
        scratch_shapes=[
            pltpu.VMEM((4 * wide * (cap + 1) + 1, 8, 128), f32),
            pltpu.VMEM((5, 2, bins, 128), f32),
            pltpu.VMEM((5, 2, UNROLL, 128), f32),
            pltpu.VMEM((2, 8 * UNROLL, 128), f32),
            pltpu.VMEM((2, 8 * UNROLL, 128), f32),
            pltpu.VMEM((2, 8 * UNROLL, 128), f32),
            pltpu.SemaphoreType.DMA((4, wide)),
            pltpu.SemaphoreType.DMA((10,)),
        ],
        cost_estimate=pl.CostEstimate(
            flops=wide * (1 << 28), bytes_accessed=1 << 23, transcendentals=0
        ),
        name="expand",
    )(table, labels, pts)


def gather_kernel(wide, *refs):
    arrived, outs = refs[:4], refs[4 : 4 + wide]
    held, labels, names, sem, sems = refs[4 + wide :]
    cap = held.shape[2] - 1
    loads = [pltpu.make_async_copy(arrived[k], held.at[k], sems.at[k]) for k in range(4)]
    for load in loads:
        load.start()
    for out in outs:
        out[...] = jnp.zeros(out.shape, f32)
    for load in loads:
        load.wait()
    for k in range(4):
        for n in range(wide):
            labels[pl.ds(8 * (k * wide + n), 8), :] = held[k, n, cap].astype(i32)
    copy = pltpu.make_async_copy(labels, names, sem)
    copy.start()
    copy.wait()
    for k in range(4):
        most = names[8 * k * wide + 1, 0]
        for n in range(1, wide):
            most = jnp.maximum(most, names[8 * (k * wide + n) + 1, 0])

        def rows4(r, carry):
            for u in range(4):
                for n in range(wide):
                    slot = r * 4 + u
                    where = names[8 * (k * wide + n), slot]
                    outs[n][where] = outs[n][where] + held[k, n, slot]
            return carry

        lax.fori_loop(0, (most + 3) // 4, rows4, 0)


def gather(arrived, leaf_count):
    wide, rows = arrived[0].shape[:2]
    return pl.pallas_call(
        functools.partial(gather_kernel, wide),
        out_shape=[jax.ShapeDtypeStruct((leaf_count + 1, 8, 128), f32)] * wide,
        in_specs=[pl.BlockSpec(memory_space=pl.ANY)] * 4,
        out_specs=[VMEM] * wide,
        scratch_shapes=[
            pltpu.VMEM((4, wide, rows, 8, 128), f32),
            pltpu.VMEM((32 * wide, 128), i32),
            pltpu.SMEM((32 * wide, 128), i32),
            pltpu.SemaphoreType.DMA(()),
            pltpu.SemaphoreType.DMA((4,)),
        ],
        cost_estimate=pl.CostEstimate(
            flops=wide * (1 << 26), bytes_accessed=wide << 22, transcendentals=0
        ),
        name="gather",
    )(*arrived)


def rows_of(shape):
    return lax.broadcasted_iota(i32, shape, len(shape) - 2)


def swap_rows(t):
    even = rows_of(t.shape) % 2 == 0
    axis = len(t.shape) - 2
    return jnp.where(even, pltpu.roll(t, 7, axis), pltpu.roll(t, 1, axis))


def spin(t, cosine, sine):
    return t * cosine + swap_rows(t) * sine


def row_mix(t, maps, bit):
    flipped = pltpu.roll(t, 64, 2)
    total = None
    for step in range(4):
        for flip in range(2):
            part = flipped if flip else t
            if step:
                part = pltpu.roll(part, 8 - 2 * step, 1)
            term = part * maps[bit, 2 * step + flip]
            total = term if total is None else total + term
    return total


def levels_kernel(
    slots, boxes, cones, box_cones, a0, a1, a2, a3, e0c, e0s, e1c, e1s, e2c, e2s, lanes, rows,
    leaves, partial, turned,
):
    owned = partial.shape[1] * 8 // 9
    upper = partial.shape[1] - owned
    partial[...] = jnp.zeros(partial.shape, f32)
    step = 32
    shape = (step, 8, 128)
    own = rows_of(shape) % 2 == lanes_of(shape) // 64

    def settle(n, carry):
        base = pl.multiple_of(n * step, step)
        t = (a0[pl.ds(base, step)] + a1[pl.ds(base, step)]) + (
            a2[pl.ds(base, step)] + a3[pl.ds(base, step)]
        )
        leaves[pl.ds(base, step)] = jnp.where(own, t, swap_rows(pltpu.roll(t, 64, 2)))
        return carry

    lax.fori_loop(0, leaves.shape[0] // step, settle, 0)

    for o in range(8):
        count = leaves.shape[0] // 8
        for j in range(count):
            e = cones[slots[o, j]] * 8 + o
            turned[j] = spin(leaves[8 * j + o], e0c[e], e0s[e])
        mixed = jnp.dot(
            turned[...].reshape(count * 8, 128), lanes[o % 4],
            precision=lax.Precision.HIGHEST, preferred_element_type=f32,
        ).reshape(count, 8, 128)
        turned[...] = row_mix(mixed, rows, o // 4)
        for j in range(count):
            p = slots[o, j]
            q, r = p // owned, p % owned
            partial[q, r] = partial[q, r] + turned[j]

    for o in range(8):
        count = boxes.shape[1]
        for j in range(count):
            p = 8 * j + o
            cone = cones[p]
            e = box_cones[boxes[o, j]] * 8 + o
            t = spin(partial[p // owned, p % owned], e1c[cone], e1s[cone])
            turned[j] = spin(t, e2c[e], e2s[e])
        mixed = jnp.dot(
            turned[...].reshape(count * 8, 128), lanes[o % 4],
            precision=lax.Precision.HIGHEST, preferred_element_type=f32,
        ).reshape(count, 8, 128)
        turned[...] = row_mix(mixed, rows, o // 4)
        for j in range(count):
            p = boxes[o, j]
            q, r = p // upper, owned + p % upper
            partial[q, r] = partial[q, r] + turned[j]


def close_kernel(first, second, cones, box_cones, got, e1c, e1s, e3c, e3s, out_one, out_two):
    owned = out_one.shape[0]
    for n in range(got.shape[1]):
        t = got[0, n]
        for s in range(1, got.shape[0]):
            t = t + got[s, n]
        if n < owned:
            e = cones[first[0] + n]
            out_one[n] = spin(t, e1c[e], e1s[e])
        else:
            e = box_cones[second[0] + n - owned]
            out_two[n - owned] = spin(t, e3c[e], e3s[e])


def phase_tables(directions, kappa, places):
    grid = jnp.asarray(places.astype(np.float32))
    angle = (
        directions[:, 0, None, None, None] * grid[None, :, 0]
        + directions[:, 1, None, None, None] * grid[None, :, 1]
        + directions[:, 2, None, None, None] * grid[None, :, 2]
    )
    angle = (kappa * angle).reshape(-1, 8, 128)
    sign = jnp.where(lax.broadcasted_iota(i32, (1, 8, 128), 1) % 2 == 0, -1.0, 1.0).astype(f32)
    return jnp.cos(angle), jnp.sin(angle) * sign


def to_nodes(tiles):
    count = tiles.shape[0]
    return tiles.reshape(count, 4, 2, 128).transpose(0, 2, 1, 3).reshape(count, 2, 512)


def cone_vectors(cone_angles):
    azimuth = cone_angles[:, 0]
    polar = cone_angles[:, 1]
    return jnp.stack(
        [jnp.cos(azimuth) * jnp.sin(polar), jnp.sin(azimuth) * jnp.sin(polar), jnp.cos(polar)],
        axis=1,
    )


def hop(x, shift, leg, groups):
    pairs = []
    for s in range(16):
        for g in range(groups):
            y, x0 = s // 4, s % 4
            if g % 2 == leg:
                x0 = (x0 + shift) % 4
            else:
                y = (y + shift) % 4
            pairs.append((s * groups + g, (4 * y + x0) * groups + g))
    return lax.ppermute(x, ("sfc", "grp"), pairs)


def per_device(
    bin_points, bin_plan, bin_leaf, leaf_slots, box_slots, parent_cone, box_cone, cone_angles
):
    peers = lax.axis_size("sfc")
    groups = lax.axis_size("grp")
    rank = lax.axis_index("grp")
    cap = bin_points.shape[0] // 8
    leaf_count = leaf_slots.shape[2] * 8
    first_owned = parent_cone.shape[1] // groups
    second_owned = box_cone.shape[1] // groups

    me = lax.axis_index("sfc")
    here = jnp.stack([me % 4, me // 4, rank % 2]).astype(i32)
    table, labels = route(here, bin_plan[:, 0], bin_leaf)
    pts = jnp.transpose(bin_points, (1, 0, 2))
    held = [None] * 4
    for c, chunk in enumerate(CHUNKS):
        sent = expand(c, table, labels, pts, cap)
        arrived = [sent[0]] + [hop(sent[k], k, 0, groups) for k in (2, 1, 3)]
        for m, sums in zip(chunk, gather(arrived, leaf_count)):
            held[m] = hop(sums, m, 1, groups) if m else sums

    directions = cone_vectors(cone_angles)
    child = np.stack(
        [
            tile_of_nodes(child_axis(o // 4), child_axis(o // 2 % 2), child_axis(o % 2))
            for o in range(8)
        ]
    )
    nodes = cheb_nodes()
    parent = tile_of_nodes(nodes, nodes, nodes)[None]
    e0c, e0s = phase_tables(directions, kappa_leaf, child)
    e1c, e1s = phase_tables(directions, -kappa_leaf, parent)
    e2c, e2s = phase_tables(directions, kappa_box, child)
    e3c, e3s = phase_tables(directions, -kappa_box, parent)

    leaves, partial = pl.pallas_call(
        levels_kernel,
        out_shape=(
            jax.ShapeDtypeStruct((leaf_count, 8, 128), f32),
            jax.ShapeDtypeStruct((groups, first_owned + second_owned, 8, 128), f32),
        ),
        in_specs=[SMEM] * 4 + [VMEM] * 12,
        out_specs=(VMEM, VMEM),
        scratch_shapes=[
            pltpu.VMEM((leaf_count // 8, 8, 128), f32),
        ],
        name="levels",
    )(
        leaf_slots[0], box_slots[0], parent_cone[0], box_cone[0], *held,
        e0c, e0s, e1c, e1s, e2c, e2s, jnp.asarray(lane_maps()), jnp.asarray(row_maps()),
    )
    got = lax.all_to_all(partial, "grp", split_axis=0, concat_axis=0, tiled=True)
    one, two = pl.pallas_call(
        close_kernel,
        out_shape=(
            jax.ShapeDtypeStruct((first_owned, 8, 128), f32),
            jax.ShapeDtypeStruct((second_owned, 8, 128), f32),
        ),
        in_specs=[SMEM] * 4 + [VMEM] * 5,
        out_specs=(VMEM, VMEM),
        name="close",
    )(
        (rank * first_owned)[None], (rank * second_owned)[None], parent_cone[0], box_cone[0],
        got, e1c, e1s, e3c, e3s,
    )
    return (to_nodes(leaves), to_nodes(one), to_nodes(two))


def solution(mesh):
    placed = (
        P(("sfc", "grp"), None, None),
        P(("sfc", "grp"), None),
        P(("sfc", "grp")),
        P("sfc", None, "grp"),
        P("sfc", None, None),
        P("sfc", None),
        P("sfc", None),
        P(),
    )
    return jax.shard_map(
        per_device,
        mesh=mesh,
        in_specs=placed,
        out_specs=(
            P(("sfc", "grp"), None, None),
            P(("sfc", "grp"), None, None),
            P(("sfc", "grp"), None, None),
        ),
        check_vma=False,
    )
```

```python
import functools

import jax
import jax.numpy as jnp
import numpy as np
from jax import lax
from jax.experimental import pallas as pl
from jax.experimental.pallas import tpu as pltpu
from jax.sharding import PartitionSpec as P

kappa_leaf = 2.0
kappa_box = 4.0
f32 = jnp.float32
i32 = jnp.int32
VMEM = pl.BlockSpec(memory_space=pltpu.VMEM)
SMEM = pl.BlockSpec(memory_space=pltpu.SMEM)
ANY = pl.BlockSpec(memory_space=pl.ANY)


def cheb_nodes():
    return np.cos((2.0 * np.arange(8) + 1.0) * np.pi / 16.0)


def lagrange_np(values):
    nodes = cheb_nodes()
    rows = []
    for center in range(8):
        weight = np.ones_like(values)
        for other in range(8):
            if other != center:
                weight = weight * (values - nodes[other]) / (nodes[center] - nodes[other])
        rows.append(weight)
    return np.stack(rows, axis=0)


def child_axis(bit):
    return 0.5 * (2 * bit - 1) + 0.5 * cheb_nodes()


def axis_maps():
    return np.stack([lagrange_np(child_axis(bit)) for bit in range(2)])


def tile_of_nodes(first, second, third):
    rows = np.arange(8)[:, None]
    lanes = np.arange(128)[None, :]
    a = 2 * (rows // 2) + lanes // 64
    b = lanes % 64 // 8 + 0 * rows
    c = lanes % 8 + 0 * rows
    return np.stack([first[a], second[b], third[c]])


def lane_maps():
    maps = axis_maps()
    out = []
    for pick in range(4):
        both = np.kron(maps[pick // 2], maps[pick % 2])
        full = np.kron(np.eye(2), both).T
        high = full.astype(jnp.bfloat16)
        low = (full - high.astype(np.float64)).astype(jnp.bfloat16)
        out.append(np.block([[high, low], [high, np.zeros_like(low)]]))
    return np.stack(out).astype(jnp.bfloat16)


def row_maps():
    maps = axis_maps()
    rows = np.arange(8)[:, None]
    half = np.arange(128)[None, :] // 64
    k = rows // 2
    out = np.zeros((2, 8, 8, 128), np.float32)
    for bit in range(2):
        for step in range(4):
            for flip in range(2):
                to = 2 * k + half
                frm = 2 * ((k + step) % 4) + (half ^ flip)
                out[bit, 2 * step + flip] = maps[bit][to, frm]
    return out


def basis(x):
    t = cheb_nodes()[:4]
    sq = t * t
    x2 = x * x
    s = [x2 - float(v) for v in sq]
    p01 = s[0] * s[1]
    p23 = s[2] * s[3]
    rest = [s[1] * p23, s[0] * p23, p01 * s[3], p01 * s[2]]
    out = [None] * 8
    for j in range(4):
        scale = 1.0 / (np.prod([sq[j] - sq[i] for i in range(4) if i != j]) * 2.0 * t[j])
        q = rest[j] * float(scale)
        out[j] = q * (x + float(t[j]))
        out[7 - j] = q * (float(t[j]) - x)
    return out


def lanes_of(shape):
    return lax.broadcasted_iota(i32, shape, len(shape) - 1)


def lanes_of(shape):
    return lax.broadcasted_iota(i32, shape, len(shape) - 1)


CHUNKS = ((2,), (1, 3), (0,))
ORDER = tuple(m for chunk in CHUNKS for m in chunk)


def route_kernel(here, plan, leaf, table, labels, picked, scaled):
    bf16 = jnp.bfloat16
    cap = labels.shape[2]
    target = plan[...]
    names = leaf[...].astype(f32)
    along_x = (target - here[0]) % 4
    along_y = (target // 4 - here[1]) % 4
    first = jnp.where(here[2] == 0, along_x, along_y)
    second = jnp.where(here[2] == 0, along_y, along_x)
    place, lead, width = target * 0, target * 0, target * 0
    for chunk in CHUNKS:
        for n, m in enumerate(chunk):
            hit = second == m
            place = jnp.where(hit, ORDER.index(m), place)
            lead = jnp.where(hit, n, lead)
            width = jnp.where(hit, len(chunk), width)
    code = place * 4 + first
    for d in range(16):
        hit = (code == d).astype(f32)
        picked[pl.ds(8 * d, 8), :] = hit
        scaled[pl.ds(8 * d, 8), :] = hit * names
    square = (128, 128)
    row, lane = rows_of(square), lanes_of(square)
    hits = picked[...].astype(bf16)
    ones = jnp.ones(square, bf16)

    def mul(a, b):
        return jnp.dot(a.astype(bf16), b.astype(bf16), preferred_element_type=f32)

    inside = mul(hits, (row < lane).astype(f32))
    ahead = mul(mul((lane < row).astype(f32), hits), ones)
    same = mul(mul(((lane < row) & (lane // 8 == row // 8)).astype(f32), hits), ones)
    order = jnp.zeros((8, 128), f32)
    slot = jnp.zeros((8, 128), f32)
    for d in range(16):
        part = slice(8 * d, 8 * d + 8)
        hit = picked[pl.ds(8 * d, 8), :]
        order = order + hit * (inside[part] + ahead[part])
        slot = slot + hit * (inside[part] + same[part])
    goal_hi = (first * width + lead).astype(f32)
    count = order.shape[0] * 128
    ranks = lax.broadcasted_iota(i32, (count, 128), 0).astype(f32)
    seats = row.astype(f32)
    sub = lax.broadcasted_iota(i32, (8, 128), 0)
    lane_f = lanes_of((8, 128)).astype(f32)
    found = jnp.zeros((8, count), f32)
    marks = jnp.zeros((32, 128), f32)
    nt = (((1,), (1,)), ((), ()))
    for r in range(8):
        at = jnp.broadcast_to(order[r : r + 1, :], (count, 128)) == ranks
        goal = jnp.broadcast_to(goal_hi[r : r + 1, :], (8, 128))
        seat = jnp.broadcast_to(slot[r : r + 1, :], (8, 128))
        values = jnp.where(
            sub == 0, float(r), jnp.where(sub == 1, lane_f, jnp.where(sub == 2, goal, seat))
        )
        found = found + lax.dot_general(
            values.astype(bf16), at.astype(f32).astype(bf16), nt, preferred_element_type=f32
        )
        both = jnp.concatenate(
            [scaled[pl.ds(r, 16, stride=8), :], picked[pl.ds(r, 16, stride=8), :]], axis=0
        )
        sits = jnp.broadcast_to(slot[r : r + 1, :], square) == seats
        marks = marks + lax.dot_general(
            both.astype(bf16), sits.astype(f32).astype(bf16), nt, preferred_element_type=f32
        )
    table[0:1, :] = (found[0:1] * 128.0 + found[1:2]).astype(i32)
    table[1:2, :] = (found[2:3] * float(cap_rows(cap)) + found[3:4]).astype(i32)
    lane_w = lanes_of((1, count))
    ends = jnp.zeros((1, count), f32)
    for q in range(4):
        upto = jnp.sum((place <= q).astype(f32), keepdims=True)
        ends = jnp.where(lane_w == q, jnp.broadcast_to(upto, (1, count)), ends)
    table[2:3, :] = ends.astype(i32)
    label = marks[:16] + 256.0 * (1.0 - marks[16:])
    for d in range(16):
        total = jnp.sum(marks[16 + d : 17 + d], axis=1, keepdims=True)
        labels[d] = jnp.where(
            sub == 0,
            jnp.broadcast_to(label[d : d + 1], (8, 128)),
            jnp.broadcast_to(total, (8, 128)),
        )


def cap_rows(cap):
    return cap + 1


def route(here, plan, leaf):
    bins = plan.shape[0]
    return pl.pallas_call(
        route_kernel,
        out_shape=(
            jax.ShapeDtypeStruct((3, bins), i32),
            jax.ShapeDtypeStruct((16, 8, 128), f32),
        ),
        in_specs=[SMEM, VMEM, VMEM],
        out_specs=(VMEM, VMEM),
        scratch_shapes=[pltpu.VMEM((128, 128), f32)] * 2,
        name="route",
    )(here, plan.reshape(bins // 128, 128), leaf.reshape(bins // 128, 128))


GROUP = 8


def expand_kernel(chunk, table, labels, pts, *refs):
    outs = refs[:4]
    held, all_pts = refs[4:6]
    banks = (refs[6:10], refs[10:14])
    sems, load_sems = refs[14:]
    first = sum(len(c) for c in CHUNKS[:chunk])
    wide = len(CHUNKS[chunk])
    rows = outs[0].shape[1]
    cap = rows - 1
    bins = all_pts.shape[2]
    loads = [
        pltpu.make_async_copy(
            pts.at[axis, :, pl.ds(128 * h, 128)], all_pts.at[axis, h], load_sems.at[2 * axis + h]
        )
        for axis in range(5)
        for h in range(2)
    ]
    for load in loads:
        load.start()
    for k in range(4):
        for n in range(wide):
            held[(k * wide + n) * rows + cap] = labels[4 * (first + n) + k]
    begin = table[2, first - 1] if first else 0
    end = table[2, first + wide - 1]
    for load in loads:
        load.wait()

    def prepare(g, bank):
        stage, bx, by, bz = bank
        for u in range(GROUP):
            number = table[0, jnp.minimum(begin + g * GROUP + u, bins - 1)]
            for axis in range(5):
                for h in range(2):
                    stage[axis, h, pl.ds(u, 1), :] = all_pts[axis, h, pl.ds(number, 1), :]
        for h in range(2):
            for axis, ref in ((0, bx), (2, bz)):
                values = basis(stage[axis, h])
                for a in range(8):
                    ref[h, pl.ds(a, GROUP, stride=8), :] = values[a]
            values = basis(stage[1, h])
            for a in range(8):
                by[h, pl.ds(GROUP * a, GROUP), :] = values[a]

    def consume(g, bank):
        stage, bx, by, bz = bank
        for u in range(GROUP):
            weighted, pair = [], []
            for h in range(2):
                lx = bx[h, pl.ds(8 * u, 8), :]
                lz = bz[h, pl.ds(8 * u, 8), :]
                re, im = (
                    jnp.broadcast_to(stage[3 + part, h, pl.ds(u, 1), :], lx.shape)
                    for part in range(2)
                )
                weighted.append(jnp.concatenate([re * lx, im * lx], axis=0).astype(jnp.bfloat16))
                pair.append(
                    jnp.concatenate(
                        [
                            jnp.broadcast_to(by[h, pl.ds(GROUP * b + u, 1), :], lz.shape) * lz
                            for b in range(8)
                        ],
                        axis=0,
                    ).astype(jnp.bfloat16)
                )
            res = lax.dot_general(
                jnp.concatenate(weighted, axis=1),
                jnp.concatenate(pair, axis=1),
                (((1,), (1,)), ((), ())),
                preferred_element_type=f32,
            )
            seat = begin + g * GROUP + u
            goal = jnp.where(
                seat < end, table[1, jnp.minimum(seat, bins - 1)], held.shape[0] - 1
            )
            held[goal] = jnp.concatenate([res[:8], res[8:]], axis=1)

    prepare(0, banks[0])

    def two(i, carry):
        prepare(2 * i + 1, banks[1])
        consume(2 * i, banks[0])
        prepare(2 * i + 2, banks[0])
        consume(2 * i + 1, banks[1])
        return carry

    lax.fori_loop(0, (end - begin + 2 * GROUP - 1) // (2 * GROUP), two, 0)
    copies = []
    for k in range(4):
        for n in range(wide):
            copies.append(
                pltpu.make_async_copy(
                    held.at[pl.ds((k * wide + n) * rows, rows)], outs[k].at[n], sems.at[k, n]
                )
            )
    for copy in copies:
        copy.start()
    for copy in copies:
        copy.wait()


def expand(chunk, table, labels, pts, cap):
    bins = pts.shape[1]
    wide = len(CHUNKS[chunk])
    bank = [pltpu.VMEM((5, 2, GROUP, 128), f32)] + [pltpu.VMEM((2, 8 * GROUP, 128), f32)] * 3
    return pl.pallas_call(
        functools.partial(expand_kernel, chunk),
        out_shape=[jax.ShapeDtypeStruct((wide, cap + 1, 8, 128), f32)] * 4,
        in_specs=[SMEM, VMEM, ANY],
        out_specs=[ANY] * 4,
        scratch_shapes=[
            pltpu.VMEM((4 * wide * (cap + 1) + 1, 8, 128), f32),
            pltpu.VMEM((5, 2, bins, 128), f32),
            *bank,
            *bank,
            pltpu.SemaphoreType.DMA((4, wide)),
            pltpu.SemaphoreType.DMA((10,)),
        ],
        cost_estimate=pl.CostEstimate(
            flops=wide * (1 << 28), bytes_accessed=1 << 23, transcendentals=0
        ),
        name="expand",
    )(table, labels, pts)


def gather_kernel(wide, *refs):
    arrived, outs = refs[:4], refs[4 : 4 + wide]
    held, labels, names, sem, sems = refs[4 + wide :]
    cap = held.shape[2] - 1
    loads = [pltpu.make_async_copy(arrived[k], held.at[k], sems.at[k]) for k in range(4)]
    for load in loads:
        load.start()
    for out in outs:
        out[...] = jnp.zeros(out.shape, f32)
    for load in loads:
        load.wait()
    for k in range(4):
        for n in range(wide):
            labels[pl.ds(8 * (k * wide + n), 8), :] = held[k, n, cap].astype(i32)
    copy = pltpu.make_async_copy(labels, names, sem)
    copy.start()
    copy.wait()
    for k in range(4):
        most = names[8 * k * wide + 1, 0]
        for n in range(1, wide):
            most = jnp.maximum(most, names[8 * (k * wide + n) + 1, 0])

        def rows4(r, carry):
            for u in range(4):
                for n in range(wide):
                    slot = r * 4 + u
                    where = names[8 * (k * wide + n), slot]
                    outs[n][where] = outs[n][where] + held[k, n, slot]
            return carry

        lax.fori_loop(0, (most + 3) // 4, rows4, 0)


def gather(arrived, leaf_count):
    wide, rows = arrived[0].shape[:2]
    return pl.pallas_call(
        functools.partial(gather_kernel, wide),
        out_shape=[jax.ShapeDtypeStruct((leaf_count + 1, 8, 128), f32)] * wide,
        in_specs=[pl.BlockSpec(memory_space=pl.ANY)] * 4,
        out_specs=[VMEM] * wide,
        scratch_shapes=[
            pltpu.VMEM((4, wide, rows, 8, 128), f32),
            pltpu.VMEM((32 * wide, 128), i32),
            pltpu.SMEM((32 * wide, 128), i32),
            pltpu.SemaphoreType.DMA(()),
            pltpu.SemaphoreType.DMA((4,)),
        ],
        cost_estimate=pl.CostEstimate(
            flops=wide * (1 << 26), bytes_accessed=wide << 22, transcendentals=0
        ),
        name="gather",
    )(*arrived)


def rows_of(shape):
    return lax.broadcasted_iota(i32, shape, len(shape) - 2)


def swap_rows(t):
    even = rows_of(t.shape) % 2 == 0
    axis = len(t.shape) - 2
    return jnp.where(even, pltpu.roll(t, 7, axis), pltpu.roll(t, 1, axis))


def spin(t, cosine, sine):
    return t * cosine + swap_rows(t) * sine


def row_mix(t, maps, bit):
    flipped = pltpu.roll(t, 64, 2)
    total = None
    for step in range(4):
        for flip in range(2):
            part = flipped if flip else t
            if step:
                part = pltpu.roll(part, 8 - 2 * step, 1)
            term = part * maps[bit, 2 * step + flip]
            total = term if total is None else total + term
    return total


SEATS = 36


def phases_kernel(
    here, slots, boxes, cones, box_cones, e0c, e0s, e1c, e1s, e2c, e2s, p0c, p0s, p1c, p1s, goal
):
    side = here[2]
    for o in range(8):

        def child(j, carry):
            p = slots[o, j]
            e = cones[p] * 8 + o
            p0c[o, j] = e0c[e]
            p0s[o, j] = e0s[e]
            owner = p >> 5
            goal[o, j] = ((((owner & 1) ^ side) << 2) + (owner >> 1)) * SEATS + (p & 31)
            q = boxes[o, j]
            a = cones[8 * j + o]
            b = box_cones[q] * 8 + o
            ca, sa, cb, sb = e1c[a], e1s[a], e2c[b], e2s[b]
            p1c[o, j] = ca * cb - sa * sb
            p1s[o, j] = sa * cb + ca * sb
            owner = q >> 2
            goal[8 + o, j] = ((((owner & 1) ^ side) << 2) + (owner >> 1)) * SEATS + 32 + (q & 3)
            return carry

        lax.fori_loop(0, 32, child, 0, unroll=4)


def translate(t, both, rows, octant):
    count = t.shape[0]
    flat = t.reshape(count * 8, 128)
    high = flat.astype(jnp.bfloat16)
    low = (flat - high.astype(f32)).astype(jnp.bfloat16)
    res = jnp.dot(
        jnp.concatenate([high, low], axis=1), both[octant % 4], preferred_element_type=f32
    )
    return row_mix((res[:, :128] + res[:, 128:]).reshape(count, 8, 128), rows, octant // 4)


def levels_kernel(
    here, goal, a0, a1, a2, a3, p0c, p0s, p1c, p1s, both, rows, leaves, mine, other, acc, moved
):
    acc[...] = jnp.zeros(acc.shape, f32)
    step = 16
    shape = (step, 8, 128)
    own = rows_of(shape) % 2 == lanes_of(shape) // 64

    def settle(n, carry):
        base = pl.multiple_of(n * step, step)
        t = (a0[pl.ds(base, step)] + a1[pl.ds(base, step)]) + (
            a2[pl.ds(base, step)] + a3[pl.ds(base, step)]
        )
        leaves[pl.ds(base, step)] = jnp.where(own, t, swap_rows(pltpu.roll(t, 64, 2)))
        return carry

    lax.fori_loop(0, leaves.shape[0] // step, settle, 0)

    def spread(o, lead):
        for start in range(0, 32, 8):
            spots = [goal[lead + o, start + j] for j in range(8)]
            sums = [acc[spots[j]] + moved[o % 2, start + j] for j in range(8)]
            for j in range(8):
                acc[spots[j]] = sums[j]

    for o in range(8):
        for part in range(0, 32, 8):
            t = jnp.stack([leaves[8 * (part + j) + o] for j in range(8)])
            t = spin(t, p0c[o, part : part + 8], p0s[o, part : part + 8])
            moved[o % 2, part : part + 8] = translate(t, both, rows, o)
        spread(o, 0)

    apart = [here[2] * 4 * SEATS, (1 - here[2]) * 4 * SEATS]
    for o in range(8):
        for part in range(0, 32, 8):
            tiles = []
            for j in range(8):
                p = 8 * (part + j) + o
                owner = p // 32
                tiles.append(acc[(owner // 2) * SEATS + p % 32 + apart[owner % 2]])
            t = spin(jnp.stack(tiles), p1c[o, part : part + 8], p1s[o, part : part + 8])
            moved[o % 2, part : part + 8] = translate(t, both, rows, o)
        spread(o, 8)
    for z in range(4):
        mine[z] = acc[pl.ds(z * SEATS, SEATS)]
        other[z] = acc[pl.ds((4 + z) * SEATS, SEATS)]


def merge_kernel(here, mine, got, *outs):
    for k in range(4):
        z = (here[3] + k) % 4
        outs[k][...] = mine[z] + got[z]


def close_kernel(here, cones, box_cones, g0, g1, g2, g3, e1c, e1s, e3c, e3s, out_one, out_two):
    owned, upper = out_one.shape[0], out_two.shape[0]
    me = 2 * here[3] + here[2]
    for n in range(SEATS):
        t = (g0[n] + g1[n]) + (g2[n] + g3[n])
        if n < owned:
            e = cones[me * owned + n]
            out_one[n] = spin(t, e1c[e], e1s[e])
        else:
            e = box_cones[me * upper + n - owned]
            out_two[n - owned] = spin(t, e3c[e], e3s[e])


def phase_tables(directions, kappa, places):
    grid = jnp.asarray(places.astype(np.float32))
    angle = (
        directions[:, 0, None, None, None] * grid[None, :, 0]
        + directions[:, 1, None, None, None] * grid[None, :, 1]
        + directions[:, 2, None, None, None] * grid[None, :, 2]
    )
    angle = (kappa * angle).reshape(-1, 8, 128)
    sign = jnp.where(lax.broadcasted_iota(i32, (1, 8, 128), 1) % 2 == 0, -1.0, 1.0).astype(f32)
    return jnp.cos(angle), jnp.sin(angle) * sign


def to_nodes(tiles):
    count = tiles.shape[0]
    return tiles.reshape(count, 4, 2, 128).transpose(0, 2, 1, 3).reshape(count, 2, 512)


def cone_vectors(cone_angles):
    azimuth = cone_angles[:, 0]
    polar = cone_angles[:, 1]
    return jnp.stack(
        [jnp.cos(azimuth) * jnp.sin(polar), jnp.sin(azimuth) * jnp.sin(polar), jnp.cos(polar)],
        axis=1,
    )


def hop(x, shift, leg, groups):
    pairs = []
    for s in range(16):
        for g in range(groups):
            y, x0 = s // 4, s % 4
            if g % 2 == leg:
                x0 = (x0 + shift) % 4
            else:
                y = (y + shift) % 4
            pairs.append((s * groups + g, (4 * y + x0) * groups + g))
    return lax.ppermute(x, ("sfc", "grp"), pairs)


def around(x, shift, groups):
    pairs = [(g, (g + 2 * shift) % groups) for g in range(groups)]
    return lax.ppermute(x, "grp", pairs)


def after(value, *others):
    return lax.optimization_barrier((value, *others))[0]


def per_device(
    bin_points, bin_plan, bin_leaf, leaf_slots, box_slots, parent_cone, box_cone, cone_angles
):
    groups = lax.axis_size("grp")
    rank = lax.axis_index("grp")
    cap = bin_points.shape[0] // 8
    leaf_count = leaf_slots.shape[2] * 8
    first_owned = parent_cone.shape[1] // groups
    second_owned = box_cone.shape[1] // groups
    tile = jax.ShapeDtypeStruct((8, 128), f32)

    def tiles(*lead):
        return jax.ShapeDtypeStruct((*lead, *tile.shape), f32)

    me = lax.axis_index("sfc")
    here = jnp.stack([me % 4, me // 4, rank % 2, rank // 2]).astype(i32)
    table, labels = route(here, bin_plan[:, 0], bin_leaf)
    pts = jnp.transpose(bin_points, (1, 0, 2))
    arrived = []
    for c in range(len(CHUNKS)):
        sent = expand(c, table, labels, pts, cap)
        table = after(table, sent[0])
        moved = [sent[0]]
        for k in (2, 1, 3):
            moved.append(hop(sent[k], k, 0, groups))
        arrived.append(moved)

    cone_angles = after(cone_angles, sent[0])
    directions = cone_vectors(cone_angles)
    child = np.stack(
        [
            tile_of_nodes(child_axis(o // 4), child_axis(o // 2 % 2), child_axis(o % 2))
            for o in range(8)
        ]
    )
    nodes = cheb_nodes()
    parent = tile_of_nodes(nodes, nodes, nodes)[None]
    e0c, e0s = phase_tables(directions, kappa_leaf, child)
    e1c, e1s = phase_tables(directions, -kappa_leaf, parent)
    e2c, e2s = phase_tables(directions, kappa_box, child)
    e3c, e3s = phase_tables(directions, -kappa_box, parent)
    make_phases = pl.pallas_call(
        phases_kernel,
        out_shape=(tiles(8, 32),) * 4 + (jax.ShapeDtypeStruct((16, 32), i32),),
        in_specs=[SMEM] * 5 + [VMEM] * 6,
        out_specs=(VMEM,) * 4 + (SMEM,),
        name="phases",
    )
    p0c, p0s, p1c, p1s, goal = make_phases(
        here, leaf_slots[0], box_slots[0], parent_cone[0], box_cone[0],
        e0c, e0s, e1c, e1s, e2c, e2s,
    )

    held = [None] * 4
    last = sent[0]
    for c, chunk in enumerate(CHUNKS):
        got = [after(arrived[c][0], last)] + arrived[c][1:]
        sums = gather(got, leaf_count)
        last = sums[0]
        for m, part in zip(chunk, sums):
            held[m] = hop(part, m, 1, groups) if m else part

    leaves, mine, other = pl.pallas_call(
        levels_kernel,
        out_shape=(tiles(leaf_count), tiles(4, SEATS), tiles(4, SEATS)),
        in_specs=[SMEM] * 2 + [VMEM] * 10,
        out_specs=(VMEM,) * 3,
        scratch_shapes=[
            pltpu.VMEM((8 * SEATS, 8, 128), f32),
            pltpu.VMEM((2, 32, 8, 128), f32),
        ],
        name="levels",
    )(
        here, goal, *held, p0c, p0s, p1c, p1s,
        jnp.asarray(lane_maps()), jnp.asarray(row_maps()),
    )
    swapped = lax.ppermute(other, "grp", [(g, g ^ 1) for g in range(groups)])
    blocks = pl.pallas_call(
        merge_kernel,
        out_shape=(tiles(SEATS),) * 4,
        in_specs=[SMEM] + [VMEM] * 2,
        out_specs=(VMEM,) * 4,
        name="merge",
    )(here, mine, swapped)
    got = [blocks[0]] + [around(blocks[k], k, groups) for k in (1, 2, 3)]
    one, two = pl.pallas_call(
        close_kernel,
        out_shape=(tiles(first_owned), tiles(second_owned)),
        in_specs=[SMEM] * 3 + [VMEM] * 8,
        out_specs=(VMEM, VMEM),
        name="close",
    )(here, parent_cone[0], box_cone[0], *got, e1c, e1s, e3c, e3s)
    return (to_nodes(leaves), to_nodes(one), to_nodes(two))


def solution(mesh):
    placed = (
        P(("sfc", "grp"), None, None),
        P(("sfc", "grp"), None),
        P(("sfc", "grp")),
        P("sfc", None, "grp"),
        P("sfc", None, None),
        P("sfc", None),
        P("sfc", None),
        P(),
    )

    return jax.shard_map(
        per_device,
        mesh=mesh,
        in_specs=placed,
        out_specs=(
            P(("sfc", "grp"), None, None),
            P(("sfc", "grp"), None, None),
            P(("sfc", "grp"), None, None),
        ),
        check_vma=False,
    )
```

```python
import functools

import jax
import jax.numpy as jnp
import numpy as np
from jax import lax
from jax.experimental import pallas as pl
from jax.experimental.pallas import tpu as pltpu
from jax.sharding import PartitionSpec as P

kappa_leaf = 2.0
kappa_box = 4.0
f32 = jnp.float32
i32 = jnp.int32
VMEM = pl.BlockSpec(memory_space=pltpu.VMEM)
SMEM = pl.BlockSpec(memory_space=pltpu.SMEM)
ANY = pl.BlockSpec(memory_space=pl.ANY)


def cheb_nodes():
    return np.cos((2.0 * np.arange(8) + 1.0) * np.pi / 16.0)


def lagrange_np(values):
    nodes = cheb_nodes()
    rows = []
    for center in range(8):
        weight = np.ones_like(values)
        for other in range(8):
            if other != center:
                weight = weight * (values - nodes[other]) / (nodes[center] - nodes[other])
        rows.append(weight)
    return np.stack(rows, axis=0)


def child_axis(bit):
    return 0.5 * (2 * bit - 1) + 0.5 * cheb_nodes()


def axis_maps():
    return np.stack([lagrange_np(child_axis(bit)) for bit in range(2)])


def tile_of_nodes(first, second, third):
    rows = np.arange(8)[:, None]
    lanes = np.arange(128)[None, :]
    a = 2 * (rows // 2) + lanes // 64
    b = lanes % 64 // 8 + 0 * rows
    c = lanes % 8 + 0 * rows
    return np.stack([first[a], second[b], third[c]])


def lane_maps():
    maps = axis_maps()
    out = []
    for pick in range(4):
        both = np.kron(maps[pick // 2], maps[pick % 2])
        full = np.kron(np.eye(2), both).T
        high = full.astype(jnp.bfloat16)
        low = (full - high.astype(np.float64)).astype(jnp.bfloat16)
        out.append(np.block([[high, low], [high, np.zeros_like(low)]]))
    return np.stack(out).astype(jnp.bfloat16)


def row_maps():
    maps = axis_maps()
    rows = np.arange(8)[:, None]
    half = np.arange(128)[None, :] // 64
    k = rows // 2
    out = np.zeros((2, 8, 8, 128), np.float32)
    for bit in range(2):
        for step in range(4):
            for flip in range(2):
                to = 2 * k + half
                frm = 2 * ((k + step) % 4) + (half ^ flip)
                out[bit, 2 * step + flip] = maps[bit][to, frm]
    return out


def basis(x):
    t = cheb_nodes()[:4]
    sq = t * t
    x2 = x * x
    s = [x2 - float(v) for v in sq]
    p01 = s[0] * s[1]
    p23 = s[2] * s[3]
    rest = [s[1] * p23, s[0] * p23, p01 * s[3], p01 * s[2]]
    out = [None] * 8
    for j in range(4):
        scale = 1.0 / (np.prod([sq[j] - sq[i] for i in range(4) if i != j]) * 2.0 * t[j])
        q = rest[j] * float(scale)
        out[j] = q * (x + float(t[j]))
        out[7 - j] = q * (float(t[j]) - x)
    return out


def lanes_of(shape):
    return lax.broadcasted_iota(i32, shape, len(shape) - 1)


def lanes_of(shape):
    return lax.broadcasted_iota(i32, shape, len(shape) - 1)


CHUNKS = ((2, 1), (3, 0))
ORDER = tuple(m for chunk in CHUNKS for m in chunk)


def route_kernel(here, plan, leaf, table, labels, picked, scaled):
    bf16 = jnp.bfloat16
    cap = labels.shape[2]
    target = plan[...]
    names = leaf[...].astype(f32)
    along_x = (target - here[0]) % 4
    along_y = (target // 4 - here[1]) % 4
    first = jnp.where(here[2] == 0, along_x, along_y)
    second = jnp.where(here[2] == 0, along_y, along_x)
    place, lead, width, part_of = target * 0, target * 0, target * 0, target * 0
    for c, chunk in enumerate(CHUNKS):
        for n, m in enumerate(chunk):
            hit = second == m
            place = jnp.where(hit, ORDER.index(m), place)
            part_of = jnp.where(hit, c, part_of)
            lead = jnp.where(hit, n, lead)
            width = jnp.where(hit, len(chunk), width)
    code = place * 4 + first
    for d in range(16):
        hit = (code == d).astype(f32)
        picked[pl.ds(8 * d, 8), :] = hit
        scaled[pl.ds(8 * d, 8), :] = hit * names
    square = (128, 128)
    row, lane = rows_of(square), lanes_of(square)
    hits = picked[...].astype(bf16)
    ones = jnp.ones(square, bf16)

    def mul(a, b):
        return jnp.dot(a.astype(bf16), b.astype(bf16), preferred_element_type=f32)

    inside = mul(hits, (row < lane).astype(f32))
    ahead = mul(mul((lane < row).astype(f32), hits), ones)
    same = mul(mul(((lane < row) & (lane // 8 == row // 8)).astype(f32), hits), ones)
    order = jnp.zeros((8, 128), f32)
    slot = jnp.zeros((8, 128), f32)
    for d in range(16):
        part = slice(8 * d, 8 * d + 8)
        hit = picked[pl.ds(8 * d, 8), :]
        order = order + hit * (inside[part] + ahead[part])
        slot = slot + hit * (inside[part] + same[part])
    count = ENTRIES
    lane_w = lanes_of((1, count))
    spans = jnp.zeros((1, count), f32)
    start = jnp.zeros((1, 1), f32)
    before = jnp.zeros((1, 1), f32)
    for c in range(len(CHUNKS)):
        size = jnp.sum((part_of == c).astype(f32), keepdims=True)
        groups = jnp.floor((size + float(GROUP - 1)) * (1.0 / GROUP))
        spans = jnp.where(lane_w == 2 * c, jnp.broadcast_to(start, (1, count)), spans)
        spans = jnp.where(lane_w == 2 * c + 1, jnp.broadcast_to(groups, (1, count)), spans)
        order = order + jnp.where(
            part_of == c, jnp.broadcast_to(start - before, order.shape), 0.0
        )
        start = start + groups * float(GROUP)
        before = before + size
    goal_hi = (first * width + lead).astype(f32)
    ranks = lax.broadcasted_iota(i32, (count, 128), 0).astype(f32)
    seats = row.astype(f32)
    sub = lax.broadcasted_iota(i32, (8, 128), 0)
    lane_f = lanes_of((8, 128)).astype(f32)
    found = jnp.zeros((8, count), f32)
    marks = jnp.zeros((32, 128), f32)
    nt = (((1,), (1,)), ((), ()))
    for r in range(8):
        at = jnp.broadcast_to(order[r : r + 1, :], (count, 128)) == ranks
        goal = jnp.broadcast_to(goal_hi[r : r + 1, :], (8, 128))
        seat = jnp.broadcast_to(slot[r : r + 1, :], (8, 128))
        values = jnp.where(
            sub == 0, 2.0 * lane_f - (lanes_of((8, 128)) % 8).astype(f32),
            jnp.where(sub == 1, float(r), jnp.where(sub == 2, goal, jnp.where(sub == 3, seat, 1.0))),
        )
        found = found + lax.dot_general(
            values.astype(bf16), at.astype(f32).astype(bf16), nt, preferred_element_type=f32
        )
        both = jnp.concatenate(
            [scaled[pl.ds(r, 16, stride=8), :], picked[pl.ds(r, 16, stride=8), :]], axis=0
        )
        sits = jnp.broadcast_to(slot[r : r + 1, :], square) == seats
        marks = marks + lax.dot_general(
            both.astype(bf16), sits.astype(f32).astype(bf16), nt, preferred_element_type=f32
        )
    lines = (found[0:1] + found[1:2] * 256.0).astype(i32)
    goals = (found[2:3] * float(cap_rows(cap)) + found[3:4] + found[4:5]).astype(i32)
    for n, values in enumerate((lines, goals)):
        for r in range(count // 128):
            at = n * (count // 128) + r
            table[at : at + 1, :] = values[:, 128 * r : 128 * r + 128]
    at = 2 * (count // 128)
    table[at : at + 1, :] = spans[:, :128].astype(i32)
    label = marks[:16] + 256.0 * (1.0 - marks[16:])
    for d in range(16):
        total = jnp.sum(marks[16 + d : 17 + d], axis=1, keepdims=True)
        labels[d] = jnp.where(
            sub == 0,
            jnp.broadcast_to(label[d : d + 1], (8, 128)),
            jnp.broadcast_to(total, (8, 128)),
        )


def cap_rows(cap):
    return cap + 1


def route(here, plan, leaf):
    bins = plan.shape[0]
    return pl.pallas_call(
        route_kernel,
        out_shape=(
            jax.ShapeDtypeStruct((24, 128), i32),
            jax.ShapeDtypeStruct((16, 8, 128), f32),
        ),
        in_specs=[SMEM, VMEM, VMEM],
        out_specs=(VMEM, VMEM),
        scratch_shapes=[pltpu.VMEM((128, 128), f32)] * 2,
        name="route",
    )(here, plan.reshape(bins // 128, 128), leaf.reshape(bins // 128, 128))


GROUP = 16
ENTRIES = 1152


def expand_kernel(chunk, table, labels, pts, *refs):
    outs = refs[:4]
    held, all_pts = refs[4:6]
    stage, bx, by, bz, sems, load_sems = refs[6:]
    first = sum(len(c) for c in CHUNKS[:chunk])
    wide = len(CHUNKS[chunk])
    rows = outs[0].shape[1]
    cap = rows - 1
    span = all_pts.shape[0] // 5
    loads = [
        pltpu.make_async_copy(
            pts.at[pl.ds(span * axis, span)], all_pts.at[pl.ds(span * axis, span)],
            load_sems.at[axis],
        )
        for axis in range(5)
    ]
    for load in loads:
        load.start()
    for k in range(4):
        for n in range(wide):
            held[1 + (k * wide + n) * rows + cap] = labels[4 * (first + n) + k]
    begin = table[2 * ENTRIES + 2 * chunk]
    trips = table[2 * ENTRIES + 2 * chunk + 1]
    for load in loads:
        load.wait()

    def fetch(g, u, bank):
        line = table[begin + g * GROUP + u]
        for axis in range(3):
            for h in range(2):
                stage[bank, axis, h, pl.ds(u, 1), :] = all_pts[
                    pl.ds(line + (span * axis + 8 * h), 1), :
                ]

    def tabulate(piece, bank):
        u, h, axis = 8 * (piece // 6), piece // 3 % 2, piece % 3
        values = basis(stage[bank, axis, h, pl.ds(u, 8), :])
        for a in range(8):
            if axis == 1:
                by[bank, h, pl.ds(GROUP * a + u, 8), :] = values[a]
            else:
                ref = bz if axis else bx
                ref[bank, h, pl.ds(8 * u + a, 8, stride=8), :] = values[a]

    def consume(g, u, bank):
        base = begin + g * GROUP
        line = table[base + u]
        weighted, pair = [], []
        for h in range(2):
            lx = bx[bank, h, pl.ds(8 * u, 8), :]
            lz = bz[bank, h, pl.ds(8 * u, 8), :]
            re, im = (
                jnp.broadcast_to(
                    all_pts[pl.ds(line + (span * (3 + part) + 8 * h), 1), :], lx.shape
                )
                for part in range(2)
            )
            weighted.append(jnp.concatenate([re * lx, im * lx], axis=0).astype(jnp.bfloat16))
            pair.append(
                jnp.concatenate(
                    [
                        jnp.broadcast_to(by[bank, h, pl.ds(GROUP * b + u, 1), :], lz.shape) * lz
                        for b in range(8)
                    ],
                    axis=0,
                ).astype(jnp.bfloat16)
            )
        res = lax.dot_general(
            jnp.concatenate(weighted, axis=1),
            jnp.concatenate(pair, axis=1),
            (((1,), (1,)), ((), ())),
            preferred_element_type=f32,
        )
        held[table[base + (ENTRIES + u)]] = jnp.concatenate([res[:8], res[8:]], axis=1)

    pieces = 6 * GROUP // 8
    for u in range(GROUP):
        fetch(0, u, 0)
    for piece in range(pieces):
        tabulate(piece, 0)
    for u in range(GROUP):
        fetch(1, u, 1)

    def step(g, carry):
        bank = g & 1
        for u in range(GROUP):
            consume(g, u, bank)
            if u % 4 == 3:
                for piece in range(3 * (u // 4), 3 * (u // 4) + 3):
                    tabulate(piece, 1 - bank)
                for v in range(u - 3, u + 1):
                    fetch(g + 2, v, bank)
        return carry

    lax.fori_loop(0, trips, step, 0)
    copies = []
    for k in range(4):
        for n in range(wide):
            copies.append(
                pltpu.make_async_copy(
                    held.at[pl.ds(1 + (k * wide + n) * rows, rows)], outs[k].at[n], sems.at[k, n]
                )
            )
    for copy in copies:
        copy.start()
    for copy in copies:
        copy.wait()


def expand(chunk, table, labels, pts, cap):
    wide = len(CHUNKS[chunk])
    return pl.pallas_call(
        functools.partial(expand_kernel, chunk),
        out_shape=[jax.ShapeDtypeStruct((wide, cap + 1, 8, 128), f32)] * 4,
        in_specs=[SMEM, VMEM, ANY],
        out_specs=[ANY] * 4,
        scratch_shapes=[
            pltpu.VMEM((4 * wide * (cap + 1) + 1, 8, 128), f32),
            pltpu.VMEM(pts.shape, f32),
            pltpu.VMEM((2, 3, 2, GROUP, 128), f32),
            *[pltpu.VMEM((2, 2, 8 * GROUP, 128), f32)] * 3,
            pltpu.SemaphoreType.DMA((4, wide)),
            pltpu.SemaphoreType.DMA((5,)),
        ],
        cost_estimate=pl.CostEstimate(
            flops=wide * (1 << 28), bytes_accessed=1 << 23, transcendentals=0
        ),
        name="expand",
    )(table, labels, pts)


def gather_kernel(wide, *refs):
    arrived, outs = refs[:4], refs[4 : 4 + wide]
    held, labels, names, sem, sems = refs[4 + wide :]
    cap = held.shape[2] - 1
    loads = [pltpu.make_async_copy(arrived[k], held.at[k], sems.at[k]) for k in range(4)]
    for load in loads:
        load.start()
    for out in outs:
        out[...] = jnp.zeros(out.shape, f32)
    for load in loads:
        load.wait()
    for k in range(4):
        for n in range(wide):
            labels[pl.ds(8 * (k * wide + n), 8), :] = held[k, n, cap].astype(i32)
    copy = pltpu.make_async_copy(labels, names, sem)
    copy.start()
    copy.wait()
    for k in range(4):
        most = names[8 * k * wide + 1, 0]
        for n in range(1, wide):
            most = jnp.maximum(most, names[8 * (k * wide + n) + 1, 0])

        def rows4(r, carry):
            for u in range(4):
                for n in range(wide):
                    slot = r * 4 + u
                    where = names[8 * (k * wide + n), slot]
                    outs[n][where] = outs[n][where] + held[k, n, slot]
            return carry

        lax.fori_loop(0, (most + 3) // 4, rows4, 0)


def gather(arrived, leaf_count):
    wide, rows = arrived[0].shape[:2]
    return pl.pallas_call(
        functools.partial(gather_kernel, wide),
        out_shape=[jax.ShapeDtypeStruct((leaf_count + 1, 8, 128), f32)] * wide,
        in_specs=[pl.BlockSpec(memory_space=pl.ANY)] * 4,
        out_specs=[VMEM] * wide,
        scratch_shapes=[
            pltpu.VMEM((4, wide, rows, 8, 128), f32),
            pltpu.VMEM((32 * wide, 128), i32),
            pltpu.SMEM((32 * wide, 128), i32),
            pltpu.SemaphoreType.DMA(()),
            pltpu.SemaphoreType.DMA((4,)),
        ],
        cost_estimate=pl.CostEstimate(
            flops=wide * (1 << 26), bytes_accessed=wide << 22, transcendentals=0
        ),
        name="gather",
    )(*arrived)


def rows_of(shape):
    return lax.broadcasted_iota(i32, shape, len(shape) - 2)


def swap_rows(t):
    even = rows_of(t.shape) % 2 == 0
    axis = len(t.shape) - 2
    return jnp.where(even, pltpu.roll(t, 7, axis), pltpu.roll(t, 1, axis))


def spin(t, cosine, sine):
    return t * cosine + swap_rows(t) * sine


def row_mix(t, maps, bit):
    flipped = pltpu.roll(t, 64, 2)
    total = None
    for step in range(4):
        for flip in range(2):
            part = flipped if flip else t
            if step:
                part = pltpu.roll(part, 8 - 2 * step, 1)
            term = part * maps[bit, 2 * step + flip]
            total = term if total is None else total + term
    return total


SEATS = 36


def phases_kernel(
    here, slots, boxes, cones, box_cones, e0c, e0s, e1c, e1s, e2c, e2s, p0c, p0s, p1c, p1s, goal
):
    side = here[2]
    for o in range(8):

        def child(j, carry):
            p = slots[o, j]
            e = cones[p] * 8 + o
            p0c[o, j] = e0c[e]
            p0s[o, j] = e0s[e]
            owner = p >> 5
            goal[o, j] = ((((owner & 1) ^ side) << 2) + (owner >> 1)) * SEATS + (p & 31)
            q = boxes[o, j]
            a = cones[8 * j + o]
            b = box_cones[q] * 8 + o
            ca, sa, cb, sb = e1c[a], e1s[a], e2c[b], e2s[b]
            p1c[o, j] = ca * cb - sa * sb
            p1s[o, j] = sa * cb + ca * sb
            owner = q >> 2
            goal[8 + o, j] = ((((owner & 1) ^ side) << 2) + (owner >> 1)) * SEATS + 32 + (q & 3)
            return carry

        lax.fori_loop(0, 32, child, 0, unroll=4)


def translate(t, both, rows, octant):
    count = t.shape[0]
    flat = t.reshape(count * 8, 128)
    high = flat.astype(jnp.bfloat16)
    low = (flat - high.astype(f32)).astype(jnp.bfloat16)
    res = jnp.dot(
        jnp.concatenate([high, low], axis=1), both[octant % 4], preferred_element_type=f32
    )
    return row_mix((res[:, :128] + res[:, 128:]).reshape(count, 8, 128), rows, octant // 4)


def levels_kernel(
    here, goal, a0, a1, a2, a3, p0c, p0s, p1c, p1s, both, rows, leaves, mine, other, acc, moved
):
    acc[...] = jnp.zeros(acc.shape, f32)
    step = 16
    shape = (step, 8, 128)
    own = rows_of(shape) % 2 == lanes_of(shape) // 64

    def settle(n, carry):
        base = pl.multiple_of(n * step, step)
        t = (a0[pl.ds(base, step)] + a1[pl.ds(base, step)]) + (
            a2[pl.ds(base, step)] + a3[pl.ds(base, step)]
        )
        leaves[pl.ds(base, step)] = jnp.where(own, t, swap_rows(pltpu.roll(t, 64, 2)))
        return carry

    lax.fori_loop(0, leaves.shape[0] // step, settle, 0)

    def spread(o, lead):
        for start in range(0, 32, 8):
            spots = [goal[lead + o, start + j] for j in range(8)]
            sums = [acc[spots[j]] + moved[o % 2, start + j] for j in range(8)]
            for j in range(8):
                acc[spots[j]] = sums[j]

    for o in range(8):
        for part in range(0, 32, 8):
            t = jnp.stack([leaves[8 * (part + j) + o] for j in range(8)])
            t = spin(t, p0c[o, part : part + 8], p0s[o, part : part + 8])
            moved[o % 2, part : part + 8] = translate(t, both, rows, o)
        spread(o, 0)

    apart = [here[2] * 4 * SEATS, (1 - here[2]) * 4 * SEATS]
    for o in range(8):
        for part in range(0, 32, 8):
            tiles = []
            for j in range(8):
                p = 8 * (part + j) + o
                owner = p // 32
                tiles.append(acc[(owner // 2) * SEATS + p % 32 + apart[owner % 2]])
            t = spin(jnp.stack(tiles), p1c[o, part : part + 8], p1s[o, part : part + 8])
            moved[o % 2, part : part + 8] = translate(t, both, rows, o)
        spread(o, 8)
    for z in range(4):
        mine[z] = acc[pl.ds(z * SEATS, SEATS)]
        other[z] = acc[pl.ds((4 + z) * SEATS, SEATS)]


def merge_kernel(here, mine, got, *outs):
    for k in range(4):
        z = (here[3] + k) % 4
        outs[k][...] = mine[z] + got[z]


def close_kernel(here, cones, box_cones, g0, g1, g2, g3, e1c, e1s, e3c, e3s, out_one, out_two):
    owned, upper = out_one.shape[0], out_two.shape[0]
    me = 2 * here[3] + here[2]
    for n in range(SEATS):
        t = (g0[n] + g1[n]) + (g2[n] + g3[n])
        if n < owned:
            e = cones[me * owned + n]
            out_one[n] = spin(t, e1c[e], e1s[e])
        else:
            e = box_cones[me * upper + n - owned]
            out_two[n - owned] = spin(t, e3c[e], e3s[e])


def phase_tables(directions, kappa, places):
    grid = jnp.asarray(places.astype(np.float32))
    angle = (
        directions[:, 0, None, None, None] * grid[None, :, 0]
        + directions[:, 1, None, None, None] * grid[None, :, 1]
        + directions[:, 2, None, None, None] * grid[None, :, 2]
    )
    angle = (kappa * angle).reshape(-1, 8, 128)
    sign = jnp.where(lax.broadcasted_iota(i32, (1, 8, 128), 1) % 2 == 0, -1.0, 1.0).astype(f32)
    return jnp.cos(angle), jnp.sin(angle) * sign


def to_nodes(tiles):
    count = tiles.shape[0]
    return tiles.reshape(count, 4, 2, 128).transpose(0, 2, 1, 3).reshape(count, 2, 512)


def cone_vectors(cone_angles):
    azimuth = cone_angles[:, 0]
    polar = cone_angles[:, 1]
    return jnp.stack(
        [jnp.cos(azimuth) * jnp.sin(polar), jnp.sin(azimuth) * jnp.sin(polar), jnp.cos(polar)],
        axis=1,
    )


def hop(x, shift, leg, groups):
    pairs = []
    for s in range(16):
        for g in range(groups):
            y, x0 = s // 4, s % 4
            if g % 2 == leg:
                x0 = (x0 + shift) % 4
            else:
                y = (y + shift) % 4
            pairs.append((s * groups + g, (4 * y + x0) * groups + g))
    return lax.ppermute(x, ("sfc", "grp"), pairs)


def around(x, shift, groups):
    pairs = [(g, (g + 2 * shift) % groups) for g in range(groups)]
    return lax.ppermute(x, "grp", pairs)


def after(value, *others):
    return lax.optimization_barrier((value, *others))[0]


def per_device(
    bin_points, bin_plan, bin_leaf, leaf_slots, box_slots, parent_cone, box_cone, cone_angles
):
    groups = lax.axis_size("grp")
    rank = lax.axis_index("grp")
    cap = bin_points.shape[0] // 8
    leaf_count = leaf_slots.shape[2] * 8
    first_owned = parent_cone.shape[1] // groups
    second_owned = box_cone.shape[1] // groups
    tile = jax.ShapeDtypeStruct((8, 128), f32)

    def tiles(*lead):
        return jax.ShapeDtypeStruct((*lead, *tile.shape), f32)

    me = lax.axis_index("sfc")
    here = jnp.stack([me % 4, me // 4, rank % 2, rank // 2]).astype(i32)
    table, labels = route(here, bin_plan[:, 0], bin_leaf)
    table = table.reshape(-1)
    bins, _, width = bin_points.shape
    pts = jnp.transpose(bin_points.reshape(bins // 8, 8, 5, width // 128, 128), (2, 0, 3, 1, 4))
    pts = pts.reshape(-1, 128)
    arrived = []
    for c in range(len(CHUNKS)):
        sent = expand(c, table, labels, pts, cap)
        table = after(table, sent[0])
        moved = [sent[0]]
        for k in (2, 1, 3):
            moved.append(hop(sent[k], k, 0, groups))
        arrived.append(moved)

    cone_angles = after(cone_angles, sent[0])
    directions = cone_vectors(cone_angles)
    child = np.stack(
        [
            tile_of_nodes(child_axis(o // 4), child_axis(o // 2 % 2), child_axis(o % 2))
            for o in range(8)
        ]
    )
    nodes = cheb_nodes()
    parent = tile_of_nodes(nodes, nodes, nodes)[None]
    e0c, e0s = phase_tables(directions, kappa_leaf, child)
    e1c, e1s = phase_tables(directions, -kappa_leaf, parent)
    e2c, e2s = phase_tables(directions, kappa_box, child)
    e3c, e3s = phase_tables(directions, -kappa_box, parent)
    make_phases = pl.pallas_call(
        phases_kernel,
        out_shape=(tiles(8, 32),) * 4 + (jax.ShapeDtypeStruct((16, 32), i32),),
        in_specs=[SMEM] * 5 + [VMEM] * 6,
        out_specs=(VMEM,) * 4 + (SMEM,),
        name="phases",
    )
    p0c, p0s, p1c, p1s, goal = make_phases(
        here, leaf_slots[0], box_slots[0], parent_cone[0], box_cone[0],
        e0c, e0s, e1c, e1s, e2c, e2s,
    )

    held = [None] * 4
    last = sent[0]
    for c, chunk in enumerate(CHUNKS):
        got = [after(arrived[c][0], last)] + arrived[c][1:]
        sums = gather(got, leaf_count)
        last = sums[0]
        for m, part in zip(chunk, sums):
            held[m] = hop(part, m, 1, groups) if m else part

    leaves, mine, other = pl.pallas_call(
        levels_kernel,
        out_shape=(tiles(leaf_count), tiles(4, SEATS), tiles(4, SEATS)),
        in_specs=[SMEM] * 2 + [VMEM] * 10,
        out_specs=(VMEM,) * 3,
        scratch_shapes=[
            pltpu.VMEM((8 * SEATS, 8, 128), f32),
            pltpu.VMEM((2, 32, 8, 128), f32),
        ],
        name="levels",
    )(
        here, goal, *held, p0c, p0s, p1c, p1s,
        jnp.asarray(lane_maps()), jnp.asarray(row_maps()),
    )
    swapped = lax.ppermute(other, "grp", [(g, g ^ 1) for g in range(groups)])
    blocks = pl.pallas_call(
        merge_kernel,
        out_shape=(tiles(SEATS),) * 4,
        in_specs=[SMEM] + [VMEM] * 2,
        out_specs=(VMEM,) * 4,
        name="merge",
    )(here, mine, swapped)
    got = [blocks[0]] + [around(blocks[k], k, groups) for k in (1, 2, 3)]
    one, two = pl.pallas_call(
        close_kernel,
        out_shape=(tiles(first_owned), tiles(second_owned)),
        in_specs=[SMEM] * 3 + [VMEM] * 8,
        out_specs=(VMEM, VMEM),
        name="close",
    )(here, parent_cone[0], box_cone[0], *got, e1c, e1s, e3c, e3s)
    return (to_nodes(leaves), to_nodes(one), to_nodes(two))


def solution(mesh):
    placed = (
        P(("sfc", "grp"), None, None),
        P(("sfc", "grp"), None),
        P(("sfc", "grp")),
        P("sfc", None, "grp"),
        P("sfc", None, None),
        P("sfc", None),
        P("sfc", None),
        P(),
    )

    return jax.shard_map(
        per_device,
        mesh=mesh,
        in_specs=placed,
        out_specs=(
            P(("sfc", "grp"), None, None),
            P(("sfc", "grp"), None, None),
            P(("sfc", "grp"), None, None),
        ),
        check_vma=False,
    )
```

```python
import functools

import jax
import jax.numpy as jnp
import numpy as np
from jax import lax
from jax.experimental import pallas as pl
from jax.experimental.pallas import tpu as pltpu
from jax.sharding import PartitionSpec as P

kappa_leaf = 2.0
f32 = jnp.float32
i32 = jnp.int32
VMEM = pl.BlockSpec(memory_space=pltpu.VMEM)
SMEM = pl.BlockSpec(memory_space=pltpu.SMEM)
ANY = pl.BlockSpec(memory_space=pl.ANY)


def cheb_nodes():
    return np.cos((2.0 * np.arange(8) + 1.0) * np.pi / 16.0)


def lagrange_np(values):
    nodes = cheb_nodes()
    rows = []
    for center in range(8):
        weight = np.ones_like(values)
        for other in range(8):
            if other != center:
                weight = weight * (values - nodes[other]) / (nodes[center] - nodes[other])
        rows.append(weight)
    return np.stack(rows, axis=0)


def child_axis(bit):
    return 0.5 * (2 * bit - 1) + 0.5 * cheb_nodes()


def axis_maps():
    return np.stack([lagrange_np(child_axis(bit)) for bit in range(2)])


def lane_maps():
    maps = axis_maps()
    out = []
    for pick in range(4):
        both = np.kron(maps[pick // 2], maps[pick % 2])
        full = np.kron(np.eye(2), both).T
        high = full.astype(jnp.bfloat16)
        low = (full - high.astype(np.float64)).astype(jnp.bfloat16)
        out.append(np.block([[high, low], [high, np.zeros_like(low)]]))
    return np.stack(out).astype(jnp.bfloat16)


def row_maps():
    maps = axis_maps()
    rows = np.arange(8)[:, None]
    half = np.arange(128)[None, :] // 64
    k = rows // 2
    out = np.zeros((2, 8, 8, 128), np.float32)
    for bit in range(2):
        for step in range(4):
            for flip in range(2):
                to = 2 * k + half
                frm = 2 * ((k + step) % 4) + (half ^ flip)
                out[bit, 2 * step + flip] = maps[bit][to, frm]
    return out


def basis(x):
    t = cheb_nodes()[:4]
    sq = t * t
    x2 = x * x
    s = [x2 - float(v) for v in sq]
    p01 = s[0] * s[1]
    p23 = s[2] * s[3]
    rest = [s[1] * p23, s[0] * p23, p01 * s[3], p01 * s[2]]
    out = [None] * 8
    for j in range(4):
        scale = 1.0 / (np.prod([sq[j] - sq[i] for i in range(4) if i != j]) * 2.0 * t[j])
        q = rest[j] * float(scale)
        out[j] = q * (x + float(t[j]))
        out[7 - j] = q * (float(t[j]) - x)
    return out


def lanes_of(shape):
    return lax.broadcasted_iota(i32, shape, len(shape) - 1)


def lanes_of(shape):
    return lax.broadcasted_iota(i32, shape, len(shape) - 1)


CHUNKS = ((2,), (1, 3), (0,))
ORDER = tuple(m for chunk in CHUNKS for m in chunk)


def route_kernel(here, plan, leaf, table, labels, picked, scaled):
    bf16 = jnp.bfloat16
    cap = labels.shape[2]
    target = plan[...]
    names = leaf[...].astype(f32)
    along_x = (target - here[0]) % 4
    along_y = (target // 4 - here[1]) % 4
    first = jnp.where(here[2] == 0, along_x, along_y)
    second = jnp.where(here[2] == 0, along_y, along_x)
    place, lead, width, part_of = target * 0, target * 0, target * 0, target * 0
    for c, chunk in enumerate(CHUNKS):
        for n, m in enumerate(chunk):
            hit = second == m
            place = jnp.where(hit, ORDER.index(m), place)
            part_of = jnp.where(hit, c, part_of)
            lead = jnp.where(hit, n, lead)
            width = jnp.where(hit, len(chunk), width)
    code = place * 4 + first
    for d in range(16):
        hit = (code == d).astype(f32)
        picked[pl.ds(8 * d, 8), :] = hit
        scaled[pl.ds(8 * d, 8), :] = hit * names
    square = (128, 128)
    row, lane = rows_of(square), lanes_of(square)
    hits = picked[...].astype(bf16)
    ones = jnp.ones(square, bf16)

    def mul(a, b):
        return jnp.dot(a.astype(bf16), b.astype(bf16), preferred_element_type=f32)

    inside = mul(hits, (row < lane).astype(f32))
    ahead = mul(mul((lane < row).astype(f32), hits), ones)
    same = mul(mul(((lane < row) & (lane // 8 == row // 8)).astype(f32), hits), ones)
    order = jnp.zeros((8, 128), f32)
    slot = jnp.zeros((8, 128), f32)
    for d in range(16):
        part = slice(8 * d, 8 * d + 8)
        hit = picked[pl.ds(8 * d, 8), :]
        order = order + hit * (inside[part] + ahead[part])
        slot = slot + hit * (inside[part] + same[part])
    count = ENTRIES
    lane_w = lanes_of((1, count))
    spans = jnp.zeros((1, count), f32)
    start = jnp.zeros((1, 1), f32)
    before = jnp.zeros((1, 1), f32)
    for c in range(len(CHUNKS)):
        size = jnp.sum((part_of == c).astype(f32), keepdims=True)
        groups = jnp.floor((size + float(GROUP - 1)) * (1.0 / GROUP))
        spans = jnp.where(lane_w == 2 * c, jnp.broadcast_to(start, (1, count)), spans)
        spans = jnp.where(lane_w == 2 * c + 1, jnp.broadcast_to(groups, (1, count)), spans)
        order = order + jnp.where(
            part_of == c, jnp.broadcast_to(start - before, order.shape), 0.0
        )
        start = start + groups * float(GROUP)
        before = before + size
    goal_hi = (first * width + lead).astype(f32)
    ranks = lax.broadcasted_iota(i32, (count, 128), 0).astype(f32)
    seats = row.astype(f32)
    sub = lax.broadcasted_iota(i32, (8, 128), 0)
    lane_f = lanes_of((8, 128)).astype(f32)
    found = jnp.zeros((8, count), f32)
    marks = jnp.zeros((32, 128), f32)
    nt = (((1,), (1,)), ((), ()))
    for r in range(8):
        at = jnp.broadcast_to(order[r : r + 1, :], (count, 128)) == ranks
        goal = jnp.broadcast_to(goal_hi[r : r + 1, :], (8, 128))
        seat = jnp.broadcast_to(slot[r : r + 1, :], (8, 128))
        values = jnp.where(
            sub == 0, 2.0 * lane_f - (lanes_of((8, 128)) % 8).astype(f32),
            jnp.where(sub == 1, float(r), jnp.where(sub == 2, goal, jnp.where(sub == 3, seat, 1.0))),
        )
        found = found + lax.dot_general(
            values.astype(bf16), at.astype(f32).astype(bf16), nt, preferred_element_type=f32
        )
        both = jnp.concatenate(
            [scaled[pl.ds(r, 16, stride=8), :], picked[pl.ds(r, 16, stride=8), :]], axis=0
        )
        sits = jnp.broadcast_to(slot[r : r + 1, :], square) == seats
        marks = marks + lax.dot_general(
            both.astype(bf16), sits.astype(f32).astype(bf16), nt, preferred_element_type=f32
        )
    lines = (found[0:1] + found[1:2] * 256.0).astype(i32)
    goals = (found[2:3] * float(cap_rows(cap)) + found[3:4] + found[4:5]).astype(i32)
    for n, values in enumerate((lines, goals)):
        for r in range(count // 128):
            at = n * (count // 128) + r
            table[at : at + 1, :] = values[:, 128 * r : 128 * r + 128]
    at = 2 * (count // 128)
    table[at : at + 1, :] = spans[:, :128].astype(i32)
    label = marks[:16] + 256.0 * (1.0 - marks[16:])
    for d in range(16):
        total = jnp.sum(marks[16 + d : 17 + d], axis=1, keepdims=True)
        labels[d] = jnp.where(
            sub == 0,
            jnp.broadcast_to(label[d : d + 1], (8, 128)),
            jnp.broadcast_to(total, (8, 128)),
        )


def cap_rows(cap):
    return cap + 1


def route(here, plan, leaf):
    bins = plan.shape[0]
    return pl.pallas_call(
        route_kernel,
        out_shape=(
            jax.ShapeDtypeStruct((24, 128), i32),
            jax.ShapeDtypeStruct((16, 8, 128), f32),
        ),
        in_specs=[SMEM, VMEM, VMEM],
        out_specs=(VMEM, VMEM),
        scratch_shapes=[pltpu.VMEM((128, 128), f32)] * 2,
        name="route",
    )(here, plan.reshape(bins // 128, 128), leaf.reshape(bins // 128, 128))


GROUP = 16
ENTRIES = 1152


def expand_kernel(chunk, table, labels, pts, *refs):
    outs = refs[:4]
    held, all_pts = refs[4:6]
    stage, bx, by, bz, sems, load_sems = refs[6:]
    first = sum(len(c) for c in CHUNKS[:chunk])
    wide = len(CHUNKS[chunk])
    rows = outs[0].shape[1]
    cap = rows - 1
    span = all_pts.shape[0] // 5
    loads = [
        pltpu.make_async_copy(
            pts.at[pl.ds(span * axis, span)], all_pts.at[pl.ds(span * axis, span)],
            load_sems.at[axis],
        )
        for axis in range(5)
    ]
    for load in loads:
        load.start()
    for k in range(4):
        for n in range(wide):
            held[1 + (k * wide + n) * rows + cap] = labels[4 * (first + n) + k]
    begin = table[2 * ENTRIES + 2 * chunk]
    trips = table[2 * ENTRIES + 2 * chunk + 1]
    for load in loads:
        load.wait()

    def fetch(g, u, bank):
        line = table[begin + g * GROUP + u]
        for axis in range(3):
            for h in range(2):
                stage[bank, axis, h, pl.ds(u, 1), :] = all_pts[
                    pl.ds(line + (span * axis + 8 * h), 1), :
                ]

    def tabulate(piece, bank):
        u, h, axis = 8 * (piece // 6), piece // 3 % 2, piece % 3
        values = basis(stage[bank, axis, h, pl.ds(u, 8), :])
        for a in range(8):
            if axis == 1:
                by[bank, h, pl.ds(GROUP * a + u, 8), :] = values[a]
            else:
                ref = bz if axis else bx
                ref[bank, h, pl.ds(8 * u + a, 8, stride=8), :] = values[a]

    def consume(g, u, bank):
        base = begin + g * GROUP
        line = table[base + u]
        weighted, pair = [], []
        for h in range(2):
            lx = bx[bank, h, pl.ds(8 * u, 8), :]
            lz = bz[bank, h, pl.ds(8 * u, 8), :]
            re, im = (
                jnp.broadcast_to(
                    all_pts[pl.ds(line + (span * (3 + part) + 8 * h), 1), :], lx.shape
                )
                for part in range(2)
            )
            weighted.append(jnp.concatenate([re * lx, im * lx], axis=0).astype(jnp.bfloat16))
            pair.append(
                jnp.concatenate(
                    [
                        jnp.broadcast_to(by[bank, h, pl.ds(GROUP * b + u, 1), :], lz.shape) * lz
                        for b in range(8)
                    ],
                    axis=0,
                ).astype(jnp.bfloat16)
            )
        res = lax.dot_general(
            jnp.concatenate(weighted, axis=1),
            jnp.concatenate(pair, axis=1),
            (((1,), (1,)), ((), ())),
            preferred_element_type=f32,
        )
        held[table[base + (ENTRIES + u)]] = jnp.concatenate([res[:8], res[8:]], axis=1)

    pieces = 6 * GROUP // 8
    for u in range(GROUP):
        fetch(0, u, 0)
    for piece in range(pieces):
        tabulate(piece, 0)
    for u in range(GROUP):
        fetch(1, u, 1)

    def step(g, carry):
        bank = g & 1
        for u in range(GROUP):
            consume(g, u, bank)
            if u % 4 == 3:
                for piece in range(3 * (u // 4), 3 * (u // 4) + 3):
                    tabulate(piece, 1 - bank)
                for v in range(u - 3, u + 1):
                    fetch(g + 2, v, bank)
        return carry

    lax.fori_loop(0, trips, step, 0)
    copies = []
    for k in range(4):
        for n in range(wide):
            copies.append(
                pltpu.make_async_copy(
                    held.at[pl.ds(1 + (k * wide + n) * rows, rows)], outs[k].at[n], sems.at[k, n]
                )
            )
    for copy in copies:
        copy.start()
    for copy in copies:
        copy.wait()


def expand(chunk, table, labels, pts, cap):
    wide = len(CHUNKS[chunk])
    return pl.pallas_call(
        functools.partial(expand_kernel, chunk),
        out_shape=[jax.ShapeDtypeStruct((wide, cap + 1, 8, 128), f32)] * 4,
        in_specs=[SMEM, VMEM, ANY],
        out_specs=[ANY] * 4,
        scratch_shapes=[
            pltpu.VMEM((4 * wide * (cap + 1) + 1, 8, 128), f32),
            pltpu.VMEM(pts.shape, f32),
            pltpu.VMEM((2, 3, 2, GROUP, 128), f32),
            *[pltpu.VMEM((2, 2, 8 * GROUP, 128), f32)] * 3,
            pltpu.SemaphoreType.DMA((4, wide)),
            pltpu.SemaphoreType.DMA((5,)),
        ],
        cost_estimate=pl.CostEstimate(
            flops=wide * (1 << 28), bytes_accessed=1 << 23, transcendentals=0
        ),
        name="expand",
    )(table, labels, pts)


def gather_kernel(wide, *refs):
    arrived, outs = refs[:4], refs[4 : 4 + wide]
    held, labels, names, sem, sems = refs[4 + wide :]
    cap = held.shape[2] - 1
    loads = [pltpu.make_async_copy(arrived[k], held.at[k], sems.at[k]) for k in range(4)]
    for load in loads:
        load.start()
    for out in outs:
        out[...] = jnp.zeros(out.shape, f32)
    for load in loads:
        load.wait()
    for k in range(4):
        for n in range(wide):
            labels[pl.ds(8 * (k * wide + n), 8), :] = held[k, n, cap].astype(i32)
    copy = pltpu.make_async_copy(labels, names, sem)
    copy.start()
    copy.wait()
    for k in range(4):
        most = names[8 * k * wide + 1, 0]
        for n in range(1, wide):
            most = jnp.maximum(most, names[8 * (k * wide + n) + 1, 0])

        def rows4(r, carry):
            for u in range(4):
                for n in range(wide):
                    slot = r * 4 + u
                    where = names[8 * (k * wide + n), slot]
                    outs[n][where] = outs[n][where] + held[k, n, slot]
            return carry

        lax.fori_loop(0, (most + 3) // 4, rows4, 0)


def gather(arrived, leaf_count):
    wide, rows = arrived[0].shape[:2]
    return pl.pallas_call(
        functools.partial(gather_kernel, wide),
        out_shape=[jax.ShapeDtypeStruct((leaf_count + 1, 8, 128), f32)] * wide,
        in_specs=[pl.BlockSpec(memory_space=pl.ANY)] * 4,
        out_specs=[VMEM] * wide,
        scratch_shapes=[
            pltpu.VMEM((4, wide, rows, 8, 128), f32),
            pltpu.VMEM((32 * wide, 128), i32),
            pltpu.SMEM((32 * wide, 128), i32),
            pltpu.SemaphoreType.DMA(()),
            pltpu.SemaphoreType.DMA((4,)),
        ],
        cost_estimate=pl.CostEstimate(
            flops=wide * (1 << 26), bytes_accessed=wide << 22, transcendentals=0
        ),
        name="gather",
    )(*arrived)


def rows_of(shape):
    return lax.broadcasted_iota(i32, shape, len(shape) - 2)


def swap_rows(t):
    even = rows_of(t.shape) % 2 == 0
    axis = len(t.shape) - 2
    return jnp.where(even, pltpu.roll(t, 7, axis), pltpu.roll(t, 1, axis))


def spin(t, cosine, sine):
    return t * cosine + swap_rows(t) * sine


def row_mix(t, maps, bit):
    flipped = pltpu.roll(t, 64, 2)
    total = None
    for step in range(4):
        for flip in range(2):
            part = flipped if flip else t
            if step:
                part = pltpu.roll(part, 8 - 2 * step, 1)
            term = part * maps[bit, 2 * step + flip]
            total = term if total is None else total + term
    return total


SEATS = 36


def turn(ca, sa, cb, sb):
    return ca * cb - sa * sb, sa * cb + ca * sb


def twice(c, s):
    return c * c - s * s, 2.0 * (s * c)


def phases_kernel(
    here, slots, boxes, cones, box_cones, cosine, sine, p0c, p0s, p1c, p1s, ec, es, goal,
    t0c, t0s, t1c, t1s, t2c, t2s,
):
    side = here[2]
    sign = jnp.where(rows_of((8, 128)) % 2 == 0, -1.0, 1.0)

    def cone_tables(n, carry):
        xs = [(cosine[n, v], sine[n, v]) for v in range(3)]
        wide = [
            tuple(jnp.broadcast_to(t[n, 3, pl.ds(v, 1), :], (8, 128)) for t in (cosine, sine))
            for v in range(5)
        ]
        t1c[n], t1s[n] = turn(*xs[2], *wide[4])
        xs2 = [twice(*x) for x in xs[:2]]
        for v in range(4):
            wide2 = twice(*wide[v])
            for bit in range(2):
                at = n * 8 + 4 * bit + v
                t0c[at], t0s[at] = turn(*xs[bit], *wide[v])
                t2c[at], t2s[at] = turn(*xs2[bit], *wide2)
        return carry

    lax.fori_loop(0, cosine.shape[0], cone_tables, 0)

    def child(j, carry):
        for o in range(8):
            p = slots[32 * o + j]
            e = cones[p] * 8 + o
            p0c[o, j] = t0c[e]
            p0s[o, j] = t0s[e] * sign
            owner = p >> 5
            goal[32 * o + j] = ((((owner & 1) ^ side) << 2) + (owner >> 1)) * SEATS + (p & 31)
            a = cones[8 * j + o]
            b = box_cones[boxes[32 * o + j]] * 8 + o
            c, s = turn(t1c[a], t1s[a], t2c[b], t2s[b])
            p1c[o, j] = c
            p1s[o, j] = s * sign
        return carry

    lax.fori_loop(0, 32, child, 0)
    me = 2 * here[3] + side
    for n in range(SEATS):
        if n < 32:
            a = cones[32 * me + n]
            c, s = t1c[a], t1s[a]
        else:
            a = box_cones[4 * me + n - 32]
            c, s = twice(t1c[a], t1s[a])
        ec[n] = c
        es[n] = s * sign


def lane_mix(t, both, octant):
    count = t.shape[0]
    flat = t.reshape(count * 8, 128)
    high = flat.astype(jnp.bfloat16)
    low = (flat - high.astype(f32)).astype(jnp.bfloat16)
    res = jnp.dot(
        jnp.concatenate([high, low], axis=1), both[octant % 4], preferred_element_type=f32
    )
    return (res[:, :128] + res[:, 128:]).reshape(count, 8, 128)


def levels_kernel(
    here, goal, boxes, a0, a1, a2, a3, p0c, p0s, p1c, p1s, both, rows, leaves, mine, other,
    acc, upper, moved,
):
    acc[...] = jnp.zeros(acc.shape, f32)
    upper[...] = jnp.zeros(upper.shape, f32)
    step = 16
    shape = (step, 8, 128)
    own = rows_of(shape) % 2 == lanes_of(shape) // 64

    def settle(n, carry):
        base = pl.multiple_of(n * step, step)
        t = (a0[pl.ds(base, step)] + a1[pl.ds(base, step)]) + (
            a2[pl.ds(base, step)] + a3[pl.ds(base, step)]
        )
        leaves[pl.ds(base, step)] = jnp.where(own, t, swap_rows(pltpu.roll(t, 64, 2)))
        return carry

    lax.fori_loop(0, leaves.shape[0] // step, settle, 0)

    def spread(o, start, ref, spots):
        sums = [ref[spots[j]] + moved[o % 2, start + j] for j in range(8)]
        for j in range(8):
            ref[spots[j]] = sums[j]

    for o in range(8):
        for part in range(0, 32, 8):
            t = jnp.stack([leaves[8 * (part + j) + o] for j in range(8)])
            t = spin(t, p0c[o, part : part + 8], p0s[o, part : part + 8])
            moved[o % 2, part : part + 8] = row_mix(lane_mix(t, both, o), rows, o // 4)
        for part in range(0, 32, 8):
            spread(o, part, acc, [goal[32 * o + part + j] for j in range(8)])

    apart = [here[2] * 4 * SEATS, (1 - here[2]) * 4 * SEATS]
    for o in range(8):
        for part in range(0, 32, 8):
            tiles = []
            for j in range(8):
                p = 8 * (part + j) + o
                owner = p // 32
                tiles.append(acc[(owner // 2) * SEATS + p % 32 + apart[owner % 2]])
            t = spin(jnp.stack(tiles), p1c[o, part : part + 8], p1s[o, part : part + 8])
            moved[o % 2, part : part + 8] = lane_mix(t, both, o)
        for part in range(0, 32, 8):
            spread(
                o, part, upper,
                [boxes[32 * o + part + j] + 32 * (o // 4) for j in range(8)],
            )
    for part in range(0, 32, 8):
        t = row_mix(upper[part : part + 8], rows, 0) + row_mix(upper[32 + part : 40 + part], rows, 1)
        for j in range(8):
            q = part + j
            owner = q // 4
            acc[(owner // 2) * SEATS + 32 + q % 4 + apart[owner % 2]] = t[j]
    for k in range(4):
        z = (here[3] + k) % 4
        mine[k] = acc[pl.ds(z * SEATS, SEATS)]
        other[k] = acc[pl.ds((4 + z) * SEATS, SEATS)]


def close_kernel(g0, g1, g2, g3, ec, es, out_one, out_two):
    owned = out_one.shape[0]
    for n in range(SEATS):
        t = spin((g0[n] + g1[n]) + (g2[n] + g3[n]), ec[n], es[n])
        if n < owned:
            out_one[n] = t
        else:
            out_two[n - owned] = t


def cone_places():
    nodes = cheb_nodes()
    rows = np.arange(8)[:, None]
    lanes = np.arange(128)[None, :]
    a = 2 * (rows // 2) + lanes // 64
    out = np.zeros((3, 4, 8, 128))
    out[0, 0], out[0, 1], out[0, 2] = child_axis(0)[a], child_axis(1)[a], -nodes[a]
    b, c = np.arange(128) % 64 // 8, np.arange(128) % 8
    for v in range(4):
        out[1, 3, v], out[2, 3, v] = child_axis(v // 2)[b], child_axis(v % 2)[c]
    out[1, 3, 4], out[2, 3, 4] = -nodes[b], -nodes[c]
    return out.astype(np.float32)


def to_nodes(tiles):
    count = tiles.shape[0]
    return tiles.reshape(count, 4, 2, 128).transpose(0, 2, 1, 3).reshape(count, 2, 512)


def cone_vectors(cone_angles):
    azimuth = cone_angles[:, 0]
    polar = cone_angles[:, 1]
    return jnp.stack(
        [jnp.cos(azimuth) * jnp.sin(polar), jnp.sin(azimuth) * jnp.sin(polar), jnp.cos(polar)],
        axis=1,
    )


def hop(x, shift, leg, groups):
    pairs = []
    for s in range(16):
        for g in range(groups):
            y, x0 = s // 4, s % 4
            if g % 2 == leg:
                x0 = (x0 + shift) % 4
            else:
                y = (y + shift) % 4
            pairs.append((s * groups + g, (4 * y + x0) * groups + g))
    return lax.ppermute(x, ("sfc", "grp"), pairs)


def around(x, shift, groups):
    pairs = [(g, (g + 2 * shift) % groups) for g in range(groups)]
    return lax.ppermute(x, "grp", pairs)


def after(value, *others):
    return lax.optimization_barrier((value, *others))[0]


def per_device(
    bin_points, bin_plan, bin_leaf, leaf_slots, box_slots, parent_cone, box_cone, cone_angles
):
    groups = lax.axis_size("grp")
    rank = lax.axis_index("grp")
    cap = bin_points.shape[0] // 8
    leaf_count = leaf_slots.shape[2] * 8
    first_owned = parent_cone.shape[1] // groups
    second_owned = box_cone.shape[1] // groups
    tile = jax.ShapeDtypeStruct((8, 128), f32)

    def tiles(*lead):
        return jax.ShapeDtypeStruct((*lead, *tile.shape), f32)

    me = lax.axis_index("sfc")
    here = jnp.stack([me % 4, me // 4, rank % 2, rank // 2]).astype(i32)
    table, labels = route(here, bin_plan[:, 0], bin_leaf)
    table = table.reshape(-1)
    bins, _, width = bin_points.shape
    pts = jnp.transpose(bin_points.reshape(bins // 8, 8, 5, width // 128, 128), (2, 0, 3, 1, 4))
    pts = pts.reshape(-1, 128)
    arrived = []
    for c in range(len(CHUNKS)):
        sent = expand(c, table, labels, pts, cap)
        table = after(table, sent[0])
        moved = [sent[0]]
        for k in (2, 1, 3):
            moved.append(hop(sent[k], k, 0, groups))
        arrived.append(moved)

    cone_angles = after(cone_angles, sent[0])
    directions = cone_vectors(cone_angles)
    places = jnp.asarray(cone_places())
    angle = (
        directions[:, 0, None, None, None] * places[None, 0]
        + directions[:, 1, None, None, None] * places[None, 1]
        + directions[:, 2, None, None, None] * places[None, 2]
    ) * kappa_leaf
    make_phases = pl.pallas_call(
        phases_kernel,
        out_shape=(tiles(8, 32),) * 4 + (tiles(SEATS),) * 2 + (jax.ShapeDtypeStruct((256,), i32),),
        in_specs=[SMEM] * 5 + [VMEM] * 2,
        out_specs=(VMEM,) * 6 + (SMEM,),
        scratch_shapes=[pltpu.VMEM((n, 8, 128), f32) for n in (128, 128, 16, 16, 128, 128)],
        name="phases",
    )
    slots, boxes = leaf_slots.reshape(-1), box_slots.reshape(-1)
    p0c, p0s, p1c, p1s, ec, es, goal = make_phases(
        here, slots, boxes, parent_cone[0], box_cone[0], jnp.cos(angle), jnp.sin(angle)
    )

    held = [None] * 4
    last = sent[0]
    for c, chunk in enumerate(CHUNKS):
        got = [after(arrived[c][0], last)] + arrived[c][1:]
        sums = gather(got, leaf_count)
        last = sums[0]
        for m, part in zip(chunk, sums):
            held[m] = hop(part, m, 1, groups) if m else part

    leaves, mine, other = pl.pallas_call(
        levels_kernel,
        out_shape=(tiles(leaf_count), tiles(4, SEATS), tiles(4, SEATS)),
        in_specs=[SMEM] * 3 + [VMEM] * 10,
        out_specs=(VMEM,) * 3,
        scratch_shapes=[
            pltpu.VMEM((8 * SEATS, 8, 128), f32),
            pltpu.VMEM((64, 8, 128), f32),
            pltpu.VMEM((2, 32, 8, 128), f32),
        ],
        name="levels",
    )(
        here, goal, boxes, *held, p0c, p0s, p1c, p1s,
        jnp.asarray(lane_maps()), jnp.asarray(row_maps()),
    )
    swapped = lax.ppermute(other, "grp", [(g, g ^ 1) for g in range(groups)])
    blocks = [mine[k] + swapped[k] for k in range(4)]
    got = [blocks[0]] + [around(blocks[k], k, groups) for k in (1, 2, 3)]
    one, two = pl.pallas_call(
        close_kernel,
        out_shape=(tiles(first_owned), tiles(second_owned)),
        in_specs=[VMEM] * 6,
        out_specs=(VMEM, VMEM),
        name="close",
    )(*got, ec, es)
    return (to_nodes(leaves), to_nodes(one), to_nodes(two))


def solution(mesh):
    placed = (
        P(("sfc", "grp"), None, None),
        P(("sfc", "grp"), None),
        P(("sfc", "grp")),
        P("sfc", None, "grp"),
        P("sfc", None, None),
        P("sfc", None),
        P("sfc", None),
        P(),
    )

    return jax.shard_map(
        per_device,
        mesh=mesh,
        in_specs=placed,
        out_specs=(
            P(("sfc", "grp"), None, None),
            P(("sfc", "grp"), None, None),
            P(("sfc", "grp"), None, None),
        ),
        check_vma=False,
    )
```

```python
import functools

import jax
import jax.numpy as jnp
import numpy as np
from jax import lax
from jax.experimental import pallas as pl
from jax.experimental.pallas import tpu as pltpu
from jax.sharding import PartitionSpec as P

kappa_leaf = 2.0
f32 = jnp.float32
i32 = jnp.int32
VMEM = pl.BlockSpec(memory_space=pltpu.VMEM)
SMEM = pl.BlockSpec(memory_space=pltpu.SMEM)
ANY = pl.BlockSpec(memory_space=pl.ANY)


def cheb_nodes():
    return np.cos((2.0 * np.arange(8) + 1.0) * np.pi / 16.0)


def lagrange_np(values):
    nodes = cheb_nodes()
    rows = []
    for center in range(8):
        weight = np.ones_like(values)
        for other in range(8):
            if other != center:
                weight = weight * (values - nodes[other]) / (nodes[center] - nodes[other])
        rows.append(weight)
    return np.stack(rows, axis=0)


def child_axis(bit):
    return 0.5 * (2 * bit - 1) + 0.5 * cheb_nodes()


def axis_maps():
    return np.stack([lagrange_np(child_axis(bit)) for bit in range(2)])


def lane_maps():
    maps = axis_maps()
    out = []
    for pick in range(4):
        both = np.kron(maps[pick // 2], maps[pick % 2])
        full = np.kron(np.eye(2), both).T
        high = full.astype(jnp.bfloat16)
        low = (full - high.astype(np.float64)).astype(jnp.bfloat16)
        out.append(np.block([[high, low], [high, np.zeros_like(low)]]))
    return np.stack(out).astype(jnp.bfloat16)


def row_maps():
    maps = axis_maps()
    rows = np.arange(8)[:, None]
    half = np.arange(128)[None, :] // 64
    k = rows // 2
    out = np.zeros((2, 8, 8, 128), np.float32)
    for bit in range(2):
        for step in range(4):
            for flip in range(2):
                to = 2 * k + half
                frm = 2 * ((k + step) % 4) + (half ^ flip)
                out[bit, 2 * step + flip] = maps[bit][to, frm]
    return out


def basis(x):
    t = cheb_nodes()[:4]
    sq = t * t
    x2 = x * x
    s = [x2 - float(v) for v in sq]
    p01 = s[0] * s[1]
    p23 = s[2] * s[3]
    rest = [s[1] * p23, s[0] * p23, p01 * s[3], p01 * s[2]]
    out = [None] * 8
    for j in range(4):
        scale = 1.0 / (np.prod([sq[j] - sq[i] for i in range(4) if i != j]) * 2.0 * t[j])
        q = rest[j] * float(scale)
        out[j] = q * (x + float(t[j]))
        out[7 - j] = q * (float(t[j]) - x)
    return out


def lanes_of(shape):
    return lax.broadcasted_iota(i32, shape, len(shape) - 1)


def lanes_of(shape):
    return lax.broadcasted_iota(i32, shape, len(shape) - 1)


CHUNKS = ((2,), (1, 3), (0,))
ORDER = tuple(m for chunk in CHUNKS for m in chunk)


def route(here, plan, leaf, table, labels, picked, scaled):
    bf16 = jnp.bfloat16
    cap = labels.shape[2]
    target = plan[...]
    names = leaf[...].astype(f32)
    along_x = (target - here[0]) % 4
    along_y = (target // 4 - here[1]) % 4
    first = jnp.where(here[2] == 0, along_x, along_y)
    second = jnp.where(here[2] == 0, along_y, along_x)
    place, lead, width, part_of = target * 0, target * 0, target * 0, target * 0
    for c, chunk in enumerate(CHUNKS):
        for n, m in enumerate(chunk):
            hit = second == m
            place = jnp.where(hit, ORDER.index(m), place)
            part_of = jnp.where(hit, c, part_of)
            lead = jnp.where(hit, n, lead)
            width = jnp.where(hit, len(chunk), width)
    code = place * 4 + first
    for d in range(16):
        hit = (code == d).astype(f32)
        picked[pl.ds(8 * d, 8), :] = hit
        scaled[pl.ds(8 * d, 8), :] = hit * names
    square = (128, 128)
    row, lane = rows_of(square), lanes_of(square)
    hits = picked[...].astype(bf16)
    ones = jnp.ones(square, bf16)

    def mul(a, b):
        return jnp.dot(a.astype(bf16), b.astype(bf16), preferred_element_type=f32)

    inside = mul(hits, (row < lane).astype(f32))
    ahead = mul(mul((lane < row).astype(f32), hits), ones)
    same = mul(mul(((lane < row) & (lane // 8 == row // 8)).astype(f32), hits), ones)
    order = jnp.zeros((8, 128), f32)
    slot = jnp.zeros((8, 128), f32)
    for d in range(16):
        part = slice(8 * d, 8 * d + 8)
        hit = picked[pl.ds(8 * d, 8), :]
        order = order + hit * (inside[part] + ahead[part])
        slot = slot + hit * (inside[part] + same[part])
    count = ENTRIES
    lane_w = lanes_of((1, count))
    spans = jnp.zeros((1, count), f32)
    start = jnp.zeros((1, 1), f32)
    before = jnp.zeros((1, 1), f32)
    for c in range(len(CHUNKS)):
        size = jnp.sum((part_of == c).astype(f32), keepdims=True)
        groups = jnp.floor((size + float(GROUP - 1)) * (1.0 / GROUP))
        spans = jnp.where(lane_w == 2 * c, jnp.broadcast_to(start, (1, count)), spans)
        spans = jnp.where(lane_w == 2 * c + 1, jnp.broadcast_to(groups, (1, count)), spans)
        order = order + jnp.where(
            part_of == c, jnp.broadcast_to(start - before, order.shape), 0.0
        )
        start = start + groups * float(GROUP)
        before = before + size
    goal_hi = (first * width + lead).astype(f32)
    ranks = lax.broadcasted_iota(i32, (count, 128), 0).astype(f32)
    seats = row.astype(f32)
    sub = lax.broadcasted_iota(i32, (8, 128), 0)
    lane_f = lanes_of((8, 128)).astype(f32)
    found = jnp.zeros((8, count), f32)
    marks = jnp.zeros((32, 128), f32)
    nt = (((1,), (1,)), ((), ()))
    for r in range(8):
        at = jnp.broadcast_to(order[r : r + 1, :], (count, 128)) == ranks
        goal = jnp.broadcast_to(goal_hi[r : r + 1, :], (8, 128))
        seat = jnp.broadcast_to(slot[r : r + 1, :], (8, 128))
        values = jnp.where(
            sub == 0, 2.0 * lane_f - (lanes_of((8, 128)) % 8).astype(f32),
            jnp.where(sub == 1, float(r), jnp.where(sub == 2, goal, jnp.where(sub == 3, seat, 1.0))),
        )
        found = found + lax.dot_general(
            values.astype(bf16), at.astype(f32).astype(bf16), nt, preferred_element_type=f32
        )
        both = jnp.concatenate(
            [scaled[pl.ds(r, 16, stride=8), :], picked[pl.ds(r, 16, stride=8), :]], axis=0
        )
        sits = jnp.broadcast_to(slot[r : r + 1, :], square) == seats
        marks = marks + lax.dot_general(
            both.astype(bf16), sits.astype(f32).astype(bf16), nt, preferred_element_type=f32
        )
    lines = (found[0:1] + found[1:2] * 256.0).astype(i32)
    goals = (found[2:3] * float(cap_rows(cap)) + found[3:4] + found[4:5]).astype(i32)
    for n, values in enumerate((lines, goals)):
        for r in range(count // 128):
            at = n * (count // 128) + r
            table[at : at + 1, :] = values[:, 128 * r : 128 * r + 128]
    at = 2 * (count // 128)
    table[at : at + 1, :] = spans[:, :128].astype(i32)
    label = marks[:16] + 256.0 * (1.0 - marks[16:])
    for d in range(16):
        total = jnp.sum(marks[16 + d : 17 + d], axis=1, keepdims=True)
        labels[d] = jnp.where(
            sub == 0,
            jnp.broadcast_to(label[d : d + 1], (8, 128)),
            jnp.broadcast_to(total, (8, 128)),
        )


def cap_rows(cap):
    return cap + 1


GROUP = 16
ENTRIES = 1152


def expand_kernel(chunk, *refs):
    if chunk:
        table, labels, pts, *refs = refs
    else:
        here, plan, leaf, pts, *refs = refs
    outs, refs = refs[:4], refs[4:]
    if not chunk:
        listed, labels, *refs = refs
    held, all_pts, stage, bx, by, bz, sems, load_sems, *refs = refs
    first = sum(len(c) for c in CHUNKS[:chunk])
    wide = len(CHUNKS[chunk])
    rows = outs[0].shape[1]
    cap = rows - 1
    span = all_pts.shape[0] // 5
    loads = [
        pltpu.make_async_copy(
            pts.at[pl.ds(span * axis, span)], all_pts.at[pl.ds(span * axis, span)],
            load_sems.at[axis],
        )
        for axis in range(5)
    ]
    for load in loads:
        load.start()
    if not chunk:
        table, picked, scaled, sem = refs
        route(here, plan, leaf, listed, labels, picked, scaled)
        copy = pltpu.make_async_copy(listed, table, sem)
        copy.start()
        copy.wait()

    def look(n):
        return table[n] if chunk else table[n >> 7, n & 127]

    for k in range(4):
        for n in range(wide):
            held[1 + (k * wide + n) * rows + cap] = labels[4 * (first + n) + k]
    begin = look(i32(2 * ENTRIES + 2 * chunk))
    trips = look(i32(2 * ENTRIES + 2 * chunk + 1))
    for load in loads:
        load.wait()

    def fetch(g, u, bank):
        line = look(begin + g * GROUP + u)
        for axis in range(3):
            for h in range(2):
                stage[bank, axis, h, pl.ds(u, 1), :] = all_pts[
                    pl.ds(line + (span * axis + 8 * h), 1), :
                ]

    def tabulate(piece, bank):
        u, h, axis = 8 * (piece // 6), piece // 3 % 2, piece % 3
        values = basis(stage[bank, axis, h, pl.ds(u, 8), :])
        for a in range(8):
            if axis == 1:
                by[bank, h, pl.ds(GROUP * a + u, 8), :] = values[a]
            else:
                ref = bz if axis else bx
                ref[bank, h, pl.ds(8 * u + a, 8, stride=8), :] = values[a]

    def consume(g, u, bank):
        base = begin + g * GROUP
        line = look(base + u)
        weighted, pair = [], []
        for h in range(2):
            lx = bx[bank, h, pl.ds(8 * u, 8), :]
            lz = bz[bank, h, pl.ds(8 * u, 8), :]
            re, im = (
                jnp.broadcast_to(
                    all_pts[pl.ds(line + (span * (3 + part) + 8 * h), 1), :], lx.shape
                )
                for part in range(2)
            )
            weighted.append(jnp.concatenate([re * lx, im * lx], axis=0).astype(jnp.bfloat16))
            pair.append(
                jnp.concatenate(
                    [
                        jnp.broadcast_to(by[bank, h, pl.ds(GROUP * b + u, 1), :], lz.shape) * lz
                        for b in range(8)
                    ],
                    axis=0,
                ).astype(jnp.bfloat16)
            )
        res = lax.dot_general(
            jnp.concatenate(weighted, axis=1),
            jnp.concatenate(pair, axis=1),
            (((1,), (1,)), ((), ())),
            preferred_element_type=f32,
        )
        held[look(base + (ENTRIES + u))] = jnp.concatenate([res[:8], res[8:]], axis=1)

    pieces = 6 * GROUP // 8
    for u in range(GROUP):
        fetch(0, u, 0)
    for piece in range(pieces):
        tabulate(piece, 0)
    for u in range(GROUP):
        fetch(1, u, 1)

    def step(g, carry):
        bank = g & 1
        for u in range(GROUP):
            consume(g, u, bank)
            if u % 4 == 3:
                for piece in range(3 * (u // 4), 3 * (u // 4) + 3):
                    tabulate(piece, 1 - bank)
                for v in range(u - 3, u + 1):
                    fetch(g + 2, v, bank)
        return carry

    lax.fori_loop(0, trips, step, 0)
    copies = []
    for k in range(4):
        for n in range(wide):
            copies.append(
                pltpu.make_async_copy(
                    held.at[pl.ds(1 + (k * wide + n) * rows, rows)], outs[k].at[n], sems.at[k, n]
                )
            )
    for copy in copies:
        copy.start()
    for copy in copies:
        copy.wait()


def expand(chunk, routing, pts, cap):
    wide = len(CHUNKS[chunk])
    out_shape = [jax.ShapeDtypeStruct((wide, cap + 1, 8, 128), f32)] * 4
    out_specs = [ANY] * 4
    scratch = []
    if chunk:
        in_specs = [SMEM, VMEM, ANY]
    else:
        in_specs = [SMEM, VMEM, VMEM, ANY]
        out_shape += [
            jax.ShapeDtypeStruct((24, 128), i32),
            jax.ShapeDtypeStruct((16, 8, 128), f32),
        ]
        out_specs += [VMEM] * 2
        scratch = [
            pltpu.SMEM((24, 128), i32),
            pltpu.VMEM((128, 128), f32),
            pltpu.VMEM((128, 128), f32),
            pltpu.SemaphoreType.DMA(()),
        ]
    return pl.pallas_call(
        functools.partial(expand_kernel, chunk),
        out_shape=out_shape,
        in_specs=in_specs,
        out_specs=out_specs,
        scratch_shapes=[
            pltpu.VMEM((4 * wide * (cap + 1) + 1, 8, 128), f32),
            pltpu.VMEM(pts.shape, f32),
            pltpu.VMEM((2, 3, 2, GROUP, 128), f32),
            *[pltpu.VMEM((2, 2, 8 * GROUP, 128), f32)] * 3,
            pltpu.SemaphoreType.DMA((4, wide)),
            pltpu.SemaphoreType.DMA((5,)),
            *scratch,
        ],
        cost_estimate=pl.CostEstimate(
            flops=wide * (1 << 28), bytes_accessed=1 << 23, transcendentals=0
        ),
        name="expand",
    )(*routing, pts)


def gather_kernel(wide, *refs):
    arrived, outs = refs[:4], refs[4 : 4 + wide]
    held, labels, names, sem, sems = refs[4 + wide :]
    cap = held.shape[2] - 1
    loads = [pltpu.make_async_copy(arrived[k], held.at[k], sems.at[k]) for k in range(4)]
    for load in loads:
        load.start()
    for out in outs:
        out[...] = jnp.zeros(out.shape, f32)
    for load in loads:
        load.wait()
    for k in range(4):
        for n in range(wide):
            labels[pl.ds(8 * (k * wide + n), 8), :] = held[k, n, cap].astype(i32)
    copy = pltpu.make_async_copy(labels, names, sem)
    copy.start()
    copy.wait()
    for k in range(4):
        most = names[8 * k * wide + 1, 0]
        for n in range(1, wide):
            most = jnp.maximum(most, names[8 * (k * wide + n) + 1, 0])

        def rows4(r, carry):
            for u in range(4):
                for n in range(wide):
                    slot = r * 4 + u
                    where = names[8 * (k * wide + n), slot]
                    outs[n][where] = outs[n][where] + held[k, n, slot]
            return carry

        lax.fori_loop(0, (most + 3) // 4, rows4, 0)


def gather(arrived, leaf_count):
    wide, rows = arrived[0].shape[:2]
    return pl.pallas_call(
        functools.partial(gather_kernel, wide),
        out_shape=[jax.ShapeDtypeStruct((leaf_count + 1, 8, 128), f32)] * wide,
        in_specs=[pl.BlockSpec(memory_space=pl.ANY)] * 4,
        out_specs=[VMEM] * wide,
        scratch_shapes=[
            pltpu.VMEM((4, wide, rows, 8, 128), f32),
            pltpu.VMEM((32 * wide, 128), i32),
            pltpu.SMEM((32 * wide, 128), i32),
            pltpu.SemaphoreType.DMA(()),
            pltpu.SemaphoreType.DMA((4,)),
        ],
        cost_estimate=pl.CostEstimate(
            flops=wide * (1 << 26), bytes_accessed=wide << 22, transcendentals=0
        ),
        name="gather",
    )(*arrived)


def rows_of(shape):
    return lax.broadcasted_iota(i32, shape, len(shape) - 2)


def swap_rows(t):
    even = rows_of(t.shape) % 2 == 0
    axis = len(t.shape) - 2
    return jnp.where(even, pltpu.roll(t, 7, axis), pltpu.roll(t, 1, axis))


def spin(t, cosine, sine):
    return t * cosine + swap_rows(t) * sine


def row_mix(t, maps, bit):
    flipped = pltpu.roll(t, 64, 2)
    total = None
    for step in range(4):
        for flip in range(2):
            part = flipped if flip else t
            if step:
                part = pltpu.roll(part, 8 - 2 * step, 1)
            term = part * maps[bit, 2 * step + flip]
            total = term if total is None else total + term
    return total


SEATS = 36


def turn(ca, sa, cb, sb):
    return ca * cb - sa * sb, sa * cb + ca * sb


def twice(c, s):
    return c * c - s * s, 2.0 * (s * c)


def phases_kernel(
    here, slots, boxes, cones, box_cones, cosine, sine, p0c, p0s, p1c, p1s, ec, es, goal,
    t0c, t0s, t1c, t1s, t2c, t2s,
):
    side = here[2]
    sign = jnp.where(rows_of((8, 128)) % 2 == 0, -1.0, 1.0)

    def cone_tables(n, carry):
        xs = [(cosine[n, v], sine[n, v]) for v in range(3)]
        wide = [
            tuple(jnp.broadcast_to(t[n, 3, pl.ds(v, 1), :], (8, 128)) for t in (cosine, sine))
            for v in range(5)
        ]
        t1c[n], t1s[n] = turn(*xs[2], *wide[4])
        xs2 = [twice(*x) for x in xs[:2]]
        for v in range(4):
            wide2 = twice(*wide[v])
            for bit in range(2):
                at = n * 8 + 4 * bit + v
                t0c[at], t0s[at] = turn(*xs[bit], *wide[v])
                t2c[at], t2s[at] = turn(*xs2[bit], *wide2)
        return carry

    lax.fori_loop(0, cosine.shape[0], cone_tables, 0)

    def child(j, carry):
        for o in range(8):
            p = slots[32 * o + j]
            e = cones[p] * 8 + o
            p0c[o, j] = t0c[e]
            p0s[o, j] = t0s[e] * sign
            owner = p >> 5
            goal[32 * o + j] = ((((owner & 1) ^ side) << 2) + (owner >> 1)) * SEATS + (p & 31)
            a = cones[8 * j + o]
            b = box_cones[boxes[32 * o + j]] * 8 + o
            c, s = turn(t1c[a], t1s[a], t2c[b], t2s[b])
            p1c[o, j] = c
            p1s[o, j] = s * sign
        return carry

    lax.fori_loop(0, 32, child, 0)
    me = 2 * here[3] + side
    for n in range(SEATS):
        if n < 32:
            a = cones[32 * me + n]
            c, s = t1c[a], t1s[a]
        else:
            a = box_cones[4 * me + n - 32]
            c, s = twice(t1c[a], t1s[a])
        ec[n] = c
        es[n] = s * sign


def lane_mix(t, both, octant):
    count = t.shape[0]
    flat = t.reshape(count * 8, 128)
    high = flat.astype(jnp.bfloat16)
    low = (flat - high.astype(f32)).astype(jnp.bfloat16)
    res = jnp.dot(
        jnp.concatenate([high, low], axis=1), both[octant % 4], preferred_element_type=f32
    )
    return (res[:, :128] + res[:, 128:]).reshape(count, 8, 128)


def levels_kernel(
    here, goal, boxes, a0, a1, a2, a3, p0c, p0s, p1c, p1s, both, rows, leaves, mine, other,
    held, turns, lanes_in, rows_in, solved, acc, upper, moved, sems, out_sems,
):
    count = leaves.shape[0]
    sums = [
        pltpu.make_async_copy(ref.at[pl.ds(0, count)], held.at[n], sems.at[n])
        for n, ref in enumerate((a0, a1, a2, a3))
    ]
    maps = [
        pltpu.make_async_copy(both, lanes_in, sems.at[4]),
        pltpu.make_async_copy(rows, rows_in, sems.at[5]),
    ]
    angles = [
        pltpu.make_async_copy(ref, turns.at[n], sems.at[6 + n])
        for n, ref in enumerate((p0c, p0s, p1c, p1s))
    ]
    for copy in sums + maps + angles:
        copy.start()
    acc[...] = jnp.zeros(acc.shape, f32)
    upper[...] = jnp.zeros(upper.shape, f32)
    for copy in sums:
        copy.wait()
    step = 16
    shape = (step, 8, 128)
    own = rows_of(shape) % 2 == lanes_of(shape) // 64

    def settle(n, carry):
        base = pl.multiple_of(n * step, step)
        t = (held[0, pl.ds(base, step)] + held[1, pl.ds(base, step)]) + (
            held[2, pl.ds(base, step)] + held[3, pl.ds(base, step)]
        )
        solved[pl.ds(base, step)] = jnp.where(own, t, swap_rows(pltpu.roll(t, 64, 2)))
        return carry

    lax.fori_loop(0, count // step, settle, 0)
    done = [pltpu.make_async_copy(solved, leaves, out_sems.at[8])]
    done[0].start()
    for copy in maps + angles[:2]:
        copy.wait()

    def spread(o, start, ref, spots):
        sums = [ref[spots[j]] + moved[o % 2, start + j] for j in range(8)]
        for j in range(8):
            ref[spots[j]] = sums[j]

    for o in range(8):
        for part in range(0, 32, 8):
            t = jnp.stack([solved[8 * (part + j) + o] for j in range(8)])
            t = spin(t, turns[0, o, part : part + 8], turns[1, o, part : part + 8])
            moved[o % 2, part : part + 8] = row_mix(lane_mix(t, lanes_in, o), rows_in, o // 4)
        for part in range(0, 32, 8):
            spread(o, part, acc, [goal[32 * o + part + j] for j in range(8)])

    apart = [here[2] * 4 * SEATS, (1 - here[2]) * 4 * SEATS]
    for copy in angles[2:]:
        copy.wait()
    for o in range(8):
        for part in range(0, 32, 8):
            tiles = []
            for j in range(8):
                p = 8 * (part + j) + o
                owner = p // 32
                tiles.append(acc[(owner // 2) * SEATS + p % 32 + apart[owner % 2]])
            t = spin(
                jnp.stack(tiles), turns[2, o, part : part + 8], turns[3, o, part : part + 8]
            )
            moved[o % 2, part : part + 8] = lane_mix(t, lanes_in, o)
        for part in range(0, 32, 8):
            spread(
                o, part, upper,
                [boxes[32 * o + part + j] + 32 * (o // 4) for j in range(8)],
            )
    for part in range(0, 32, 8):
        t = row_mix(upper[part : part + 8], rows_in, 0)
        t = t + row_mix(upper[32 + part : 40 + part], rows_in, 1)
        for j in range(8):
            q = part + j
            owner = q // 4
            acc[(owner // 2) * SEATS + 32 + q % 4 + apart[owner % 2]] = t[j]
    for k in range(4):
        z = (here[3] + k) % 4
        done += [
            pltpu.make_async_copy(
                acc.at[pl.ds((4 + z) * SEATS, SEATS)], other.at[k], out_sems.at[4 + k]
            ),
            pltpu.make_async_copy(acc.at[pl.ds(z * SEATS, SEATS)], mine.at[k], out_sems.at[k]),
        ]
    for copy in done[1:]:
        copy.start()
    for copy in done:
        copy.wait()


def close_kernel(g0, g1, g2, g3, ec, es, out_one, out_two):
    owned = out_one.shape[0]
    for n in range(SEATS):
        t = spin((g0[n] + g1[n]) + (g2[n] + g3[n]), ec[n], es[n])
        if n < owned:
            out_one[n] = t
        else:
            out_two[n - owned] = t


def cone_places():
    nodes = cheb_nodes()
    rows = np.arange(8)[:, None]
    lanes = np.arange(128)[None, :]
    a = 2 * (rows // 2) + lanes // 64
    out = np.zeros((3, 4, 8, 128))
    out[0, 0], out[0, 1], out[0, 2] = child_axis(0)[a], child_axis(1)[a], -nodes[a]
    b, c = np.arange(128) % 64 // 8, np.arange(128) % 8
    for v in range(4):
        out[1, 3, v], out[2, 3, v] = child_axis(v // 2)[b], child_axis(v % 2)[c]
    out[1, 3, 4], out[2, 3, 4] = -nodes[b], -nodes[c]
    return out.astype(np.float32)


def to_nodes(tiles):
    count = tiles.shape[0]
    return tiles.reshape(count, 4, 2, 128).transpose(0, 2, 1, 3).reshape(count, 2, 512)


def cone_vectors(cone_angles):
    azimuth = cone_angles[:, 0]
    polar = cone_angles[:, 1]
    return jnp.stack(
        [jnp.cos(azimuth) * jnp.sin(polar), jnp.sin(azimuth) * jnp.sin(polar), jnp.cos(polar)],
        axis=1,
    )


def hop(x, shift, leg, groups):
    pairs = []
    for s in range(16):
        for g in range(groups):
            y, x0 = s // 4, s % 4
            if g % 2 == leg:
                x0 = (x0 + shift) % 4
            else:
                y = (y + shift) % 4
            pairs.append((s * groups + g, (4 * y + x0) * groups + g))
    return lax.ppermute(x, ("sfc", "grp"), pairs)


def around(x, shift, groups):
    pairs = [(g, (g + 2 * shift) % groups) for g in range(groups)]
    return lax.ppermute(x, "grp", pairs)


def after(value, *others):
    return lax.optimization_barrier((value, *others))[0]


def per_device(
    bin_points, bin_plan, bin_leaf, leaf_slots, box_slots, parent_cone, box_cone, cone_angles
):
    groups = lax.axis_size("grp")
    rank = lax.axis_index("grp")
    cap = bin_points.shape[0] // 8
    leaf_count = leaf_slots.shape[2] * 8
    first_owned = parent_cone.shape[1] // groups
    second_owned = box_cone.shape[1] // groups
    tile = jax.ShapeDtypeStruct((8, 128), f32)

    def tiles(*lead):
        return jax.ShapeDtypeStruct((*lead, *tile.shape), f32)

    me = lax.axis_index("sfc")
    here = jnp.stack([me % 4, me // 4, rank % 2, rank // 2]).astype(i32)
    bins, _, width = bin_points.shape
    pts = jnp.transpose(bin_points.reshape(bins // 8, 8, 5, width // 128, 128), (2, 0, 3, 1, 4))
    pts = pts.reshape(-1, 128)
    arrived = []
    routing = (here, bin_plan.reshape(bins // 128, 128), bin_leaf.reshape(bins // 128, 128))
    for c in range(len(CHUNKS)):
        sent = expand(c, routing, pts, cap)
        if not c:
            *sent, table, labels = sent
            table = table.reshape(-1)
        table = after(table, sent[0])
        routing = (table, labels)
        moved = [sent[0]]
        for k in (2, 1, 3):
            moved.append(hop(sent[k], k, 0, groups))
        arrived.append(moved)

    cone_angles = after(cone_angles, sent[0])
    directions = cone_vectors(cone_angles)
    places = jnp.asarray(cone_places())
    angle = (
        directions[:, 0, None, None, None] * places[None, 0]
        + directions[:, 1, None, None, None] * places[None, 1]
        + directions[:, 2, None, None, None] * places[None, 2]
    ) * kappa_leaf
    make_phases = pl.pallas_call(
        phases_kernel,
        out_shape=(tiles(8, 32),) * 4 + (tiles(SEATS),) * 2 + (jax.ShapeDtypeStruct((256,), i32),),
        in_specs=[SMEM] * 5 + [VMEM] * 2,
        out_specs=(VMEM,) * 6 + (SMEM,),
        scratch_shapes=[pltpu.VMEM((n, 8, 128), f32) for n in (128, 128, 16, 16, 128, 128)],
        name="phases",
    )
    slots, boxes = leaf_slots.reshape(-1), box_slots.reshape(-1)
    p0c, p0s, p1c, p1s, ec, es, goal = make_phases(
        here, slots, boxes, parent_cone[0], box_cone[0], jnp.cos(angle), jnp.sin(angle)
    )

    held = [None] * 4
    last = sent[0]
    for c, chunk in enumerate(CHUNKS):
        got = [after(arrived[c][0], last)] + arrived[c][1:]
        sums = gather(got, leaf_count)
        last = sums[0]
        for m, part in zip(chunk, sums):
            held[m] = hop(part, m, 1, groups) if m else part

    leaves, mine, other = pl.pallas_call(
        levels_kernel,
        out_shape=(tiles(leaf_count), tiles(4, SEATS), tiles(4, SEATS)),
        in_specs=[SMEM] * 3 + [ANY] * 10,
        out_specs=(ANY,) * 3,
        scratch_shapes=[
            pltpu.VMEM((4, leaf_count, 8, 128), f32),
            pltpu.VMEM((4, 8, 32, 8, 128), f32),
            pltpu.VMEM((4, 256, 256), jnp.bfloat16),
            pltpu.VMEM((2, 8, 8, 128), f32),
            pltpu.VMEM((leaf_count, 8, 128), f32),
            pltpu.VMEM((8 * SEATS, 8, 128), f32),
            pltpu.VMEM((64, 8, 128), f32),
            pltpu.VMEM((2, 32, 8, 128), f32),
            pltpu.SemaphoreType.DMA((10,)),
            pltpu.SemaphoreType.DMA((9,)),
        ],
        name="levels",
    )(
        here, goal, boxes, *held, p0c, p0s, p1c, p1s,
        jnp.asarray(lane_maps()), jnp.asarray(row_maps()),
    )
    swapped = lax.ppermute(other, "grp", [(g, g ^ 1) for g in range(groups)])
    blocks = [mine[k] + swapped[k] for k in range(4)]
    got = [blocks[0]] + [around(blocks[k], k, groups) for k in (1, 2, 3)]
    one, two = pl.pallas_call(
        close_kernel,
        out_shape=(tiles(first_owned), tiles(second_owned)),
        in_specs=[VMEM] * 6,
        out_specs=(VMEM, VMEM),
        name="close",
    )(*got, ec, es)
    return (to_nodes(leaves), to_nodes(one), to_nodes(two))


def solution(mesh):
    placed = (
        P(("sfc", "grp"), None, None),
        P(("sfc", "grp"), None),
        P(("sfc", "grp")),
        P("sfc", None, "grp"),
        P("sfc", None, None),
        P("sfc", None),
        P("sfc", None),
        P(),
    )

    return jax.shard_map(
        per_device,
        mesh=mesh,
        in_specs=placed,
        out_specs=(
            P(("sfc", "grp"), None, None),
            P(("sfc", "grp"), None, None),
            P(("sfc", "grp"), None, None),
        ),
        check_vma=False,
    )
```

```python
import functools

import jax
import jax.numpy as jnp
import numpy as np
from jax import lax
from jax.experimental import pallas as pl
from jax.experimental.pallas import tpu as pltpu
from jax.sharding import PartitionSpec as P

kappa_leaf = 2.0
f32 = jnp.float32
i32 = jnp.int32
VMEM = pl.BlockSpec(memory_space=pltpu.VMEM)
SMEM = pl.BlockSpec(memory_space=pltpu.SMEM)
ANY = pl.BlockSpec(memory_space=pl.ANY)


def cheb_nodes():
    return np.cos((2.0 * np.arange(8) + 1.0) * np.pi / 16.0)


def lagrange_np(values):
    nodes = cheb_nodes()
    rows = []
    for center in range(8):
        weight = np.ones_like(values)
        for other in range(8):
            if other != center:
                weight = weight * (values - nodes[other]) / (nodes[center] - nodes[other])
        rows.append(weight)
    return np.stack(rows, axis=0)


def child_axis(bit):
    return 0.5 * (2 * bit - 1) + 0.5 * cheb_nodes()


def axis_maps():
    return np.stack([lagrange_np(child_axis(bit)) for bit in range(2)])


def lane_maps():
    maps = axis_maps()
    out = []
    for pick in range(4):
        both = np.kron(maps[pick // 2], maps[pick % 2])
        full = np.kron(np.eye(2), both).T
        high = full.astype(jnp.bfloat16)
        low = (full - high.astype(np.float64)).astype(jnp.bfloat16)
        out.append(np.block([[high, low], [high, np.zeros_like(low)]]))
    return np.stack(out).astype(jnp.bfloat16)


def row_maps():
    maps = axis_maps()
    rows = np.arange(8)[:, None]
    half = np.arange(128)[None, :] // 64
    k = rows // 2
    out = np.zeros((2, 8, 8, 128), np.float32)
    for bit in range(2):
        for step in range(4):
            for flip in range(2):
                to = 2 * k + half
                frm = 2 * ((k + step) % 4) + (half ^ flip)
                out[bit, 2 * step + flip] = maps[bit][to, frm]
    return out


def basis(x):
    t = cheb_nodes()[:4]
    sq = t * t
    x2 = x * x
    s = [x2 - float(v) for v in sq]
    p01 = s[0] * s[1]
    p23 = s[2] * s[3]
    rest = [s[1] * p23, s[0] * p23, p01 * s[3], p01 * s[2]]
    out = [None] * 8
    for j in range(4):
        scale = 1.0 / (np.prod([sq[j] - sq[i] for i in range(4) if i != j]) * 2.0 * t[j])
        q = rest[j] * float(scale)
        out[j] = q * (x + float(t[j]))
        out[7 - j] = q * (float(t[j]) - x)
    return out


def lanes_of(shape):
    return lax.broadcasted_iota(i32, shape, len(shape) - 1)


def lanes_of(shape):
    return lax.broadcasted_iota(i32, shape, len(shape) - 1)


CHUNKS = ((1, 3), (2, 0))
ORDER = tuple(m for chunk in CHUNKS for m in chunk)


def route(here, plan, leaf, table, labels, picked, scaled):
    bf16 = jnp.bfloat16
    cap = labels.shape[2]
    target = plan[...]
    names = leaf[...].astype(f32)
    along_x = (target - here[0]) % 4
    along_y = (target // 4 - here[1]) % 4
    first = jnp.where(here[2] == 0, along_x, along_y)
    second = jnp.where(here[2] == 0, along_y, along_x)
    place, lead, width, part_of = target * 0, target * 0, target * 0, target * 0
    for c, chunk in enumerate(CHUNKS):
        for n, m in enumerate(chunk):
            hit = second == m
            place = jnp.where(hit, ORDER.index(m), place)
            part_of = jnp.where(hit, c, part_of)
            lead = jnp.where(hit, n, lead)
            width = jnp.where(hit, len(chunk), width)
    code = place * 4 + first
    for d in range(16):
        hit = (code == d).astype(f32)
        picked[pl.ds(8 * d, 8), :] = hit
        scaled[pl.ds(8 * d, 8), :] = hit * names
    square = (128, 128)
    row, lane = rows_of(square), lanes_of(square)
    hits = picked[...].astype(bf16)
    ones = jnp.ones(square, bf16)

    def mul(a, b):
        return jnp.dot(a.astype(bf16), b.astype(bf16), preferred_element_type=f32)

    inside = mul(hits, (row < lane).astype(f32))
    ahead = mul(mul((lane < row).astype(f32), hits), ones)
    same = mul(mul(((lane < row) & (lane // 8 == row // 8)).astype(f32), hits), ones)
    order = jnp.zeros((8, 128), f32)
    slot = jnp.zeros((8, 128), f32)
    for d in range(16):
        part = slice(8 * d, 8 * d + 8)
        hit = picked[pl.ds(8 * d, 8), :]
        order = order + hit * (inside[part] + ahead[part])
        slot = slot + hit * (inside[part] + same[part])
    count = ENTRIES
    lane_w = lanes_of((1, count))
    spans = jnp.zeros((1, count), f32)
    start = jnp.zeros((1, 1), f32)
    before = jnp.zeros((1, 1), f32)
    for c in range(len(CHUNKS)):
        size = jnp.sum((part_of == c).astype(f32), keepdims=True)
        groups = jnp.floor((size + float(GROUP - 1)) * (1.0 / GROUP))
        spans = jnp.where(lane_w == 2 * c, jnp.broadcast_to(start, (1, count)), spans)
        spans = jnp.where(lane_w == 2 * c + 1, jnp.broadcast_to(groups, (1, count)), spans)
        order = order + jnp.where(
            part_of == c, jnp.broadcast_to(start - before, order.shape), 0.0
        )
        start = start + groups * float(GROUP)
        before = before + size
    goal_hi = (first * width + lead).astype(f32)
    ranks = lax.broadcasted_iota(i32, (count, 128), 0).astype(f32)
    seats = row.astype(f32)
    sub = lax.broadcasted_iota(i32, (8, 128), 0)
    lane_f = lanes_of((8, 128)).astype(f32)
    found = jnp.zeros((8, count), f32)
    marks = jnp.zeros((32, 128), f32)
    nt = (((1,), (1,)), ((), ()))
    for r in range(8):
        at = jnp.broadcast_to(order[r : r + 1, :], (count, 128)) == ranks
        goal = jnp.broadcast_to(goal_hi[r : r + 1, :], (8, 128))
        seat = jnp.broadcast_to(slot[r : r + 1, :], (8, 128))
        values = jnp.where(
            sub == 0, 2.0 * lane_f - (lanes_of((8, 128)) % 8).astype(f32),
            jnp.where(sub == 1, float(r), jnp.where(sub == 2, goal, jnp.where(sub == 3, seat, 1.0))),
        )
        found = found + lax.dot_general(
            values.astype(bf16), at.astype(f32).astype(bf16), nt, preferred_element_type=f32
        )
        both = jnp.concatenate(
            [scaled[pl.ds(r, 16, stride=8), :], picked[pl.ds(r, 16, stride=8), :]], axis=0
        )
        sits = jnp.broadcast_to(slot[r : r + 1, :], square) == seats
        marks = marks + lax.dot_general(
            both.astype(bf16), sits.astype(f32).astype(bf16), nt, preferred_element_type=f32
        )
    lines = (found[0:1] + found[1:2] * 256.0).astype(i32)
    goals = (found[2:3] * float(cap_rows(cap)) + found[3:4] + found[4:5]).astype(i32)
    for n, values in enumerate((lines, goals)):
        for r in range(count // 128):
            at = n * (count // 128) + r
            table[at : at + 1, :] = values[:, 128 * r : 128 * r + 128]
    at = 2 * (count // 128)
    table[at : at + 1, :] = spans[:, :128].astype(i32)
    label = marks[:16] + 256.0 * (1.0 - marks[16:])
    for d in range(16):
        total = jnp.sum(marks[16 + d : 17 + d], axis=1, keepdims=True)
        labels[d] = jnp.where(
            sub == 0,
            jnp.broadcast_to(label[d : d + 1], (8, 128)),
            jnp.broadcast_to(total, (8, 128)),
        )


def cap_rows(cap):
    return cap + 1


GROUP = 16
ENTRIES = 1152


def expand_kernel(chunk, *refs):
    if chunk:
        table, labels, pts, *refs = refs
    else:
        here, plan, leaf, pts, *refs = refs
    outs, refs = refs[:4], refs[4:]
    if not chunk:
        listed, labels, *refs = refs
    held, all_pts, stage, bx, by, bz, sems, load_sems, *refs = refs
    first = sum(len(c) for c in CHUNKS[:chunk])
    wide = len(CHUNKS[chunk])
    rows = outs[0].shape[1]
    cap = rows - 1
    span = all_pts.shape[0] // 5
    loads = [
        pltpu.make_async_copy(
            pts.at[pl.ds(span * axis, span)], all_pts.at[pl.ds(span * axis, span)],
            load_sems.at[axis],
        )
        for axis in range(5)
    ]
    for load in loads:
        load.start()
    if not chunk:
        table, picked, scaled, sem = refs
        route(here, plan, leaf, listed, labels, picked, scaled)
        copy = pltpu.make_async_copy(listed, table, sem)
        copy.start()
        copy.wait()

    def look(base, which, u=0):
        if chunk:
            return table[base + (which * ENTRIES + u)]
        return table[(base >> 7) + which * (ENTRIES // 128), (base & 127) + u]

    for k in range(4):
        for n in range(wide):
            held[1 + (k * wide + n) * rows + cap] = labels[4 * (first + n) + k]
    begin = look(i32(0), 2, 2 * chunk)
    trips = look(i32(0), 2, 2 * chunk + 1)
    for load in loads:
        load.wait()

    def fetch(g, u, bank):
        line = look(begin + g * GROUP, 0, u)
        for axis in range(3):
            for h in range(2):
                stage[bank, axis, h, pl.ds(u, 1), :] = all_pts[
                    pl.ds(line + (span * axis + 8 * h), 1), :
                ]

    def tabulate(piece, bank):
        u, h, axis = 8 * (piece // 6), piece // 3 % 2, piece % 3
        values = basis(stage[bank, axis, h, pl.ds(u, 8), :])
        for a in range(8):
            if axis == 1:
                by[bank, h, pl.ds(GROUP * a + u, 8), :] = values[a]
            else:
                ref = bz if axis else bx
                ref[bank, h, pl.ds(8 * u + a, 8, stride=8), :] = values[a]

    def consume(g, u, bank):
        base = begin + g * GROUP
        line = look(base, 0, u)
        weighted, pair = [], []
        for h in range(2):
            lx = bx[bank, h, pl.ds(8 * u, 8), :]
            lz = bz[bank, h, pl.ds(8 * u, 8), :]
            re, im = (
                jnp.broadcast_to(
                    all_pts[pl.ds(line + (span * (3 + part) + 8 * h), 1), :], lx.shape
                )
                for part in range(2)
            )
            weighted.append(jnp.concatenate([re * lx, im * lx], axis=0).astype(jnp.bfloat16))
            pair.append(
                jnp.concatenate(
                    [
                        jnp.broadcast_to(by[bank, h, pl.ds(GROUP * b + u, 1), :], lz.shape) * lz
                        for b in range(8)
                    ],
                    axis=0,
                ).astype(jnp.bfloat16)
            )
        res = lax.dot_general(
            jnp.concatenate(weighted, axis=1),
            jnp.concatenate(pair, axis=1),
            (((1,), (1,)), ((), ())),
            preferred_element_type=f32,
        )
        held[look(base, 1, u)] = jnp.concatenate([res[:8], res[8:]], axis=1)

    pieces = 6 * GROUP // 8
    for u in range(GROUP):
        fetch(0, u, 0)
    for piece in range(pieces):
        tabulate(piece, 0)
    for u in range(GROUP):
        fetch(1, u, 1)

    def step(g, carry):
        bank = g & 1
        for u in range(GROUP):
            consume(g, u, bank)
            if u % 4 == 3:
                for piece in range(3 * (u // 4), 3 * (u // 4) + 3):
                    tabulate(piece, 1 - bank)
                for v in range(u - 3, u + 1):
                    fetch(g + 2, v, bank)
        return carry

    lax.fori_loop(0, trips, step, 0)
    copies = []
    for k in range(4):
        for n in range(wide):
            copies.append(
                pltpu.make_async_copy(
                    held.at[pl.ds(1 + (k * wide + n) * rows, rows)], outs[k].at[n], sems.at[k, n]
                )
            )
    for copy in copies:
        copy.start()
    for copy in copies:
        copy.wait()


def expand(chunk, routing, pts, cap):
    wide = len(CHUNKS[chunk])
    out_shape = [jax.ShapeDtypeStruct((wide, cap + 1, 8, 128), f32)] * 4
    out_specs = [ANY] * 4
    scratch = []
    if chunk:
        in_specs = [SMEM, VMEM, ANY]
    else:
        in_specs = [SMEM, VMEM, VMEM, ANY]
        out_shape += [
            jax.ShapeDtypeStruct((24, 128), i32),
            jax.ShapeDtypeStruct((16, 8, 128), f32),
        ]
        out_specs += [VMEM] * 2
        scratch = [
            pltpu.SMEM((24, 128), i32),
            pltpu.VMEM((128, 128), f32),
            pltpu.VMEM((128, 128), f32),
            pltpu.SemaphoreType.DMA(()),
        ]
    return pl.pallas_call(
        functools.partial(expand_kernel, chunk),
        out_shape=out_shape,
        in_specs=in_specs,
        out_specs=out_specs,
        scratch_shapes=[
            pltpu.VMEM((4 * wide * (cap + 1) + 1, 8, 128), f32),
            pltpu.VMEM(pts.shape, f32),
            pltpu.VMEM((2, 3, 2, GROUP, 128), f32),
            *[pltpu.VMEM((2, 2, 8 * GROUP, 128), f32)] * 3,
            pltpu.SemaphoreType.DMA((4, wide)),
            pltpu.SemaphoreType.DMA((5,)),
            *scratch,
        ],
        cost_estimate=pl.CostEstimate(
            flops=wide * (1 << 28), bytes_accessed=1 << 23, transcendentals=0
        ),
        name="expand",
    )(*routing, pts)


def gather_kernel(wide, *refs):
    arrived, outs = refs[:4], refs[4 : 4 + wide]
    held, banks, labels, names, sem, sems = refs[4 + wide :]
    cap = held.shape[2] - 1
    loads = [pltpu.make_async_copy(arrived[k], held.at[k], sems.at[k]) for k in range(4)]
    for load in loads:
        load.start()
    for n in range(wide):
        outs[n][...] = jnp.zeros(outs[n].shape, f32)
        for bank in range(3):
            banks[bank, n] = jnp.zeros(outs[n].shape, f32)
    for load in loads:
        load.wait()
    for k in range(4):
        for n in range(wide):
            labels[pl.ds(8 * (k * wide + n), 8), :] = held[k, n, cap].astype(i32)
    copy = pltpu.make_async_copy(labels, names, sem)
    copy.start()
    copy.wait()
    for k in range(4):
        most = names[8 * k * wide + 1, 0]
        for n in range(1, wide):
            most = jnp.maximum(most, names[8 * (k * wide + n) + 1, 0])

        def rows4(r, carry):
            for u in range(4):
                for n in range(wide):
                    slot = r * 4 + u
                    where = names[8 * (k * wide + n), slot]
                    if u:
                        banks[u - 1, n, where] = banks[u - 1, n, where] + held[k, n, slot]
                    else:
                        outs[n][where] = outs[n][where] + held[k, n, slot]
            return carry

        lax.fori_loop(0, (most + 3) // 4, rows4, 0)

    def join(i, carry):
        part = pl.ds(pl.multiple_of(i * 16, 16), 16)
        for n in range(wide):
            outs[n][part] = (outs[n][part] + banks[0, n, part]) + (
                banks[1, n, part] + banks[2, n, part]
            )
        return carry

    lax.fori_loop(0, (outs[0].shape[0] - 1) // 16, join, 0)


def gather(arrived, leaf_count):
    wide, rows = arrived[0].shape[:2]
    return pl.pallas_call(
        functools.partial(gather_kernel, wide),
        out_shape=[jax.ShapeDtypeStruct((leaf_count + 1, 8, 128), f32)] * wide,
        in_specs=[pl.BlockSpec(memory_space=pl.ANY)] * 4,
        out_specs=[VMEM] * wide,
        scratch_shapes=[
            pltpu.VMEM((4, wide, rows, 8, 128), f32),
            pltpu.VMEM((3, wide, leaf_count + 1, 8, 128), f32),
            pltpu.VMEM((32 * wide, 128), i32),
            pltpu.SMEM((32 * wide, 128), i32),
            pltpu.SemaphoreType.DMA(()),
            pltpu.SemaphoreType.DMA((4,)),
        ],
        cost_estimate=pl.CostEstimate(
            flops=wide * (1 << 26), bytes_accessed=wide << 22, transcendentals=0
        ),
        compiler_params=pltpu.CompilerParams(vmem_limit_bytes=(8 + 10 * wide) << 20),
        name="gather",
    )(*arrived)


def rows_of(shape):
    return lax.broadcasted_iota(i32, shape, len(shape) - 2)


def swap_rows(t):
    even = rows_of(t.shape) % 2 == 0
    axis = len(t.shape) - 2
    return jnp.where(even, pltpu.roll(t, 7, axis), pltpu.roll(t, 1, axis))


def spin(t, cosine, sine):
    return t * cosine + swap_rows(t) * sine


def row_mix(t, maps, bit):
    flipped = pltpu.roll(t, 64, 2)
    total = None
    for step in range(4):
        for flip in range(2):
            part = flipped if flip else t
            if step:
                part = pltpu.roll(part, 8 - 2 * step, 1)
            term = part * maps[bit, 2 * step + flip]
            total = term if total is None else total + term
    return total


SEATS = 36


def turn(ca, sa, cb, sb):
    return ca * cb - sa * sb, sa * cb + ca * sb


def twice(c, s):
    return c * c - s * s, 2.0 * (s * c)


def phases_kernel(
    here, slots, boxes, cones, box_cones, cosine, sine, p0c, p0s, p1c, p1s, ec, es, goal,
    t0c, t0s, t1c, t1s, t2c, t2s,
):
    side = here[2]
    sign = jnp.where(rows_of((8, 128)) % 2 == 0, -1.0, 1.0)

    def cone_tables(n, carry):
        xs = [(cosine[n, v], sine[n, v]) for v in range(3)]
        wide = [
            tuple(jnp.broadcast_to(t[n, 3, pl.ds(v, 1), :], (8, 128)) for t in (cosine, sine))
            for v in range(5)
        ]
        t1c[n], t1s[n] = turn(*xs[2], *wide[4])
        xs2 = [twice(*x) for x in xs[:2]]
        for v in range(4):
            wide2 = twice(*wide[v])
            for bit in range(2):
                at = n * 8 + 4 * bit + v
                t0c[at], t0s[at] = turn(*xs[bit], *wide[v])
                t2c[at], t2s[at] = turn(*xs2[bit], *wide2)
        return carry

    lax.fori_loop(0, cosine.shape[0], cone_tables, 0)

    def child(j, carry):
        for o in range(8):
            p = slots[32 * o + j]
            e = cones[p] * 8 + o
            p0c[o, j] = t0c[e]
            p0s[o, j] = t0s[e] * sign
            owner = p >> 5
            goal[32 * o + j] = ((((owner & 1) ^ side) << 2) + (owner >> 1)) * SEATS + (p & 31)
            a = cones[8 * j + o]
            b = box_cones[boxes[32 * o + j]] * 8 + o
            c, s = turn(t1c[a], t1s[a], t2c[b], t2s[b])
            p1c[o, j] = c
            p1s[o, j] = s * sign
        return carry

    lax.fori_loop(0, 32, child, 0)
    me = 2 * here[3] + side
    for n in range(SEATS):
        if n < 32:
            a = cones[32 * me + n]
            c, s = t1c[a], t1s[a]
        else:
            a = box_cones[4 * me + n - 32]
            c, s = twice(t1c[a], t1s[a])
        ec[n] = c
        es[n] = s * sign


def lane_mix(t, both, octant):
    count = t.shape[0]
    flat = t.reshape(count * 8, 128)
    high = flat.astype(jnp.bfloat16)
    low = (flat - high.astype(f32)).astype(jnp.bfloat16)
    res = jnp.dot(
        jnp.concatenate([high, low], axis=1), both[octant % 4], preferred_element_type=f32
    )
    return (res[:, :128] + res[:, 128:]).reshape(count, 8, 128)


def levels_kernel(
    here, goal, boxes, a0, a1, a2, a3, p0c, p0s, p1c, p1s, both, rows, leaves, mine, other,
    held, turns, lanes_in, rows_in, solved, acc, upper, moved, sems, out_sems,
):
    count = leaves.shape[0]
    sums = [
        pltpu.make_async_copy(ref.at[pl.ds(0, count)], held.at[n], sems.at[n])
        for n, ref in enumerate((a0, a1, a2, a3))
    ]
    maps = [
        pltpu.make_async_copy(both, lanes_in, sems.at[4]),
        pltpu.make_async_copy(rows, rows_in, sems.at[5]),
    ]
    angles = [
        pltpu.make_async_copy(ref, turns.at[n], sems.at[6 + n])
        for n, ref in enumerate((p0c, p0s, p1c, p1s))
    ]
    for copy in sums + maps + angles:
        copy.start()
    acc[...] = jnp.zeros(acc.shape, f32)
    upper[...] = jnp.zeros(upper.shape, f32)
    for copy in sums:
        copy.wait()
    step = 16
    shape = (step, 8, 128)
    own = rows_of(shape) % 2 == lanes_of(shape) // 64

    def settle(n, carry):
        base = pl.multiple_of(n * step, step)
        t = (held[0, pl.ds(base, step)] + held[1, pl.ds(base, step)]) + (
            held[2, pl.ds(base, step)] + held[3, pl.ds(base, step)]
        )
        solved[pl.ds(base, step)] = jnp.where(own, t, swap_rows(pltpu.roll(t, 64, 2)))
        return carry

    lax.fori_loop(0, count // step, settle, 0)
    done = [pltpu.make_async_copy(solved, leaves, out_sems.at[8])]
    done[0].start()
    for copy in maps + angles[:2]:
        copy.wait()

    def spread(o, start, ref, spots):
        sums = [ref[spots[j]] + moved[o % 2, start + j] for j in range(8)]
        for j in range(8):
            ref[spots[j]] = sums[j]

    for o in range(8):
        for part in range(0, 32, 8):
            t = jnp.stack([solved[8 * (part + j) + o] for j in range(8)])
            t = spin(t, turns[0, o, part : part + 8], turns[1, o, part : part + 8])
            moved[o % 2, part : part + 8] = row_mix(lane_mix(t, lanes_in, o), rows_in, o // 4)
        for part in range(0, 32, 8):
            spread(o, part, acc, [goal[32 * o + part + j] for j in range(8)])

    apart = [here[2] * 4 * SEATS, (1 - here[2]) * 4 * SEATS]
    for copy in angles[2:]:
        copy.wait()
    for o in range(8):
        for part in range(0, 32, 8):
            tiles = []
            for j in range(8):
                p = 8 * (part + j) + o
                owner = p // 32
                tiles.append(acc[(owner // 2) * SEATS + p % 32 + apart[owner % 2]])
            t = spin(
                jnp.stack(tiles), turns[2, o, part : part + 8], turns[3, o, part : part + 8]
            )
            moved[o % 2, part : part + 8] = lane_mix(t, lanes_in, o)
        for part in range(0, 32, 8):
            spread(
                o, part, upper,
                [boxes[32 * o + part + j] + 32 * (o // 4) for j in range(8)],
            )
    for part in range(0, 32, 8):
        t = row_mix(upper[part : part + 8], rows_in, 0)
        t = t + row_mix(upper[32 + part : 40 + part], rows_in, 1)
        for j in range(8):
            q = part + j
            owner = q // 4
            acc[(owner // 2) * SEATS + 32 + q % 4 + apart[owner % 2]] = t[j]
    for k in range(4):
        z = (here[3] + k) % 4
        done += [
            pltpu.make_async_copy(
                acc.at[pl.ds((4 + z) * SEATS, SEATS)], other.at[k], out_sems.at[4 + k]
            ),
            pltpu.make_async_copy(acc.at[pl.ds(z * SEATS, SEATS)], mine.at[k], out_sems.at[k]),
        ]
    for copy in done[1:]:
        copy.start()
    for copy in done:
        copy.wait()


def close_kernel(g0, g1, g2, g3, ec, es, out_one, out_two):
    owned = out_one.shape[0]
    for n in range(SEATS):
        t = spin((g0[n] + g1[n]) + (g2[n] + g3[n]), ec[n], es[n])
        if n < owned:
            out_one[n] = t
        else:
            out_two[n - owned] = t


def cone_places():
    nodes = cheb_nodes()
    rows = np.arange(8)[:, None]
    lanes = np.arange(128)[None, :]
    a = 2 * (rows // 2) + lanes // 64
    out = np.zeros((3, 4, 8, 128))
    out[0, 0], out[0, 1], out[0, 2] = child_axis(0)[a], child_axis(1)[a], -nodes[a]
    b, c = np.arange(128) % 64 // 8, np.arange(128) % 8
    for v in range(4):
        out[1, 3, v], out[2, 3, v] = child_axis(v // 2)[b], child_axis(v % 2)[c]
    out[1, 3, 4], out[2, 3, 4] = -nodes[b], -nodes[c]
    return out.astype(np.float32)


def to_nodes(tiles):
    count = tiles.shape[0]
    return tiles.reshape(count, 4, 2, 128).transpose(0, 2, 1, 3).reshape(count, 2, 512)


def cone_vectors(cone_angles):
    azimuth = cone_angles[:, 0]
    polar = cone_angles[:, 1]
    return jnp.stack(
        [jnp.cos(azimuth) * jnp.sin(polar), jnp.sin(azimuth) * jnp.sin(polar), jnp.cos(polar)],
        axis=1,
    )


def hop(x, shift, leg, groups):
    pairs = []
    for s in range(16):
        for g in range(groups):
            y, x0 = s // 4, s % 4
            if g % 2 == leg:
                x0 = (x0 + shift) % 4
            else:
                y = (y + shift) % 4
            pairs.append((s * groups + g, (4 * y + x0) * groups + g))
    return lax.ppermute(x, ("sfc", "grp"), pairs)


def around(x, shift, groups):
    pairs = [(g, (g + 2 * shift) % groups) for g in range(groups)]
    return lax.ppermute(x, "grp", pairs)


def after(value, *others):
    return lax.optimization_barrier((value, *others))[0]


def per_device(
    bin_points, bin_plan, bin_leaf, leaf_slots, box_slots, parent_cone, box_cone, cone_angles
):
    groups = lax.axis_size("grp")
    rank = lax.axis_index("grp")
    cap = bin_points.shape[0] // 8
    leaf_count = leaf_slots.shape[2] * 8
    first_owned = parent_cone.shape[1] // groups
    second_owned = box_cone.shape[1] // groups
    tile = jax.ShapeDtypeStruct((8, 128), f32)

    def tiles(*lead):
        return jax.ShapeDtypeStruct((*lead, *tile.shape), f32)

    me = lax.axis_index("sfc")
    here = jnp.stack([me % 4, me // 4, rank % 2, rank // 2]).astype(i32)
    bins, _, width = bin_points.shape
    pts = jnp.transpose(bin_points.reshape(bins // 8, 8, 5, width // 128, 128), (2, 0, 3, 1, 4))
    pts = pts.reshape(-1, 128)
    arrived = []
    routing = (here, bin_plan.reshape(bins // 128, 128), bin_leaf.reshape(bins // 128, 128))
    for c in range(len(CHUNKS)):
        sent = expand(c, routing, pts, cap)
        if not c:
            *sent, table, labels = sent
            table = table.reshape(-1)
        table = after(table, sent[0])
        routing = (table, labels)
        moved = [sent[0]]
        for k in (2, 1, 3):
            moved.append(hop(sent[k], k, 0, groups))
        arrived.append(moved)

    cone_angles = after(cone_angles, sent[0])
    directions = cone_vectors(cone_angles)
    places = jnp.asarray(cone_places())
    angle = (
        directions[:, 0, None, None, None] * places[None, 0]
        + directions[:, 1, None, None, None] * places[None, 1]
        + directions[:, 2, None, None, None] * places[None, 2]
    ) * kappa_leaf
    make_phases = pl.pallas_call(
        phases_kernel,
        out_shape=(tiles(8, 32),) * 4 + (tiles(SEATS),) * 2 + (jax.ShapeDtypeStruct((256,), i32),),
        in_specs=[SMEM] * 5 + [VMEM] * 2,
        out_specs=(VMEM,) * 6 + (SMEM,),
        scratch_shapes=[pltpu.VMEM((n, 8, 128), f32) for n in (128, 128, 16, 16, 128, 128)],
        compiler_params=pltpu.CompilerParams(vmem_limit_bytes=16 << 20),
        name="phases",
    )
    slots, boxes = leaf_slots.reshape(-1), box_slots.reshape(-1)
    p0c, p0s, p1c, p1s, ec, es, goal = make_phases(
        here, slots, boxes, parent_cone[0], box_cone[0], jnp.cos(angle), jnp.sin(angle)
    )

    held = [None] * 4
    last = sent[0]
    for c, chunk in enumerate(CHUNKS):
        got = [after(arrived[c][0], last)] + arrived[c][1:]
        sums = gather(got, leaf_count)
        last = sums[0]
        for m, part in zip(chunk, sums):
            held[m] = hop(part, m, 1, groups) if m else part

    leaves, mine, other = pl.pallas_call(
        levels_kernel,
        out_shape=(tiles(leaf_count), tiles(4, SEATS), tiles(4, SEATS)),
        in_specs=[SMEM] * 3 + [ANY] * 10,
        out_specs=(ANY,) * 3,
        scratch_shapes=[
            pltpu.VMEM((4, leaf_count, 8, 128), f32),
            pltpu.VMEM((4, 8, 32, 8, 128), f32),
            pltpu.VMEM((4, 256, 256), jnp.bfloat16),
            pltpu.VMEM((2, 8, 8, 128), f32),
            pltpu.VMEM((leaf_count, 8, 128), f32),
            pltpu.VMEM((8 * SEATS, 8, 128), f32),
            pltpu.VMEM((64, 8, 128), f32),
            pltpu.VMEM((2, 32, 8, 128), f32),
            pltpu.SemaphoreType.DMA((10,)),
            pltpu.SemaphoreType.DMA((9,)),
        ],
        compiler_params=pltpu.CompilerParams(vmem_limit_bytes=20 << 20),
        name="levels",
    )(
        here, goal, boxes, *held, p0c, p0s, p1c, p1s,
        jnp.asarray(lane_maps()), jnp.asarray(row_maps()),
    )
    swapped = lax.ppermute(other, "grp", [(g, g ^ 1) for g in range(groups)])
    blocks = [mine[k] + swapped[k] for k in range(4)]
    got = [blocks[0]] + [around(blocks[k], k, groups) for k in (1, 2, 3)]
    one, two = pl.pallas_call(
        close_kernel,
        out_shape=(tiles(first_owned), tiles(second_owned)),
        in_specs=[VMEM] * 6,
        out_specs=(VMEM, VMEM),
        compiler_params=pltpu.CompilerParams(vmem_limit_bytes=8 << 20),
        name="close",
    )(*got, ec, es)
    return (to_nodes(leaves), to_nodes(one), to_nodes(two))


def solution(mesh):
    placed = (
        P(("sfc", "grp"), None, None),
        P(("sfc", "grp"), None),
        P(("sfc", "grp")),
        P("sfc", None, "grp"),
        P("sfc", None, None),
        P("sfc", None),
        P("sfc", None),
        P(),
    )

    return jax.shard_map(
        per_device,
        mesh=mesh,
        in_specs=placed,
        out_specs=(
            P(("sfc", "grp"), None, None),
            P(("sfc", "grp"), None, None),
            P(("sfc", "grp"), None, None),
        ),
        check_vma=False,
    )
```

```python
import functools

import jax
import jax.numpy as jnp
import numpy as np
from jax import lax
from jax.experimental import pallas as pl
from jax.experimental.pallas import tpu as pltpu
from jax.sharding import PartitionSpec as P

kappa_leaf = 2.0
f32 = jnp.float32
i32 = jnp.int32
VMEM = pl.BlockSpec(memory_space=pltpu.VMEM)
SMEM = pl.BlockSpec(memory_space=pltpu.SMEM)
ANY = pl.BlockSpec(memory_space=pl.ANY)


def cheb_nodes():
    return np.cos((2.0 * np.arange(8) + 1.0) * np.pi / 16.0)


def lagrange_np(values):
    nodes = cheb_nodes()
    rows = []
    for center in range(8):
        weight = np.ones_like(values)
        for other in range(8):
            if other != center:
                weight = weight * (values - nodes[other]) / (nodes[center] - nodes[other])
        rows.append(weight)
    return np.stack(rows, axis=0)


def child_axis(bit):
    return 0.5 * (2 * bit - 1) + 0.5 * cheb_nodes()


def axis_maps():
    return np.stack([lagrange_np(child_axis(bit)) for bit in range(2)])


def lane_maps():
    maps = axis_maps()
    out = []
    for pick in range(4):
        both = np.kron(maps[pick // 2], maps[pick % 2])
        full = np.kron(np.eye(2), both).T
        high = full.astype(jnp.bfloat16)
        low = (full - high.astype(np.float64)).astype(jnp.bfloat16)
        out.append(np.block([[high, low], [high, np.zeros_like(low)]]))
    return np.stack(out).astype(jnp.bfloat16)


def row_maps():
    maps = axis_maps()
    rows = np.arange(8)[:, None]
    half = np.arange(128)[None, :] // 64
    k = rows // 2
    out = np.zeros((2, 8, 8, 128), np.float32)
    for bit in range(2):
        for step in range(4):
            for flip in range(2):
                to = 2 * k + half
                frm = 2 * ((k + step) % 4) + (half ^ flip)
                out[bit, 2 * step + flip] = maps[bit][to, frm]
    return out


def basis(x):
    t = cheb_nodes()[:4]
    sq = t * t
    x2 = x * x
    s = [x2 - float(v) for v in sq]
    p01 = s[0] * s[1]
    p23 = s[2] * s[3]
    rest = [s[1] * p23, s[0] * p23, p01 * s[3], p01 * s[2]]
    out = [None] * 8
    for j in range(4):
        scale = 1.0 / (np.prod([sq[j] - sq[i] for i in range(4) if i != j]) * 2.0 * t[j])
        q = rest[j] * float(scale)
        out[j] = q * (x + float(t[j]))
        out[7 - j] = q * (float(t[j]) - x)
    return out


def lanes_of(shape):
    return lax.broadcasted_iota(i32, shape, len(shape) - 1)


def lanes_of(shape):
    return lax.broadcasted_iota(i32, shape, len(shape) - 1)


CHUNKS = ((2,), (1,), (3,), (0,))
ORDER = tuple(m for chunk in CHUNKS for m in chunk)


def route(here, plan, leaf, table, labels, picked, scaled):
    bf16 = jnp.bfloat16
    cap = labels.shape[2]
    target = plan[...]
    names = leaf[...].astype(f32)
    along_x = (target - here[0]) % 4
    along_y = (target // 4 - here[1]) % 4
    first = jnp.where(here[2] == 0, along_x, along_y)
    second = jnp.where(here[2] == 0, along_y, along_x)
    place, lead, width, part_of = target * 0, target * 0, target * 0, target * 0
    for c, chunk in enumerate(CHUNKS):
        for n, m in enumerate(chunk):
            hit = second == m
            place = jnp.where(hit, ORDER.index(m), place)
            part_of = jnp.where(hit, c, part_of)
            lead = jnp.where(hit, n, lead)
            width = jnp.where(hit, len(chunk), width)
    code = place * 4 + first
    for d in range(16):
        hit = (code == d).astype(f32)
        picked[pl.ds(8 * d, 8), :] = hit
        scaled[pl.ds(8 * d, 8), :] = hit * names
    square = (128, 128)
    row, lane = rows_of(square), lanes_of(square)
    hits = picked[...].astype(bf16)
    ones = jnp.ones(square, bf16)

    def mul(a, b):
        return jnp.dot(a.astype(bf16), b.astype(bf16), preferred_element_type=f32)

    inside = mul(hits, (row < lane).astype(f32))
    ahead = mul(mul((lane < row).astype(f32), hits), ones)
    same = mul(mul(((lane < row) & (lane // 8 == row // 8)).astype(f32), hits), ones)
    order = jnp.zeros((8, 128), f32)
    slot = jnp.zeros((8, 128), f32)
    for d in range(16):
        part = slice(8 * d, 8 * d + 8)
        hit = picked[pl.ds(8 * d, 8), :]
        order = order + hit * (inside[part] + ahead[part])
        slot = slot + hit * (inside[part] + same[part])
    count = ENTRIES
    lane_w = lanes_of((1, count))
    spans = jnp.zeros((1, count), f32)
    start = jnp.zeros((1, 1), f32)
    before = jnp.zeros((1, 1), f32)
    for c in range(len(CHUNKS)):
        size = jnp.sum((part_of == c).astype(f32), keepdims=True)
        groups = jnp.floor((size + float(GROUP - 1)) * (1.0 / GROUP))
        spans = jnp.where(lane_w == 2 * c, jnp.broadcast_to(start, (1, count)), spans)
        spans = jnp.where(lane_w == 2 * c + 1, jnp.broadcast_to(groups, (1, count)), spans)
        order = order + jnp.where(
            part_of == c, jnp.broadcast_to(start - before, order.shape), 0.0
        )
        start = start + groups * float(GROUP)
        before = before + size
    goal_hi = (first * width + lead).astype(f32)
    ranks = lax.broadcasted_iota(i32, (count, 128), 0).astype(f32)
    seats = row.astype(f32)
    sub = lax.broadcasted_iota(i32, (8, 128), 0)
    lane_f = lanes_of((8, 128)).astype(f32)
    found = jnp.zeros((8, count), f32)
    marks = jnp.zeros((32, 128), f32)
    nt = (((1,), (1,)), ((), ()))
    for r in range(8):
        at = jnp.broadcast_to(order[r : r + 1, :], (count, 128)) == ranks
        goal = jnp.broadcast_to(goal_hi[r : r + 1, :], (8, 128))
        seat = jnp.broadcast_to(slot[r : r + 1, :], (8, 128))
        values = jnp.where(
            sub == 0, 2.0 * lane_f - (lanes_of((8, 128)) % 8).astype(f32),
            jnp.where(sub == 1, float(r), jnp.where(sub == 2, goal, jnp.where(sub == 3, seat, 1.0))),
        )
        found = found + lax.dot_general(
            values.astype(bf16), at.astype(f32).astype(bf16), nt, preferred_element_type=f32
        )
        both = jnp.concatenate(
            [scaled[pl.ds(r, 16, stride=8), :], picked[pl.ds(r, 16, stride=8), :]], axis=0
        )
        sits = jnp.broadcast_to(slot[r : r + 1, :], square) == seats
        marks = marks + lax.dot_general(
            both.astype(bf16), sits.astype(f32).astype(bf16), nt, preferred_element_type=f32
        )
    lines = (found[0:1] + found[1:2] * 256.0).astype(i32)
    goals = (found[2:3] * float(cap_rows(cap)) + found[3:4] + found[4:5]).astype(i32)
    for n, values in enumerate((lines, goals)):
        for r in range(count // 128):
            at = n * (count // 128) + r
            table[at : at + 1, :] = values[:, 128 * r : 128 * r + 128]
    at = 2 * (count // 128)
    table[at : at + 1, :] = spans[:, :128].astype(i32)
    label = marks[:16] + 256.0 * (1.0 - marks[16:])
    for d in range(16):
        total = jnp.sum(marks[16 + d : 17 + d], axis=1, keepdims=True)
        labels[d] = jnp.where(
            sub == 0,
            jnp.broadcast_to(label[d : d + 1], (8, 128)),
            jnp.broadcast_to(total, (8, 128)),
        )


def cap_rows(cap):
    return cap + 1


GROUP = 16
ENTRIES = 1152


def expand_kernel(chunk, *refs):
    if chunk:
        table, labels, pts, *refs = refs
    else:
        here, plan, leaf, pts, *refs = refs
    outs, refs = refs[:4], refs[4:]
    if not chunk:
        listed, labels, *refs = refs
    held, all_pts, stage, bx, by, bz, sems, load_sems, *refs = refs
    first = sum(len(c) for c in CHUNKS[:chunk])
    wide = len(CHUNKS[chunk])
    rows = outs[0].shape[1]
    cap = rows - 1
    span = all_pts.shape[0] // 5
    loads = [
        pltpu.make_async_copy(
            pts.at[pl.ds(span * axis, span)], all_pts.at[pl.ds(span * axis, span)],
            load_sems.at[axis],
        )
        for axis in range(5)
    ]
    for load in loads:
        load.start()
    if not chunk:
        table, picked, scaled, sem = refs
        route(here, plan, leaf, listed, labels, picked, scaled)
        copy = pltpu.make_async_copy(listed, table, sem)
        copy.start()
        copy.wait()

    def look(base, which, u=0):
        if chunk:
            return table[base + (which * ENTRIES + u)]
        return table[(base >> 7) + which * (ENTRIES // 128), (base & 127) + u]

    for k in range(4):
        for n in range(wide):
            held[1 + (k * wide + n) * rows + cap] = labels[4 * (first + n) + k]
    begin = look(i32(0), 2, 2 * chunk)
    trips = look(i32(0), 2, 2 * chunk + 1)
    for load in loads:
        load.wait()

    def fetch(g, u, bank):
        line = look(begin + g * GROUP, 0, u)
        for axis in range(3):
            for h in range(2):
                stage[bank, axis, h, pl.ds(u, 1), :] = all_pts[
                    pl.ds(line + (span * axis + 8 * h), 1), :
                ]

    def tabulate(piece, bank):
        u, h, axis = 8 * (piece // 6), piece // 3 % 2, piece % 3
        values = basis(stage[bank, axis, h, pl.ds(u, 8), :])
        for a in range(8):
            if axis == 1:
                by[bank, h, pl.ds(GROUP * a + u, 8), :] = values[a]
            else:
                ref = bz if axis else bx
                ref[bank, h, pl.ds(8 * u + a, 8, stride=8), :] = values[a]

    def consume(g, u, bank):
        base = begin + g * GROUP
        line = look(base, 0, u)
        weighted, pair = [], []
        for h in range(2):
            lx = bx[bank, h, pl.ds(8 * u, 8), :]
            lz = bz[bank, h, pl.ds(8 * u, 8), :]
            re, im = (
                jnp.broadcast_to(
                    all_pts[pl.ds(line + (span * (3 + part) + 8 * h), 1), :], lx.shape
                )
                for part in range(2)
            )
            weighted.append(jnp.concatenate([re * lx, im * lx], axis=0).astype(jnp.bfloat16))
            pair.append(
                jnp.concatenate(
                    [
                        jnp.broadcast_to(by[bank, h, pl.ds(GROUP * b + u, 1), :], lz.shape) * lz
                        for b in range(8)
                    ],
                    axis=0,
                ).astype(jnp.bfloat16)
            )
        res = lax.dot_general(
            jnp.concatenate(weighted, axis=1),
            jnp.concatenate(pair, axis=1),
            (((1,), (1,)), ((), ())),
            preferred_element_type=f32,
        )
        held[look(base, 1, u)] = jnp.concatenate([res[:8], res[8:]], axis=1)

    pieces = 6 * GROUP // 8
    for u in range(GROUP):
        fetch(0, u, 0)
    for piece in range(pieces):
        tabulate(piece, 0)
    for u in range(GROUP):
        fetch(1, u, 1)

    def step(g, carry):
        bank = g & 1
        for u in range(GROUP):
            consume(g, u, bank)
            if u % 4 == 3:
                for piece in range(3 * (u // 4), 3 * (u // 4) + 3):
                    tabulate(piece, 1 - bank)
                for v in range(u - 3, u + 1):
                    fetch(g + 2, v, bank)
        return carry

    lax.fori_loop(0, trips, step, 0)
    copies = []
    for k in range(4):
        for n in range(wide):
            copies.append(
                pltpu.make_async_copy(
                    held.at[pl.ds(1 + (k * wide + n) * rows, rows)], outs[k].at[n], sems.at[k, n]
                )
            )
    for copy in copies:
        copy.start()
    for copy in copies:
        copy.wait()


def expand(chunk, routing, pts, cap):
    wide = len(CHUNKS[chunk])
    out_shape = [jax.ShapeDtypeStruct((wide, cap + 1, 8, 128), f32)] * 4
    out_specs = [ANY] * 4
    scratch = []
    if chunk:
        in_specs = [SMEM, VMEM, ANY]
    else:
        in_specs = [SMEM, VMEM, VMEM, ANY]
        out_shape += [
            jax.ShapeDtypeStruct((24, 128), i32),
            jax.ShapeDtypeStruct((16, 8, 128), f32),
        ]
        out_specs += [VMEM] * 2
        scratch = [
            pltpu.SMEM((24, 128), i32),
            pltpu.VMEM((128, 128), f32),
            pltpu.VMEM((128, 128), f32),
            pltpu.SemaphoreType.DMA(()),
        ]
    return pl.pallas_call(
        functools.partial(expand_kernel, chunk),
        out_shape=out_shape,
        in_specs=in_specs,
        out_specs=out_specs,
        scratch_shapes=[
            pltpu.VMEM((4 * wide * (cap + 1) + 1, 8, 128), f32),
            pltpu.VMEM(pts.shape, f32),
            pltpu.VMEM((2, 3, 2, GROUP, 128), f32),
            *[pltpu.VMEM((2, 2, 8 * GROUP, 128), f32)] * 3,
            pltpu.SemaphoreType.DMA((4, wide)),
            pltpu.SemaphoreType.DMA((5,)),
            *scratch,
        ],
        cost_estimate=pl.CostEstimate(
            flops=wide * (1 << 28), bytes_accessed=1 << 23, transcendentals=0
        ),
        name="expand",
    )(*routing, pts)


def gather_kernel(wide, *refs):
    arrived, outs = refs[:4], refs[4 : 4 + wide]
    held, banks, labels, names, sem, sems = refs[4 + wide :]
    cap = held.shape[2] - 1
    loads = [pltpu.make_async_copy(arrived[k], held.at[k], sems.at[k]) for k in range(4)]
    for load in loads:
        load.start()
    for n in range(wide):
        outs[n][...] = jnp.zeros(outs[n].shape, f32)
        for bank in range(3):
            banks[bank, n] = jnp.zeros(outs[n].shape, f32)
    for load in loads:
        load.wait()
    for k in range(4):
        for n in range(wide):
            labels[pl.ds(8 * (k * wide + n), 8), :] = held[k, n, cap].astype(i32)
    copy = pltpu.make_async_copy(labels, names, sem)
    copy.start()
    copy.wait()
    for k in range(4):
        most = names[8 * k * wide + 1, 0]
        for n in range(1, wide):
            most = jnp.maximum(most, names[8 * (k * wide + n) + 1, 0])

        def rows4(r, carry):
            for u in range(4):
                for n in range(wide):
                    slot = r * 4 + u
                    where = names[8 * (k * wide + n), slot]
                    if u:
                        banks[u - 1, n, where] = banks[u - 1, n, where] + held[k, n, slot]
                    else:
                        outs[n][where] = outs[n][where] + held[k, n, slot]
            return carry

        lax.fori_loop(0, (most + 3) // 4, rows4, 0)

    def join(i, carry):
        part = pl.ds(pl.multiple_of(i * 16, 16), 16)
        for n in range(wide):
            outs[n][part] = (outs[n][part] + banks[0, n, part]) + (
                banks[1, n, part] + banks[2, n, part]
            )
        return carry

    lax.fori_loop(0, (outs[0].shape[0] - 1) // 16, join, 0)


def gather(arrived, leaf_count):
    wide, rows = arrived[0].shape[:2]
    return pl.pallas_call(
        functools.partial(gather_kernel, wide),
        out_shape=[jax.ShapeDtypeStruct((leaf_count + 1, 8, 128), f32)] * wide,
        in_specs=[pl.BlockSpec(memory_space=pl.ANY)] * 4,
        out_specs=[VMEM] * wide,
        scratch_shapes=[
            pltpu.VMEM((4, wide, rows, 8, 128), f32),
            pltpu.VMEM((3, wide, leaf_count + 1, 8, 128), f32),
            pltpu.VMEM((32 * wide, 128), i32),
            pltpu.SMEM((32 * wide, 128), i32),
            pltpu.SemaphoreType.DMA(()),
            pltpu.SemaphoreType.DMA((4,)),
        ],
        cost_estimate=pl.CostEstimate(
            flops=wide * (1 << 26), bytes_accessed=wide << 22, transcendentals=0
        ),
        compiler_params=pltpu.CompilerParams(vmem_limit_bytes=(8 + 10 * wide) << 20),
        name="gather",
    )(*arrived)


def rows_of(shape):
    return lax.broadcasted_iota(i32, shape, len(shape) - 2)


def swap_rows(t):
    even = rows_of(t.shape) % 2 == 0
    axis = len(t.shape) - 2
    return jnp.where(even, pltpu.roll(t, 7, axis), pltpu.roll(t, 1, axis))


def spin(t, cosine, sine):
    return t * cosine + swap_rows(t) * sine


def row_mix(t, maps, bit):
    flipped = pltpu.roll(t, 64, 2)
    total = None
    for step in range(4):
        for flip in range(2):
            part = flipped if flip else t
            if step:
                part = pltpu.roll(part, 8 - 2 * step, 1)
            term = part * maps[bit, 2 * step + flip]
            total = term if total is None else total + term
    return total


EARLY = 2

SEATS = 36


def turn(ca, sa, cb, sb):
    return ca * cb - sa * sb, sa * cb + ca * sb


def twice(c, s):
    return c * c - s * s, 2.0 * (s * c)


def phases_kernel(
    here, slots, boxes, cones, box_cones, cosine, sine, p0c, p0s, p1c, p1s, ec, es, goal,
    t0c, t0s, t1c, t1s, t2c, t2s,
):
    side = here[2]
    sign = jnp.where(rows_of((8, 128)) % 2 == 0, -1.0, 1.0)

    def cone_tables(n, carry):
        xs = [(cosine[n, v], sine[n, v]) for v in range(3)]
        wide = [
            tuple(jnp.broadcast_to(t[n, 3, pl.ds(v, 1), :], (8, 128)) for t in (cosine, sine))
            for v in range(5)
        ]
        t1c[n], t1s[n] = turn(*xs[2], *wide[4])
        xs2 = [twice(*x) for x in xs[:2]]
        for v in range(4):
            wide2 = twice(*wide[v])
            for bit in range(2):
                at = n * 8 + 4 * bit + v
                t0c[at], t0s[at] = turn(*xs[bit], *wide[v])
                t2c[at], t2s[at] = turn(*xs2[bit], *wide2)
        return carry

    lax.fori_loop(0, cosine.shape[0], cone_tables, 0)

    def child(j, carry):
        for o in range(8):
            p = slots[32 * o + j]
            e = cones[p] * 8 + o
            p0c[o, j] = t0c[e]
            p0s[o, j] = t0s[e] * sign
            owner = p >> 5
            goal[32 * o + j] = ((((owner & 1) ^ side) << 2) + (owner >> 1)) * SEATS + (p & 31)
            a = cones[8 * j + o]
            b = box_cones[boxes[32 * o + j]] * 8 + o
            c, s = turn(t1c[a], t1s[a], t2c[b], t2s[b])
            p1c[o, j] = c
            p1s[o, j] = s * sign
        return carry

    lax.fori_loop(0, 32, child, 0)
    me = 2 * here[3] + side
    for n in range(SEATS):
        if n < 32:
            a = cones[32 * me + n]
            c, s = t1c[a], t1s[a]
        else:
            a = box_cones[4 * me + n - 32]
            c, s = twice(t1c[a], t1s[a])
        ec[n] = c
        es[n] = s * sign


def lane_mix(t, both, octant):
    count = t.shape[0]
    flat = t.reshape(count * 8, 128)
    high = flat.astype(jnp.bfloat16)
    low = (flat - high.astype(f32)).astype(jnp.bfloat16)
    res = jnp.dot(
        jnp.concatenate([high, low], axis=1), both[octant % 4], preferred_element_type=f32
    )
    return (res[:, :128] + res[:, 128:]).reshape(count, 8, 128)


def levels_kernel(
    here, goal, boxes, a0, a1, a2, a3, p0c, p0s, p1c, p1s, both, rows, leaves, mine, other,
    held, turns, lanes_in, rows_in, solved, acc, upper, moved, sems, out_sems,
):
    count = leaves.shape[0]
    sums = [
        pltpu.make_async_copy(ref.at[pl.ds(0, count)], held.at[n], sems.at[n])
        for n, ref in enumerate((a0, a1, a2, a3))
    ]
    maps = [
        pltpu.make_async_copy(both, lanes_in, sems.at[4]),
        pltpu.make_async_copy(rows, rows_in, sems.at[5]),
    ]
    angles = [
        pltpu.make_async_copy(ref, turns.at[n], sems.at[6 + n])
        for n, ref in enumerate((p0c, p0s, p1c, p1s))
    ]
    for copy in sums + maps + angles:
        copy.start()
    acc[...] = jnp.zeros(acc.shape, f32)
    upper[...] = jnp.zeros(upper.shape, f32)
    for copy in sums:
        copy.wait()
    step = 16
    shape = (step, 8, 128)
    own = rows_of(shape) % 2 == lanes_of(shape) // 64

    def settle(n, carry):
        base = pl.multiple_of(n * step, step)
        t = (held[0, pl.ds(base, step)] + held[1, pl.ds(base, step)]) + (
            held[2, pl.ds(base, step)] + held[3, pl.ds(base, step)]
        )
        solved[pl.ds(base, step)] = jnp.where(own, t, swap_rows(pltpu.roll(t, 64, 2)))
        return carry

    lax.fori_loop(0, count // step, settle, 0)
    done = [pltpu.make_async_copy(solved, leaves, out_sems.at[8])]
    done[0].start()
    for copy in maps + angles[:2]:
        copy.wait()

    def spread(o, start, ref, spots):
        sums = [ref[spots[j]] + moved[o % 2, start + j] for j in range(8)]
        for j in range(8):
            ref[spots[j]] = sums[j]

    for o in range(8):
        for part in range(0, 32, 8):
            t = jnp.stack([solved[8 * (part + j) + o] for j in range(8)])
            t = spin(t, turns[0, o, part : part + 8], turns[1, o, part : part + 8])
            moved[o % 2, part : part + 8] = row_mix(lane_mix(t, lanes_in, o), rows_in, o // 4)
        for part in range(0, 32, 8):
            spread(o, part, acc, [goal[32 * o + part + j] for j in range(8)])

    apart = [here[2] * 4 * SEATS, (1 - here[2]) * 4 * SEATS]
    for copy in angles[2:]:
        copy.wait()
    for o in range(8):
        for part in range(0, 32, 8):
            tiles = []
            for j in range(8):
                p = 8 * (part + j) + o
                owner = p // 32
                tiles.append(acc[(owner // 2) * SEATS + p % 32 + apart[owner % 2]])
            t = spin(
                jnp.stack(tiles), turns[2, o, part : part + 8], turns[3, o, part : part + 8]
            )
            moved[o % 2, part : part + 8] = lane_mix(t, lanes_in, o)
        for part in range(0, 32, 8):
            spread(
                o, part, upper,
                [boxes[32 * o + part + j] + 32 * (o // 4) for j in range(8)],
            )
    for part in range(0, 32, 8):
        t = row_mix(upper[part : part + 8], rows_in, 0)
        t = t + row_mix(upper[32 + part : 40 + part], rows_in, 1)
        for j in range(8):
            q = part + j
            owner = q // 4
            acc[(owner // 2) * SEATS + 32 + q % 4 + apart[owner % 2]] = t[j]
    for k in range(4):
        z = (here[3] + k) % 4
        done += [
            pltpu.make_async_copy(
                acc.at[pl.ds((4 + z) * SEATS, SEATS)], other.at[k], out_sems.at[4 + k]
            ),
            pltpu.make_async_copy(acc.at[pl.ds(z * SEATS, SEATS)], mine.at[k], out_sems.at[k]),
        ]
    for copy in done[1:]:
        copy.start()
    for copy in done:
        copy.wait()


def close_kernel(g0, g1, g2, g3, ec, es, out_one, out_two):
    owned = out_one.shape[0]
    for n in range(SEATS):
        t = spin((g0[n] + g1[n]) + (g2[n] + g3[n]), ec[n], es[n])
        if n < owned:
            out_one[n] = t
        else:
            out_two[n - owned] = t


def cone_places():
    nodes = cheb_nodes()
    rows = np.arange(8)[:, None]
    lanes = np.arange(128)[None, :]
    a = 2 * (rows // 2) + lanes // 64
    out = np.zeros((3, 4, 8, 128))
    out[0, 0], out[0, 1], out[0, 2] = child_axis(0)[a], child_axis(1)[a], -nodes[a]
    b, c = np.arange(128) % 64 // 8, np.arange(128) % 8
    for v in range(4):
        out[1, 3, v], out[2, 3, v] = child_axis(v // 2)[b], child_axis(v % 2)[c]
    out[1, 3, 4], out[2, 3, 4] = -nodes[b], -nodes[c]
    return out.astype(np.float32)


def to_nodes(tiles):
    count = tiles.shape[0]
    return tiles.reshape(count, 4, 2, 128).transpose(0, 2, 1, 3).reshape(count, 2, 512)


def cone_vectors(cone_angles):
    azimuth = cone_angles[:, 0]
    polar = cone_angles[:, 1]
    return jnp.stack(
        [jnp.cos(azimuth) * jnp.sin(polar), jnp.sin(azimuth) * jnp.sin(polar), jnp.cos(polar)],
        axis=1,
    )


def hop(x, shift, leg, groups):
    pairs = []
    for s in range(16):
        for g in range(groups):
            y, x0 = s // 4, s % 4
            if g % 2 == leg:
                x0 = (x0 + shift) % 4
            else:
                y = (y + shift) % 4
            pairs.append((s * groups + g, (4 * y + x0) * groups + g))
    return lax.ppermute(x, ("sfc", "grp"), pairs)


def around(x, shift, groups):
    pairs = [(g, (g + 2 * shift) % groups) for g in range(groups)]
    return lax.ppermute(x, "grp", pairs)


def after(value, *others):
    return lax.optimization_barrier((value, *others))[0]


def per_device(
    bin_points, bin_plan, bin_leaf, leaf_slots, box_slots, parent_cone, box_cone, cone_angles
):
    groups = lax.axis_size("grp")
    rank = lax.axis_index("grp")
    cap = bin_points.shape[0] // 8
    leaf_count = leaf_slots.shape[2] * 8
    first_owned = parent_cone.shape[1] // groups
    second_owned = box_cone.shape[1] // groups
    tile = jax.ShapeDtypeStruct((8, 128), f32)

    def tiles(*lead):
        return jax.ShapeDtypeStruct((*lead, *tile.shape), f32)

    me = lax.axis_index("sfc")
    here = jnp.stack([me % 4, me // 4, rank % 2, rank // 2]).astype(i32)
    bins, _, width = bin_points.shape
    pts = jnp.transpose(bin_points.reshape(bins // 8, 8, 5, width // 128, 128), (2, 0, 3, 1, 4))
    pts = pts.reshape(-1, 128)
    arrived = []
    routing = (here, bin_plan.reshape(bins // 128, 128), bin_leaf.reshape(bins // 128, 128))
    held = [None] * 4
    last = None

    def collect(c, last):
        got = [after(arrived[c][0], last)] + arrived[c][1:]
        sums = gather(got, leaf_count)
        for m, part in zip(CHUNKS[c], sums):
            held[m] = hop(part, m, 1, groups) if m else part
        return sums[0]

    for c in range(len(CHUNKS)):
        sent = expand(c, routing, pts, cap)
        if not c:
            *sent, table, labels = sent
            table = table.reshape(-1)
        last = sent[0]
        moved = [sent[0]]
        for k in (2, 1, 3):
            moved.append(hop(sent[k], k, 0, groups))
        arrived.append(moved)
        if c >= EARLY and c + 1 < len(CHUNKS):
            last = collect(c - EARLY, last)
        table = after(table, last)
        routing = (table, labels)

    cone_angles = after(cone_angles, sent[0])
    directions = cone_vectors(cone_angles)
    places = jnp.asarray(cone_places())
    angle = (
        directions[:, 0, None, None, None] * places[None, 0]
        + directions[:, 1, None, None, None] * places[None, 1]
        + directions[:, 2, None, None, None] * places[None, 2]
    ) * kappa_leaf
    make_phases = pl.pallas_call(
        phases_kernel,
        out_shape=(tiles(8, 32),) * 4 + (tiles(SEATS),) * 2 + (jax.ShapeDtypeStruct((256,), i32),),
        in_specs=[SMEM] * 5 + [VMEM] * 2,
        out_specs=(VMEM,) * 6 + (SMEM,),
        scratch_shapes=[pltpu.VMEM((n, 8, 128), f32) for n in (128, 128, 16, 16, 128, 128)],
        compiler_params=pltpu.CompilerParams(vmem_limit_bytes=16 << 20),
        name="phases",
    )
    slots, boxes = leaf_slots.reshape(-1), box_slots.reshape(-1)
    p0c, p0s, p1c, p1s, ec, es, goal = make_phases(
        here, slots, boxes, parent_cone[0], box_cone[0], jnp.cos(angle), jnp.sin(angle)
    )

    for c in range(len(CHUNKS) - 1 - EARLY, len(CHUNKS)):
        last = collect(c, last)

    leaves, mine, other = pl.pallas_call(
        levels_kernel,
        out_shape=(tiles(leaf_count), tiles(4, SEATS), tiles(4, SEATS)),
        in_specs=[SMEM] * 3 + [ANY] * 10,
        out_specs=(ANY,) * 3,
        scratch_shapes=[
            pltpu.VMEM((4, leaf_count, 8, 128), f32),
            pltpu.VMEM((4, 8, 32, 8, 128), f32),
            pltpu.VMEM((4, 256, 256), jnp.bfloat16),
            pltpu.VMEM((2, 8, 8, 128), f32),
            pltpu.VMEM((leaf_count, 8, 128), f32),
            pltpu.VMEM((8 * SEATS, 8, 128), f32),
            pltpu.VMEM((64, 8, 128), f32),
            pltpu.VMEM((2, 32, 8, 128), f32),
            pltpu.SemaphoreType.DMA((10,)),
            pltpu.SemaphoreType.DMA((9,)),
        ],
        compiler_params=pltpu.CompilerParams(vmem_limit_bytes=20 << 20),
        name="levels",
    )(
        here, goal, boxes, *held, p0c, p0s, p1c, p1s,
        jnp.asarray(lane_maps()), jnp.asarray(row_maps()),
    )
    swapped = lax.ppermute(other, "grp", [(g, g ^ 1) for g in range(groups)])
    blocks = [mine[k] + swapped[k] for k in range(4)]
    got = [blocks[0]] + [around(blocks[k], k, groups) for k in (1, 2, 3)]
    one, two = pl.pallas_call(
        close_kernel,
        out_shape=(tiles(first_owned), tiles(second_owned)),
        in_specs=[VMEM] * 6,
        out_specs=(VMEM, VMEM),
        compiler_params=pltpu.CompilerParams(vmem_limit_bytes=8 << 20),
        name="close",
    )(*got, ec, es)
    return (to_nodes(leaves), to_nodes(one), to_nodes(two))


def solution(mesh):
    placed = (
        P(("sfc", "grp"), None, None),
        P(("sfc", "grp"), None),
        P(("sfc", "grp")),
        P("sfc", None, "grp"),
        P("sfc", None, None),
        P("sfc", None),
        P("sfc", None),
        P(),
    )

    return jax.shard_map(
        per_device,
        mesh=mesh,
        in_specs=placed,
        out_specs=(
            P(("sfc", "grp"), None, None),
            P(("sfc", "grp"), None, None),
            P(("sfc", "grp"), None, None),
        ),
        check_vma=False,
    )
```

```python
import functools

import jax
import jax.numpy as jnp
import numpy as np
from jax import lax
from jax.experimental import pallas as pl
from jax.experimental.pallas import tpu as pltpu
from jax.sharding import PartitionSpec as P

kappa_leaf = 2.0
f32 = jnp.float32
i32 = jnp.int32
VMEM = pl.BlockSpec(memory_space=pltpu.VMEM)
SMEM = pl.BlockSpec(memory_space=pltpu.SMEM)
ANY = pl.BlockSpec(memory_space=pl.ANY)


def cheb_nodes():
    return np.cos((2.0 * np.arange(8) + 1.0) * np.pi / 16.0)


def lagrange_np(values):
    nodes = cheb_nodes()
    rows = []
    for center in range(8):
        weight = np.ones_like(values)
        for other in range(8):
            if other != center:
                weight = weight * (values - nodes[other]) / (nodes[center] - nodes[other])
        rows.append(weight)
    return np.stack(rows, axis=0)


def child_axis(bit):
    return 0.5 * (2 * bit - 1) + 0.5 * cheb_nodes()


def axis_maps():
    return np.stack([lagrange_np(child_axis(bit)) for bit in range(2)])


def lane_maps():
    maps = axis_maps()
    out = []
    for pick in range(4):
        both = np.kron(maps[pick // 2], maps[pick % 2])
        full = np.kron(np.eye(2), both).T
        high = full.astype(jnp.bfloat16)
        low = (full - high.astype(np.float64)).astype(jnp.bfloat16)
        out.append(np.block([[high, low], [high, np.zeros_like(low)]]))
    return np.stack(out).astype(jnp.bfloat16)


def row_maps():
    maps = axis_maps()
    rows = np.arange(8)[:, None]
    half = np.arange(128)[None, :] // 64
    k = rows // 2
    out = np.zeros((2, 8, 8, 128), np.float32)
    for bit in range(2):
        for step in range(4):
            for flip in range(2):
                to = 2 * k + half
                frm = 2 * ((k + step) % 4) + (half ^ flip)
                out[bit, 2 * step + flip] = maps[bit][to, frm]
    return out


def basis(x):
    t = cheb_nodes()[:4]
    sq = t * t
    x2 = x * x
    s = [x2 - float(v) for v in sq]
    p01 = s[0] * s[1]
    p23 = s[2] * s[3]
    rest = [s[1] * p23, s[0] * p23, p01 * s[3], p01 * s[2]]
    out = [None] * 8
    for j in range(4):
        scale = 1.0 / (np.prod([sq[j] - sq[i] for i in range(4) if i != j]) * 2.0 * t[j])
        q = rest[j] * float(scale)
        out[j] = q * (x + float(t[j]))
        out[7 - j] = q * (float(t[j]) - x)
    return out


def lanes_of(shape):
    return lax.broadcasted_iota(i32, shape, len(shape) - 1)


def lanes_of(shape):
    return lax.broadcasted_iota(i32, shape, len(shape) - 1)


CHUNKS = ((2,), (1,), (3,), (0,))
ORDER = tuple(m for chunk in CHUNKS for m in chunk)


def route(here, plan, leaf, table, labels, picked, scaled):
    bf16 = jnp.bfloat16
    cap = labels.shape[2]
    target = plan[...]
    names = leaf[...].astype(f32)
    along_x = (target - here[0]) % 4
    along_y = (target // 4 - here[1]) % 4
    first = jnp.where(here[2] == 0, along_x, along_y)
    second = jnp.where(here[2] == 0, along_y, along_x)
    place, lead, width, part_of = target * 0, target * 0, target * 0, target * 0
    for c, chunk in enumerate(CHUNKS):
        for n, m in enumerate(chunk):
            hit = second == m
            place = jnp.where(hit, ORDER.index(m), place)
            part_of = jnp.where(hit, c, part_of)
            lead = jnp.where(hit, n, lead)
            width = jnp.where(hit, len(chunk), width)
    code = place * 4 + first
    for d in range(16):
        hit = (code == d).astype(f32)
        picked[pl.ds(8 * d, 8), :] = hit
        scaled[pl.ds(8 * d, 8), :] = hit * names
    square = (128, 128)
    row, lane = rows_of(square), lanes_of(square)
    hits = picked[...].astype(bf16)
    ones = jnp.ones(square, bf16)

    def mul(a, b):
        return jnp.dot(a.astype(bf16), b.astype(bf16), preferred_element_type=f32)

    inside = mul(hits, (row < lane).astype(f32))
    ahead = mul(mul((lane < row).astype(f32), hits), ones)
    same = mul(mul(((lane < row) & (lane // 8 == row // 8)).astype(f32), hits), ones)
    order = jnp.zeros((8, 128), f32)
    slot = jnp.zeros((8, 128), f32)
    for d in range(16):
        part = slice(8 * d, 8 * d + 8)
        hit = picked[pl.ds(8 * d, 8), :]
        order = order + hit * (inside[part] + ahead[part])
        slot = slot + hit * (inside[part] + same[part])
    count = ENTRIES
    lane_w = lanes_of((1, count))
    spans = jnp.zeros((1, count), f32)
    start = jnp.zeros((1, 1), f32)
    before = jnp.zeros((1, 1), f32)
    for c in range(len(CHUNKS)):
        size = jnp.sum((part_of == c).astype(f32), keepdims=True)
        groups = jnp.floor((size + float(GROUP - 1)) * (1.0 / GROUP))
        spans = jnp.where(lane_w == 2 * c, jnp.broadcast_to(start, (1, count)), spans)
        spans = jnp.where(lane_w == 2 * c + 1, jnp.broadcast_to(groups, (1, count)), spans)
        order = order + jnp.where(
            part_of == c, jnp.broadcast_to(start - before, order.shape), 0.0
        )
        start = start + groups * float(GROUP)
        before = before + size
    goal_hi = (first * width + lead).astype(f32)
    ranks = lax.broadcasted_iota(i32, (count, 128), 0).astype(f32)
    seats = row.astype(f32)
    sub = lax.broadcasted_iota(i32, (8, 128), 0)
    lane_f = lanes_of((8, 128)).astype(f32)
    found = jnp.zeros((8, count), f32)
    marks = jnp.zeros((32, 128), f32)
    nt = (((1,), (1,)), ((), ()))
    for r in range(8):
        at = jnp.broadcast_to(order[r : r + 1, :], (count, 128)) == ranks
        goal = jnp.broadcast_to(goal_hi[r : r + 1, :], (8, 128))
        seat = jnp.broadcast_to(slot[r : r + 1, :], (8, 128))
        values = jnp.where(
            sub == 0, 2.0 * lane_f - (lanes_of((8, 128)) % 8).astype(f32),
            jnp.where(sub == 1, float(r), jnp.where(sub == 2, goal, jnp.where(sub == 3, seat, 1.0))),
        )
        found = found + lax.dot_general(
            values.astype(bf16), at.astype(f32).astype(bf16), nt, preferred_element_type=f32
        )
        both = jnp.concatenate(
            [scaled[pl.ds(r, 16, stride=8), :], picked[pl.ds(r, 16, stride=8), :]], axis=0
        )
        sits = jnp.broadcast_to(slot[r : r + 1, :], square) == seats
        marks = marks + lax.dot_general(
            both.astype(bf16), sits.astype(f32).astype(bf16), nt, preferred_element_type=f32
        )
    lines = (found[0:1] + found[1:2] * 256.0).astype(i32)
    goals = (found[2:3] * float(cap_rows(cap)) + found[3:4] + found[4:5]).astype(i32)
    for n, values in enumerate((lines, goals)):
        for r in range(count // 128):
            at = n * (count // 128) + r
            table[at : at + 1, :] = values[:, 128 * r : 128 * r + 128]
    at = 2 * (count // 128)
    table[at : at + 1, :] = spans[:, :128].astype(i32)
    label = marks[:16] + 256.0 * (1.0 - marks[16:])
    for d in range(16):
        total = jnp.sum(marks[16 + d : 17 + d], axis=1, keepdims=True)
        labels[d] = jnp.where(
            sub == 0,
            jnp.broadcast_to(label[d : d + 1], (8, 128)),
            jnp.broadcast_to(total, (8, 128)),
        )


def cap_rows(cap):
    return cap + 1


GROUP = 16
ENTRIES = 1152


def expand_kernel(chunk, *refs):
    if chunk:
        table, labels, pts, *refs = refs
    else:
        here, plan, leaf, pts, *refs = refs
    outs, refs = refs[:4], refs[4:]
    if not chunk:
        listed, labels, *refs = refs
    held, stage, bx, by, bz, sems, *refs = refs
    if chunk:
        all_pts = pts
    else:
        all_pts, load_sems, *refs = refs
    first = sum(len(c) for c in CHUNKS[:chunk])
    wide = len(CHUNKS[chunk])
    rows = outs[0].shape[1]
    cap = rows - 1
    span = all_pts.shape[0] // 5
    loads = [
        pltpu.make_async_copy(
            pts.at[pl.ds(span * axis, span)], all_pts.at[pl.ds(span * axis, span)],
            load_sems.at[axis],
        )
        for axis in range(0 if chunk else 5)
    ]
    for load in loads:
        load.start()
    if not chunk:
        table, picked, scaled, sem = refs
        route(here, plan, leaf, listed, labels, picked, scaled)
        copy = pltpu.make_async_copy(listed, table, sem)
        copy.start()
        copy.wait()

    def look(base, which, u=0):
        if chunk:
            return table[base + (which * ENTRIES + u)]
        return table[(base >> 7) + which * (ENTRIES // 128), (base & 127) + u]

    for k in range(4):
        for n in range(wide):
            held[1 + (k * wide + n) * rows + cap] = labels[4 * (first + n) + k]
    begin = look(i32(0), 2, 2 * chunk)
    trips = look(i32(0), 2, 2 * chunk + 1)
    for load in loads:
        load.wait()

    def fetch(g, u, bank):
        line = look(begin + g * GROUP, 0, u)
        for axis in range(3):
            for h in range(2):
                stage[bank, axis, h, pl.ds(u, 1), :] = all_pts[
                    pl.ds(line + (span * axis + 8 * h), 1), :
                ]

    def tabulate(piece, bank):
        u, h, axis = 8 * (piece // 6), piece // 3 % 2, piece % 3
        values = basis(stage[bank, axis, h, pl.ds(u, 8), :])
        for a in range(8):
            if axis == 1:
                by[bank, h, pl.ds(GROUP * a + u, 8), :] = values[a]
            else:
                ref = bz if axis else bx
                ref[bank, h, pl.ds(8 * u + a, 8, stride=8), :] = values[a]

    def consume(g, u, bank):
        base = begin + g * GROUP
        line = look(base, 0, u)
        weighted, pair = [], []
        for h in range(2):
            lx = bx[bank, h, pl.ds(8 * u, 8), :]
            lz = bz[bank, h, pl.ds(8 * u, 8), :]
            re, im = (
                jnp.broadcast_to(
                    all_pts[pl.ds(line + (span * (3 + part) + 8 * h), 1), :], lx.shape
                )
                for part in range(2)
            )
            weighted.append(jnp.concatenate([re * lx, im * lx], axis=0).astype(jnp.bfloat16))
            pair.append(
                jnp.concatenate(
                    [
                        jnp.broadcast_to(by[bank, h, pl.ds(GROUP * b + u, 1), :], lz.shape) * lz
                        for b in range(8)
                    ],
                    axis=0,
                ).astype(jnp.bfloat16)
            )
        res = lax.dot_general(
            jnp.concatenate(weighted, axis=1),
            jnp.concatenate(pair, axis=1),
            (((1,), (1,)), ((), ())),
            preferred_element_type=f32,
        )
        held[look(base, 1, u)] = jnp.concatenate([res[:8], res[8:]], axis=1)

    pieces = 6 * GROUP // 8
    for u in range(GROUP):
        fetch(0, u, 0)
    for piece in range(pieces):
        tabulate(piece, 0)
    for u in range(GROUP):
        fetch(1, u, 1)

    def step(g, carry):
        bank = g & 1
        for u in range(GROUP):
            consume(g, u, bank)
            if u % 4 == 3:
                for piece in range(3 * (u // 4), 3 * (u // 4) + 3):
                    tabulate(piece, 1 - bank)
                for v in range(u - 3, u + 1):
                    fetch(g + 2, v, bank)
        return carry

    lax.fori_loop(0, trips, step, 0)
    copies = []
    for k in range(4):
        for n in range(wide):
            copies.append(
                pltpu.make_async_copy(
                    held.at[pl.ds(1 + (k * wide + n) * rows, rows)], outs[k].at[n], sems.at[k, n]
                )
            )
    for copy in copies:
        copy.start()
    for copy in copies:
        copy.wait()


def expand(chunk, routing, pts, cap):
    wide = len(CHUNKS[chunk])
    out_shape = [jax.ShapeDtypeStruct((wide, cap + 1, 8, 128), f32)] * 4
    out_specs = [ANY] * 4
    scratch = []
    if chunk:
        in_specs = [SMEM, VMEM, VMEM]
    else:
        in_specs = [SMEM, VMEM, VMEM, ANY]
        out_shape += [
            jax.ShapeDtypeStruct((24, 128), i32),
            jax.ShapeDtypeStruct((16, 8, 128), f32),
        ]
        out_specs += [VMEM] * 2
        scratch = [
            pltpu.VMEM(pts.shape, f32),
            pltpu.SemaphoreType.DMA((5,)),
            pltpu.SMEM((24, 128), i32),
            pltpu.VMEM((128, 128), f32),
            pltpu.VMEM((128, 128), f32),
            pltpu.SemaphoreType.DMA(()),
        ]
    return pl.pallas_call(
        functools.partial(expand_kernel, chunk),
        out_shape=out_shape,
        in_specs=in_specs,
        out_specs=out_specs,
        scratch_shapes=[
            pltpu.VMEM((4 * wide * (cap + 1) + 1, 8, 128), f32),
            pltpu.VMEM((2, 3, 2, GROUP, 128), f32),
            *[pltpu.VMEM((2, 2, 8 * GROUP, 128), f32)] * 3,
            pltpu.SemaphoreType.DMA((4, wide)),
            *scratch,
        ],
        cost_estimate=pl.CostEstimate(
            flops=wide * (1 << 28), bytes_accessed=1 << 23, transcendentals=0
        ),
        compiler_params=pltpu.CompilerParams(vmem_limit_bytes=(20 if chunk else 60) << 20),
        name="expand",
    )(*routing, pts)


def gather_kernel(wide, *refs):
    arrived, outs = refs[:4], refs[4 : 4 + wide]
    held, banks, labels, names, sem, sems = refs[4 + wide :]
    cap = held.shape[2] - 1
    loads = [pltpu.make_async_copy(arrived[k], held.at[k], sems.at[k]) for k in range(4)]
    for load in loads:
        load.start()
    for n in range(wide):
        outs[n][...] = jnp.zeros(outs[n].shape, f32)
        for bank in range(3):
            banks[bank, n] = jnp.zeros(outs[n].shape, f32)
    for load in loads:
        load.wait()
    for k in range(4):
        for n in range(wide):
            labels[pl.ds(8 * (k * wide + n), 8), :] = held[k, n, cap].astype(i32)
    copy = pltpu.make_async_copy(labels, names, sem)
    copy.start()
    copy.wait()
    for k in range(4):
        most = names[8 * k * wide + 1, 0]
        for n in range(1, wide):
            most = jnp.maximum(most, names[8 * (k * wide + n) + 1, 0])

        def rows4(r, carry):
            for u in range(4):
                for n in range(wide):
                    slot = r * 4 + u
                    where = names[8 * (k * wide + n), slot]
                    if u:
                        banks[u - 1, n, where] = banks[u - 1, n, where] + held[k, n, slot]
                    else:
                        outs[n][where] = outs[n][where] + held[k, n, slot]
            return carry

        lax.fori_loop(0, (most + 3) // 4, rows4, 0)

    def join(i, carry):
        part = pl.ds(pl.multiple_of(i * 16, 16), 16)
        for n in range(wide):
            outs[n][part] = (outs[n][part] + banks[0, n, part]) + (
                banks[1, n, part] + banks[2, n, part]
            )
        return carry

    lax.fori_loop(0, (outs[0].shape[0] - 1) // 16, join, 0)


def gather(arrived, leaf_count):
    wide, rows = arrived[0].shape[:2]
    return pl.pallas_call(
        functools.partial(gather_kernel, wide),
        out_shape=[jax.ShapeDtypeStruct((leaf_count + 1, 8, 128), f32)] * wide,
        in_specs=[pl.BlockSpec(memory_space=pl.ANY)] * 4,
        out_specs=[VMEM] * wide,
        scratch_shapes=[
            pltpu.VMEM((4, wide, rows, 8, 128), f32),
            pltpu.VMEM((3, wide, leaf_count + 1, 8, 128), f32),
            pltpu.VMEM((32 * wide, 128), i32),
            pltpu.SMEM((32 * wide, 128), i32),
            pltpu.SemaphoreType.DMA(()),
            pltpu.SemaphoreType.DMA((4,)),
        ],
        cost_estimate=pl.CostEstimate(
            flops=wide * (1 << 26), bytes_accessed=wide << 22, transcendentals=0
        ),
        compiler_params=pltpu.CompilerParams(vmem_limit_bytes=(8 + 10 * wide) << 20),
        name="gather",
    )(*arrived)


def rows_of(shape):
    return lax.broadcasted_iota(i32, shape, len(shape) - 2)


def swap_rows(t):
    even = rows_of(t.shape) % 2 == 0
    axis = len(t.shape) - 2
    return jnp.where(even, pltpu.roll(t, 7, axis), pltpu.roll(t, 1, axis))


def spin(t, cosine, sine):
    return t * cosine + swap_rows(t) * sine


def row_mix(t, maps, bit):
    flipped = pltpu.roll(t, 64, 2)
    total = None
    for step in range(4):
        for flip in range(2):
            part = flipped if flip else t
            if step:
                part = pltpu.roll(part, 8 - 2 * step, 1)
            term = part * maps[bit, 2 * step + flip]
            total = term if total is None else total + term
    return total


EARLY = 2

SEATS = 36


def turn(ca, sa, cb, sb):
    return ca * cb - sa * sb, sa * cb + ca * sb


def twice(c, s):
    return c * c - s * s, 2.0 * (s * c)


def phases_kernel(
    here, slots, boxes, cones, box_cones, cosine, sine, p0c, p0s, p1c, p1s, ec, es, goal,
    t0c, t0s, t1c, t1s, t2c, t2s,
):
    side = here[2]
    sign = jnp.where(rows_of((8, 128)) % 2 == 0, -1.0, 1.0)

    def cone_tables(n, carry):
        xs = [(cosine[n, v], sine[n, v]) for v in range(3)]
        wide = [
            tuple(jnp.broadcast_to(t[n, 3, pl.ds(v, 1), :], (8, 128)) for t in (cosine, sine))
            for v in range(5)
        ]
        t1c[n], t1s[n] = turn(*xs[2], *wide[4])
        xs2 = [twice(*x) for x in xs[:2]]
        for v in range(4):
            wide2 = twice(*wide[v])
            for bit in range(2):
                at = n * 8 + 4 * bit + v
                t0c[at], t0s[at] = turn(*xs[bit], *wide[v])
                t2c[at], t2s[at] = turn(*xs2[bit], *wide2)
        return carry

    lax.fori_loop(0, cosine.shape[0], cone_tables, 0)

    def child(j, carry):
        for o in range(8):
            p = slots[32 * o + j]
            e = cones[p] * 8 + o
            p0c[o, j] = t0c[e]
            p0s[o, j] = t0s[e] * sign
            owner = p >> 5
            goal[32 * o + j] = ((((owner & 1) ^ side) << 2) + (owner >> 1)) * SEATS + (p & 31)
            a = cones[8 * j + o]
            b = box_cones[boxes[32 * o + j]] * 8 + o
            c, s = turn(t1c[a], t1s[a], t2c[b], t2s[b])
            p1c[o, j] = c
            p1s[o, j] = s * sign
        return carry

    lax.fori_loop(0, 32, child, 0)
    me = 2 * here[3] + side
    for n in range(SEATS):
        if n < 32:
            a = cones[32 * me + n]
            c, s = t1c[a], t1s[a]
        else:
            a = box_cones[4 * me + n - 32]
            c, s = twice(t1c[a], t1s[a])
        ec[n] = c
        es[n] = s * sign


def lane_mix(t, both, octant):
    count = t.shape[0]
    flat = t.reshape(count * 8, 128)
    high = flat.astype(jnp.bfloat16)
    low = (flat - high.astype(f32)).astype(jnp.bfloat16)
    res = jnp.dot(
        jnp.concatenate([high, low], axis=1), both[octant % 4], preferred_element_type=f32
    )
    return (res[:, :128] + res[:, 128:]).reshape(count, 8, 128)


def levels_kernel(
    here, goal, boxes, a0, a1, a2, a3, p0c, p0s, p1c, p1s, both, rows, leaves, mine, other,
    held, turns, lanes_in, rows_in, solved, acc, upper, moved, sems, out_sems,
):
    count = leaves.shape[0]
    sums = [
        pltpu.make_async_copy(ref.at[pl.ds(0, count)], held.at[n], sems.at[n])
        for n, ref in enumerate((a0, a1, a2, a3))
    ]
    maps = [
        pltpu.make_async_copy(both, lanes_in, sems.at[4]),
        pltpu.make_async_copy(rows, rows_in, sems.at[5]),
    ]
    angles = [
        pltpu.make_async_copy(ref, turns.at[n], sems.at[6 + n])
        for n, ref in enumerate((p0c, p0s, p1c, p1s))
    ]
    for copy in sums + maps + angles:
        copy.start()
    acc[...] = jnp.zeros(acc.shape, f32)
    upper[...] = jnp.zeros(upper.shape, f32)
    for copy in sums:
        copy.wait()
    step = 16
    shape = (step, 8, 128)
    own = rows_of(shape) % 2 == lanes_of(shape) // 64

    def settle(n, carry):
        base = pl.multiple_of(n * step, step)
        t = (held[0, pl.ds(base, step)] + held[1, pl.ds(base, step)]) + (
            held[2, pl.ds(base, step)] + held[3, pl.ds(base, step)]
        )
        solved[pl.ds(base, step)] = jnp.where(own, t, swap_rows(pltpu.roll(t, 64, 2)))
        return carry

    lax.fori_loop(0, count // step, settle, 0)
    done = [pltpu.make_async_copy(solved, leaves, out_sems.at[8])]
    done[0].start()
    for copy in maps + angles[:2]:
        copy.wait()

    def spread(o, start, ref, spots):
        sums = [ref[spots[j]] + moved[o % 2, start + j] for j in range(8)]
        for j in range(8):
            ref[spots[j]] = sums[j]

    for o in range(8):
        for part in range(0, 32, 8):
            t = jnp.stack([solved[8 * (part + j) + o] for j in range(8)])
            t = spin(t, turns[0, o, part : part + 8], turns[1, o, part : part + 8])
            moved[o % 2, part : part + 8] = row_mix(lane_mix(t, lanes_in, o), rows_in, o // 4)
        for part in range(0, 32, 8):
            spread(o, part, acc, [goal[32 * o + part + j] for j in range(8)])

    apart = [here[2] * 4 * SEATS, (1 - here[2]) * 4 * SEATS]
    for copy in angles[2:]:
        copy.wait()
    for o in range(8):
        for part in range(0, 32, 8):
            tiles = []
            for j in range(8):
                p = 8 * (part + j) + o
                owner = p // 32
                tiles.append(acc[(owner // 2) * SEATS + p % 32 + apart[owner % 2]])
            t = spin(
                jnp.stack(tiles), turns[2, o, part : part + 8], turns[3, o, part : part + 8]
            )
            moved[o % 2, part : part + 8] = lane_mix(t, lanes_in, o)
        for part in range(0, 32, 8):
            spread(
                o, part, upper,
                [boxes[32 * o + part + j] + 32 * (o // 4) for j in range(8)],
            )
    for part in range(0, 32, 8):
        t = row_mix(upper[part : part + 8], rows_in, 0)
        t = t + row_mix(upper[32 + part : 40 + part], rows_in, 1)
        for j in range(8):
            q = part + j
            owner = q // 4
            acc[(owner // 2) * SEATS + 32 + q % 4 + apart[owner % 2]] = t[j]
    for k in range(4):
        z = (here[3] + k) % 4
        done += [
            pltpu.make_async_copy(
                acc.at[pl.ds((4 + z) * SEATS, SEATS)], other.at[k], out_sems.at[4 + k]
            ),
            pltpu.make_async_copy(acc.at[pl.ds(z * SEATS, SEATS)], mine.at[k], out_sems.at[k]),
        ]
    for copy in done[1:]:
        copy.start()
    for copy in done:
        copy.wait()


def close_kernel(g0, g1, g2, g3, ec, es, out_one, out_two):
    owned = out_one.shape[0]
    for n in range(SEATS):
        t = spin((g0[n] + g1[n]) + (g2[n] + g3[n]), ec[n], es[n])
        if n < owned:
            out_one[n] = t
        else:
            out_two[n - owned] = t


def cone_places():
    nodes = cheb_nodes()
    rows = np.arange(8)[:, None]
    lanes = np.arange(128)[None, :]
    a = 2 * (rows // 2) + lanes // 64
    out = np.zeros((3, 4, 8, 128))
    out[0, 0], out[0, 1], out[0, 2] = child_axis(0)[a], child_axis(1)[a], -nodes[a]
    b, c = np.arange(128) % 64 // 8, np.arange(128) % 8
    for v in range(4):
        out[1, 3, v], out[2, 3, v] = child_axis(v // 2)[b], child_axis(v % 2)[c]
    out[1, 3, 4], out[2, 3, 4] = -nodes[b], -nodes[c]
    return out.astype(np.float32)


def to_nodes(tiles):
    count = tiles.shape[0]
    return tiles.reshape(count, 4, 2, 128).transpose(0, 2, 1, 3).reshape(count, 2, 512)


def cone_vectors(cone_angles):
    azimuth = cone_angles[:, 0]
    polar = cone_angles[:, 1]
    return jnp.stack(
        [jnp.cos(azimuth) * jnp.sin(polar), jnp.sin(azimuth) * jnp.sin(polar), jnp.cos(polar)],
        axis=1,
    )


def hop(x, shift, leg, groups):
    pairs = []
    for s in range(16):
        for g in range(groups):
            y, x0 = s // 4, s % 4
            if g % 2 == leg:
                x0 = (x0 + shift) % 4
            else:
                y = (y + shift) % 4
            pairs.append((s * groups + g, (4 * y + x0) * groups + g))
    return lax.ppermute(x, ("sfc", "grp"), pairs)


def around(x, shift, groups):
    pairs = [(g, (g + 2 * shift) % groups) for g in range(groups)]
    return lax.ppermute(x, "grp", pairs)


def after(value, *others):
    return lax.optimization_barrier((value, *others))[0]


def per_device(
    bin_points, bin_plan, bin_leaf, leaf_slots, box_slots, parent_cone, box_cone, cone_angles
):
    groups = lax.axis_size("grp")
    rank = lax.axis_index("grp")
    cap = bin_points.shape[0] // 8
    leaf_count = leaf_slots.shape[2] * 8
    first_owned = parent_cone.shape[1] // groups
    second_owned = box_cone.shape[1] // groups
    tile = jax.ShapeDtypeStruct((8, 128), f32)

    def tiles(*lead):
        return jax.ShapeDtypeStruct((*lead, *tile.shape), f32)

    me = lax.axis_index("sfc")
    here = jnp.stack([me % 4, me // 4, rank % 2, rank // 2]).astype(i32)
    bins, _, width = bin_points.shape
    pts = jnp.transpose(bin_points.reshape(bins // 8, 8, 5, width // 128, 128), (2, 0, 3, 1, 4))
    pts = pts.reshape(-1, 128)
    arrived = []
    routing = (here, bin_plan.reshape(bins // 128, 128), bin_leaf.reshape(bins // 128, 128))
    held = [None] * 4
    last = None

    def collect(c, last):
        got = [after(arrived[c][0], last)] + arrived[c][1:]
        sums = gather(got, leaf_count)
        for m, part in zip(CHUNKS[c], sums):
            held[m] = hop(part, m, 1, groups) if m else part
        return sums[0]

    for c in range(len(CHUNKS)):
        sent = expand(c, routing, pts, cap)
        if not c:
            *sent, table, labels = sent
            table = table.reshape(-1)
        last = sent[0]
        moved = [sent[0]]
        for k in (2, 1, 3):
            moved.append(hop(sent[k], k, 0, groups))
        arrived.append(moved)
        if c >= EARLY and c + 1 < len(CHUNKS):
            last = collect(c - EARLY, last)
        table = after(table, last)
        routing = (table, labels)

    cone_angles = after(cone_angles, sent[0])
    directions = cone_vectors(cone_angles)
    places = jnp.asarray(cone_places())
    angle = (
        directions[:, 0, None, None, None] * places[None, 0]
        + directions[:, 1, None, None, None] * places[None, 1]
        + directions[:, 2, None, None, None] * places[None, 2]
    ) * kappa_leaf
    make_phases = pl.pallas_call(
        phases_kernel,
        out_shape=(tiles(8, 32),) * 4 + (tiles(SEATS),) * 2 + (jax.ShapeDtypeStruct((256,), i32),),
        in_specs=[SMEM] * 5 + [VMEM] * 2,
        out_specs=(VMEM,) * 6 + (SMEM,),
        scratch_shapes=[pltpu.VMEM((n, 8, 128), f32) for n in (128, 128, 16, 16, 128, 128)],
        compiler_params=pltpu.CompilerParams(vmem_limit_bytes=16 << 20),
        name="phases",
    )
    slots, boxes = leaf_slots.reshape(-1), box_slots.reshape(-1)
    p0c, p0s, p1c, p1s, ec, es, goal = make_phases(
        here, slots, boxes, parent_cone[0], box_cone[0], jnp.cos(angle), jnp.sin(angle)
    )

    for c in range(len(CHUNKS) - 1 - EARLY, len(CHUNKS)):
        last = collect(c, last)

    leaves, mine, other = pl.pallas_call(
        levels_kernel,
        out_shape=(tiles(leaf_count), tiles(4, SEATS), tiles(4, SEATS)),
        in_specs=[SMEM] * 3 + [ANY] * 10,
        out_specs=(ANY,) * 3,
        scratch_shapes=[
            pltpu.VMEM((4, leaf_count, 8, 128), f32),
            pltpu.VMEM((4, 8, 32, 8, 128), f32),
            pltpu.VMEM((4, 256, 256), jnp.bfloat16),
            pltpu.VMEM((2, 8, 8, 128), f32),
            pltpu.VMEM((leaf_count, 8, 128), f32),
            pltpu.VMEM((8 * SEATS, 8, 128), f32),
            pltpu.VMEM((64, 8, 128), f32),
            pltpu.VMEM((2, 32, 8, 128), f32),
            pltpu.SemaphoreType.DMA((10,)),
            pltpu.SemaphoreType.DMA((9,)),
        ],
        compiler_params=pltpu.CompilerParams(vmem_limit_bytes=20 << 20),
        name="levels",
    )(
        here, goal, boxes, *held, p0c, p0s, p1c, p1s,
        jnp.asarray(lane_maps()), jnp.asarray(row_maps()),
    )
    swapped = lax.ppermute(other, "grp", [(g, g ^ 1) for g in range(groups)])
    blocks = [mine[k] + swapped[k] for k in range(4)]
    got = [blocks[0]] + [around(blocks[k], k, groups) for k in (1, 2, 3)]
    one, two = pl.pallas_call(
        close_kernel,
        out_shape=(tiles(first_owned), tiles(second_owned)),
        in_specs=[VMEM] * 6,
        out_specs=(VMEM, VMEM),
        compiler_params=pltpu.CompilerParams(vmem_limit_bytes=8 << 20),
        name="close",
    )(*got, ec, es)
    return (to_nodes(leaves), to_nodes(one), to_nodes(two))


def solution(mesh):
    placed = (
        P(("sfc", "grp"), None, None),
        P(("sfc", "grp"), None),
        P(("sfc", "grp")),
        P("sfc", None, "grp"),
        P("sfc", None, None),
        P("sfc", None),
        P("sfc", None),
        P(),
    )

    return jax.shard_map(
        per_device,
        mesh=mesh,
        in_specs=placed,
        out_specs=(
            P(("sfc", "grp"), None, None),
            P(("sfc", "grp"), None, None),
            P(("sfc", "grp"), None, None),
        ),
        check_vma=False,
    )
```

```python
import functools

import jax
import jax.numpy as jnp
import numpy as np
from jax import lax
from jax.experimental import pallas as pl
from jax.experimental.pallas import tpu as pltpu
from jax.sharding import PartitionSpec as P

kappa_leaf = 2.0
f32 = jnp.float32
i32 = jnp.int32
VMEM = pl.BlockSpec(memory_space=pltpu.VMEM)
SMEM = pl.BlockSpec(memory_space=pltpu.SMEM)
ANY = pl.BlockSpec(memory_space=pl.ANY)


def cheb_nodes():
    return np.cos((2.0 * np.arange(8) + 1.0) * np.pi / 16.0)


def lagrange_np(values):
    nodes = cheb_nodes()
    rows = []
    for center in range(8):
        weight = np.ones_like(values)
        for other in range(8):
            if other != center:
                weight = weight * (values - nodes[other]) / (nodes[center] - nodes[other])
        rows.append(weight)
    return np.stack(rows, axis=0)


def child_axis(bit):
    return 0.5 * (2 * bit - 1) + 0.5 * cheb_nodes()


def axis_maps():
    return np.stack([lagrange_np(child_axis(bit)) for bit in range(2)])


def lane_maps():
    maps = axis_maps()
    out = []
    for pick in range(4):
        both = np.kron(maps[pick // 2], maps[pick % 2])
        full = np.kron(np.eye(2), both).T
        high = full.astype(jnp.bfloat16)
        low = (full - high.astype(np.float64)).astype(jnp.bfloat16)
        out.append(np.block([[high, low], [high, np.zeros_like(low)]]))
    return np.stack(out).astype(jnp.bfloat16)


def row_maps():
    maps = axis_maps()
    rows = np.arange(8)[:, None]
    half = np.arange(128)[None, :] // 64
    k = rows // 2
    out = np.zeros((2, 8, 8, 128), np.float32)
    for bit in range(2):
        for step in range(4):
            for flip in range(2):
                to = 2 * k + half
                frm = 2 * ((k + step) % 4) + (half ^ flip)
                out[bit, 2 * step + flip] = maps[bit][to, frm]
    return out


def basis(x):
    t = cheb_nodes()[:4]
    sq = t * t
    x2 = x * x
    s = [x2 - float(v) for v in sq]
    p01 = s[0] * s[1]
    p23 = s[2] * s[3]
    rest = [s[1] * p23, s[0] * p23, p01 * s[3], p01 * s[2]]
    out = [None] * 8
    for j in range(4):
        scale = 1.0 / (np.prod([sq[j] - sq[i] for i in range(4) if i != j]) * 2.0 * t[j])
        q = rest[j] * float(scale)
        out[j] = q * (x + float(t[j]))
        out[7 - j] = q * (float(t[j]) - x)
    return out


def lanes_of(shape):
    return lax.broadcasted_iota(i32, shape, len(shape) - 1)


def lanes_of(shape):
    return lax.broadcasted_iota(i32, shape, len(shape) - 1)


CHUNKS = ((2,), (1,), (3,), (0,))
ORDER = tuple(m for chunk in CHUNKS for m in chunk)


def route(here, plan, leaf, table, labels, picked, scaled):
    bf16 = jnp.bfloat16
    cap = labels.shape[2]
    target = plan[...]
    names = leaf[...].astype(f32)
    along_x = (target - here[0]) % 4
    along_y = (target // 4 - here[1]) % 4
    first = jnp.where(here[2] == 0, along_x, along_y)
    second = jnp.where(here[2] == 0, along_y, along_x)
    place, lead, width, part_of = target * 0, target * 0, target * 0, target * 0
    for c, chunk in enumerate(CHUNKS):
        for n, m in enumerate(chunk):
            hit = second == m
            place = jnp.where(hit, ORDER.index(m), place)
            part_of = jnp.where(hit, c, part_of)
            lead = jnp.where(hit, n, lead)
            width = jnp.where(hit, len(chunk), width)
    code = place * 4 + first
    for d in range(16):
        hit = (code == d).astype(f32)
        picked[pl.ds(8 * d, 8), :] = hit
        scaled[pl.ds(8 * d, 8), :] = hit * names
    square = (128, 128)
    row, lane = rows_of(square), lanes_of(square)
    hits = picked[...].astype(bf16)
    ones = jnp.ones(square, bf16)

    def mul(a, b):
        return jnp.dot(a.astype(bf16), b.astype(bf16), preferred_element_type=f32)

    inside = mul(hits, (row < lane).astype(f32))
    ahead = mul(mul((lane < row).astype(f32), hits), ones)
    same = mul(mul(((lane < row) & (lane // 8 == row // 8)).astype(f32), hits), ones)
    order = jnp.zeros((8, 128), f32)
    slot = jnp.zeros((8, 128), f32)
    for d in range(16):
        part = slice(8 * d, 8 * d + 8)
        hit = picked[pl.ds(8 * d, 8), :]
        order = order + hit * (inside[part] + ahead[part])
        slot = slot + hit * (inside[part] + same[part])
    count = ENTRIES
    lane_w = lanes_of((1, count))
    spans = jnp.zeros((1, count), f32)
    start = jnp.zeros((1, 1), f32)
    before = jnp.zeros((1, 1), f32)
    for c in range(len(CHUNKS)):
        size = jnp.sum((part_of == c).astype(f32), keepdims=True)
        groups = jnp.floor((size + float(GROUP - 1)) * (1.0 / GROUP))
        spans = jnp.where(lane_w == 2 * c, jnp.broadcast_to(start, (1, count)), spans)
        spans = jnp.where(lane_w == 2 * c + 1, jnp.broadcast_to(groups, (1, count)), spans)
        order = order + jnp.where(
            part_of == c, jnp.broadcast_to(start - before, order.shape), 0.0
        )
        start = start + groups * float(GROUP)
        before = before + size
    goal_hi = (first * width + lead).astype(f32)
    ranks = lax.broadcasted_iota(i32, (count, 128), 0).astype(f32)
    seats = row.astype(f32)
    sub = lax.broadcasted_iota(i32, (8, 128), 0)
    lane_f = lanes_of((8, 128)).astype(f32)
    found = jnp.zeros((8, count), f32)
    marks = jnp.zeros((32, 128), f32)
    nt = (((1,), (1,)), ((), ()))
    for r in range(8):
        at = jnp.broadcast_to(order[r : r + 1, :], (count, 128)) == ranks
        goal = jnp.broadcast_to(goal_hi[r : r + 1, :], (8, 128))
        seat = jnp.broadcast_to(slot[r : r + 1, :], (8, 128))
        values = jnp.where(
            sub == 0, 2.0 * lane_f - (lanes_of((8, 128)) % 8).astype(f32),
            jnp.where(sub == 1, float(r), jnp.where(sub == 2, goal, jnp.where(sub == 3, seat, 1.0))),
        )
        found = found + lax.dot_general(
            values.astype(bf16), at.astype(f32).astype(bf16), nt, preferred_element_type=f32
        )
        both = jnp.concatenate(
            [scaled[pl.ds(r, 16, stride=8), :], picked[pl.ds(r, 16, stride=8), :]], axis=0
        )
        sits = jnp.broadcast_to(slot[r : r + 1, :], square) == seats
        marks = marks + lax.dot_general(
            both.astype(bf16), sits.astype(f32).astype(bf16), nt, preferred_element_type=f32
        )
    lines = (found[0:1] + found[1:2] * 256.0).astype(i32)
    goals = (found[2:3] * float(cap_rows(cap)) + found[3:4] + found[4:5]).astype(i32)
    for n, values in enumerate((lines, goals)):
        for r in range(count // 128):
            at = n * (count // 128) + r
            table[at : at + 1, :] = values[:, 128 * r : 128 * r + 128]
    at = 2 * (count // 128)
    table[at : at + 1, :] = spans[:, :128].astype(i32)
    label = marks[:16] + 256.0 * (1.0 - marks[16:])
    for d in range(16):
        total = jnp.sum(marks[16 + d : 17 + d], axis=1, keepdims=True)
        labels[d] = jnp.where(
            sub == 0,
            jnp.broadcast_to(label[d : d + 1], (8, 128)),
            jnp.broadcast_to(total, (8, 128)),
        )


def cap_rows(cap):
    return cap + 1


GROUP = 16
ENTRIES = 1152


def expand_kernel(chunk, *refs):
    if chunk:
        table, labels, pts, *refs = refs
    else:
        here, plan, leaf, pts, *refs = refs
    outs, refs = refs[:4], refs[4:]
    if not chunk:
        listed, labels, *refs = refs
    held, stage, bx, by, bz, sems, *refs = refs
    if chunk:
        all_pts = pts
    else:
        all_pts, load_sems, *refs = refs
    first = sum(len(c) for c in CHUNKS[:chunk])
    wide = len(CHUNKS[chunk])
    rows = outs[0].shape[1]
    cap = rows - 1
    span = all_pts.shape[0] // 5
    loads = [
        pltpu.make_async_copy(
            pts.at[pl.ds(span * axis, span)], all_pts.at[pl.ds(span * axis, span)],
            load_sems.at[axis],
        )
        for axis in range(0 if chunk else 5)
    ]
    for load in loads:
        load.start()
    if not chunk:
        table, picked, scaled, sem = refs
        route(here, plan, leaf, listed, labels, picked, scaled)
        copy = pltpu.make_async_copy(listed, table, sem)
        copy.start()
        copy.wait()

    def look(base, which, u=0):
        if chunk:
            return table[base + (which * ENTRIES + u)]
        return table[(base >> 7) + which * (ENTRIES // 128), (base & 127) + u]

    for k in range(4):
        for n in range(wide):
            held[1 + (k * wide + n) * rows + cap] = labels[4 * (first + n) + k]
    begin = look(i32(0), 2, 2 * chunk)
    trips = look(i32(0), 2, 2 * chunk + 1)
    for load in loads:
        load.wait()

    def fetch(g, u, bank):
        line = look(begin + g * GROUP, 0, u)
        for axis in range(3):
            for h in range(2):
                stage[bank, axis, h, pl.ds(u, 1), :] = all_pts[
                    pl.ds(line + (span * axis + 8 * h), 1), :
                ]

    def tabulate(piece, bank):
        u, h, axis = 8 * (piece // 6), piece // 3 % 2, piece % 3
        values = basis(stage[bank, axis, h, pl.ds(u, 8), :])
        for a in range(8):
            if axis == 1:
                by[bank, h, pl.ds(GROUP * a + u, 8), :] = values[a]
            else:
                ref = bz if axis else bx
                ref[bank, h, pl.ds(8 * u + a, 8, stride=8), :] = values[a]

    def consume(g, u, bank):
        base = begin + g * GROUP
        line = look(base, 0, u)
        weighted, pair = [], []
        for h in range(2):
            lx = bx[bank, h, pl.ds(8 * u, 8), :]
            lz = bz[bank, h, pl.ds(8 * u, 8), :]
            re, im = (
                jnp.broadcast_to(
                    all_pts[pl.ds(line + (span * (3 + part) + 8 * h), 1), :], lx.shape
                )
                for part in range(2)
            )
            weighted.append(jnp.concatenate([re * lx, im * lx], axis=0).astype(jnp.bfloat16))
            pair.append(
                jnp.concatenate(
                    [
                        jnp.broadcast_to(by[bank, h, pl.ds(GROUP * b + u, 1), :], lz.shape) * lz
                        for b in range(8)
                    ],
                    axis=0,
                ).astype(jnp.bfloat16)
            )
        res = lax.dot_general(
            jnp.concatenate(weighted, axis=1),
            jnp.concatenate(pair, axis=1),
            (((1,), (1,)), ((), ())),
            preferred_element_type=f32,
        )
        held[look(base, 1, u)] = jnp.concatenate([res[:8], res[8:]], axis=1)

    pieces = 6 * GROUP // 8
    for u in range(GROUP):
        fetch(0, u, 0)
    for piece in range(pieces):
        tabulate(piece, 0)
    for u in range(GROUP):
        fetch(1, u, 1)

    def step(g, carry):
        bank = g & 1
        for u in range(GROUP):
            consume(g, u, bank)
            if u % 4 == 3:
                for piece in range(3 * (u // 4), 3 * (u // 4) + 3):
                    tabulate(piece, 1 - bank)
                for v in range(u - 3, u + 1):
                    fetch(g + 2, v, bank)
        return carry

    lax.fori_loop(0, trips, step, 0)
    copies = []
    for k in range(4):
        for n in range(wide):
            copies.append(
                pltpu.make_async_copy(
                    held.at[pl.ds(1 + (k * wide + n) * rows, rows)], outs[k].at[n], sems.at[k, n]
                )
            )
    for copy in copies:
        copy.start()
    for copy in copies:
        copy.wait()


def expand(chunk, routing, pts, cap):
    wide = len(CHUNKS[chunk])
    out_shape = [jax.ShapeDtypeStruct((wide, cap + 1, 8, 128), f32)] * 4
    out_specs = [ANY] * 4
    scratch = []
    if chunk:
        in_specs = [SMEM, VMEM, VMEM]
    else:
        in_specs = [SMEM, VMEM, VMEM, pl.BlockSpec(memory_space=pltpu.HBM)]
        out_shape += [
            jax.ShapeDtypeStruct((24, 128), i32),
            jax.ShapeDtypeStruct((16, 8, 128), f32),
        ]
        out_specs += [VMEM] * 2
        scratch = [
            pltpu.VMEM(pts.shape, f32),
            pltpu.SemaphoreType.DMA((5,)),
            pltpu.SMEM((24, 128), i32),
            pltpu.VMEM((128, 128), f32),
            pltpu.VMEM((128, 128), f32),
            pltpu.SemaphoreType.DMA(()),
        ]
    return pl.pallas_call(
        functools.partial(expand_kernel, chunk),
        out_shape=out_shape,
        in_specs=in_specs,
        out_specs=out_specs,
        scratch_shapes=[
            pltpu.VMEM((4 * wide * (cap + 1) + 1, 8, 128), f32),
            pltpu.VMEM((2, 3, 2, GROUP, 128), f32),
            *[pltpu.VMEM((2, 2, 8 * GROUP, 128), f32)] * 3,
            pltpu.SemaphoreType.DMA((4, wide)),
            *scratch,
        ],
        cost_estimate=pl.CostEstimate(
            flops=wide * (1 << 28), bytes_accessed=1 << 23, transcendentals=0
        ),
        compiler_params=pltpu.CompilerParams(vmem_limit_bytes=20 << 20),
        name="expand",
    )(*routing, pts)


def gather_kernel(wide, *refs):
    arrived, outs = refs[:4], refs[4 : 4 + wide]
    held, banks, labels, names, sem, sems = refs[4 + wide :]
    cap = held.shape[2] - 1
    loads = [pltpu.make_async_copy(arrived[k], held.at[k], sems.at[k]) for k in range(4)]
    for load in loads:
        load.start()
    for n in range(wide):
        outs[n][...] = jnp.zeros(outs[n].shape, f32)
        for bank in range(3):
            banks[bank, n] = jnp.zeros(outs[n].shape, f32)
    for load in loads:
        load.wait()
    for k in range(4):
        for n in range(wide):
            labels[pl.ds(8 * (k * wide + n), 8), :] = held[k, n, cap].astype(i32)
    copy = pltpu.make_async_copy(labels, names, sem)
    copy.start()
    copy.wait()
    for k in range(4):
        most = names[8 * k * wide + 1, 0]
        for n in range(1, wide):
            most = jnp.maximum(most, names[8 * (k * wide + n) + 1, 0])

        def rows4(r, carry):
            for u in range(4):
                for n in range(wide):
                    slot = r * 4 + u
                    where = names[8 * (k * wide + n), slot]
                    if u:
                        banks[u - 1, n, where] = banks[u - 1, n, where] + held[k, n, slot]
                    else:
                        outs[n][where] = outs[n][where] + held[k, n, slot]
            return carry

        lax.fori_loop(0, (most + 3) // 4, rows4, 0)

    def join(i, carry):
        part = pl.ds(pl.multiple_of(i * 16, 16), 16)
        for n in range(wide):
            outs[n][part] = (outs[n][part] + banks[0, n, part]) + (
                banks[1, n, part] + banks[2, n, part]
            )
        return carry

    lax.fori_loop(0, (outs[0].shape[0] - 1) // 16, join, 0)


def gather(arrived, leaf_count):
    wide, rows = arrived[0].shape[:2]
    return pl.pallas_call(
        functools.partial(gather_kernel, wide),
        out_shape=[jax.ShapeDtypeStruct((leaf_count + 1, 8, 128), f32)] * wide,
        in_specs=[pl.BlockSpec(memory_space=pl.ANY)] * 4,
        out_specs=[VMEM] * wide,
        scratch_shapes=[
            pltpu.VMEM((4, wide, rows, 8, 128), f32),
            pltpu.VMEM((3, wide, leaf_count + 1, 8, 128), f32),
            pltpu.VMEM((32 * wide, 128), i32),
            pltpu.SMEM((32 * wide, 128), i32),
            pltpu.SemaphoreType.DMA(()),
            pltpu.SemaphoreType.DMA((4,)),
        ],
        cost_estimate=pl.CostEstimate(
            flops=wide * (1 << 26), bytes_accessed=wide << 22, transcendentals=0
        ),
        compiler_params=pltpu.CompilerParams(vmem_limit_bytes=(8 + 10 * wide) << 20),
        name="gather",
    )(*arrived)


def rows_of(shape):
    return lax.broadcasted_iota(i32, shape, len(shape) - 2)


def swap_rows(t):
    even = rows_of(t.shape) % 2 == 0
    axis = len(t.shape) - 2
    return jnp.where(even, pltpu.roll(t, 7, axis), pltpu.roll(t, 1, axis))


def spin(t, cosine, sine):
    return t * cosine + swap_rows(t) * sine


def row_mix(t, maps, bit):
    flipped = pltpu.roll(t, 64, 2)
    total = None
    for step in range(4):
        for flip in range(2):
            part = flipped if flip else t
            if step:
                part = pltpu.roll(part, 8 - 2 * step, 1)
            term = part * maps[bit, 2 * step + flip]
            total = term if total is None else total + term
    return total


EARLY = 3

SEATS = 36


def turn(ca, sa, cb, sb):
    return ca * cb - sa * sb, sa * cb + ca * sb


def twice(c, s):
    return c * c - s * s, 2.0 * (s * c)


def phases_kernel(
    here, slots, boxes, cones, box_cones, cosine, sine, p0c, p0s, p1c, p1s, ec, es, goal,
    t0c, t0s, t1c, t1s, t2c, t2s,
):
    side = here[2]
    sign = jnp.where(rows_of((8, 128)) % 2 == 0, -1.0, 1.0)

    def cone_tables(n, carry):
        xs = [(cosine[n, v], sine[n, v]) for v in range(3)]
        wide = [
            tuple(jnp.broadcast_to(t[n, 3, pl.ds(v, 1), :], (8, 128)) for t in (cosine, sine))
            for v in range(5)
        ]
        t1c[n], t1s[n] = turn(*xs[2], *wide[4])
        xs2 = [twice(*x) for x in xs[:2]]
        for v in range(4):
            wide2 = twice(*wide[v])
            for bit in range(2):
                at = n * 8 + 4 * bit + v
                t0c[at], t0s[at] = turn(*xs[bit], *wide[v])
                t2c[at], t2s[at] = turn(*xs2[bit], *wide2)
        return carry

    lax.fori_loop(0, cosine.shape[0], cone_tables, 0)

    def child(j, carry):
        for o in range(8):
            p = slots[32 * o + j]
            e = cones[p] * 8 + o
            p0c[o, j] = t0c[e]
            p0s[o, j] = t0s[e] * sign
            owner = p >> 5
            goal[32 * o + j] = ((((owner & 1) ^ side) << 2) + (owner >> 1)) * SEATS + (p & 31)
            a = cones[8 * j + o]
            b = box_cones[boxes[32 * o + j]] * 8 + o
            c, s = turn(t1c[a], t1s[a], t2c[b], t2s[b])
            p1c[o, j] = c
            p1s[o, j] = s * sign
        return carry

    lax.fori_loop(0, 32, child, 0)
    me = 2 * here[3] + side
    for n in range(SEATS):
        if n < 32:
            a = cones[32 * me + n]
            c, s = t1c[a], t1s[a]
        else:
            a = box_cones[4 * me + n - 32]
            c, s = twice(t1c[a], t1s[a])
        ec[n] = c
        es[n] = s * sign


def lane_mix(t, both, octant):
    count = t.shape[0]
    flat = t.reshape(count * 8, 128)
    high = flat.astype(jnp.bfloat16)
    low = (flat - high.astype(f32)).astype(jnp.bfloat16)
    res = jnp.dot(
        jnp.concatenate([high, low], axis=1), both[octant % 4], preferred_element_type=f32
    )
    return (res[:, :128] + res[:, 128:]).reshape(count, 8, 128)


def levels_kernel(
    here, goal, boxes, a0, a1, a2, a3, p0c, p0s, p1c, p1s, both, rows, leaves, mine, other,
    held, turns, lanes_in, rows_in, solved, acc, upper, moved, sems, out_sems,
):
    count = leaves.shape[0]
    sums = [
        pltpu.make_async_copy(ref.at[pl.ds(0, count)], held.at[n], sems.at[n])
        for n, ref in enumerate((a0, a1, a2, a3))
    ]
    maps = [
        pltpu.make_async_copy(both, lanes_in, sems.at[4]),
        pltpu.make_async_copy(rows, rows_in, sems.at[5]),
    ]
    angles = [
        pltpu.make_async_copy(ref, turns.at[n], sems.at[6 + n])
        for n, ref in enumerate((p0c, p0s, p1c, p1s))
    ]
    for copy in sums + maps + angles:
        copy.start()
    acc[...] = jnp.zeros(acc.shape, f32)
    upper[...] = jnp.zeros(upper.shape, f32)
    for copy in sums:
        copy.wait()
    step = 16
    shape = (step, 8, 128)
    own = rows_of(shape) % 2 == lanes_of(shape) // 64

    def settle(n, carry):
        base = pl.multiple_of(n * step, step)
        t = (held[0, pl.ds(base, step)] + held[1, pl.ds(base, step)]) + (
            held[2, pl.ds(base, step)] + held[3, pl.ds(base, step)]
        )
        solved[pl.ds(base, step)] = jnp.where(own, t, swap_rows(pltpu.roll(t, 64, 2)))
        return carry

    lax.fori_loop(0, count // step, settle, 0)
    done = [pltpu.make_async_copy(solved, leaves, out_sems.at[8])]
    done[0].start()
    for copy in maps + angles[:2]:
        copy.wait()

    def spread(o, start, ref, spots):
        sums = [ref[spots[j]] + moved[o % 2, start + j] for j in range(8)]
        for j in range(8):
            ref[spots[j]] = sums[j]

    for o in range(8):
        for part in range(0, 32, 8):
            t = jnp.stack([solved[8 * (part + j) + o] for j in range(8)])
            t = spin(t, turns[0, o, part : part + 8], turns[1, o, part : part + 8])
            moved[o % 2, part : part + 8] = row_mix(lane_mix(t, lanes_in, o), rows_in, o // 4)
        for part in range(0, 32, 8):
            spread(o, part, acc, [goal[32 * o + part + j] for j in range(8)])

    apart = [here[2] * 4 * SEATS, (1 - here[2]) * 4 * SEATS]
    for copy in angles[2:]:
        copy.wait()
    for o in range(8):
        for part in range(0, 32, 8):
            tiles = []
            for j in range(8):
                p = 8 * (part + j) + o
                owner = p // 32
                tiles.append(acc[(owner // 2) * SEATS + p % 32 + apart[owner % 2]])
            t = spin(
                jnp.stack(tiles), turns[2, o, part : part + 8], turns[3, o, part : part + 8]
            )
            moved[o % 2, part : part + 8] = lane_mix(t, lanes_in, o)
        for part in range(0, 32, 8):
            spread(
                o, part, upper,
                [boxes[32 * o + part + j] + 32 * (o // 4) for j in range(8)],
            )
    for part in range(0, 32, 8):
        t = row_mix(upper[part : part + 8], rows_in, 0)
        t = t + row_mix(upper[32 + part : 40 + part], rows_in, 1)
        for j in range(8):
            q = part + j
            owner = q // 4
            acc[(owner // 2) * SEATS + 32 + q % 4 + apart[owner % 2]] = t[j]
    for k in range(4):
        z = (here[3] + k) % 4
        done += [
            pltpu.make_async_copy(
                acc.at[pl.ds((4 + z) * SEATS, SEATS)], other.at[k], out_sems.at[4 + k]
            ),
            pltpu.make_async_copy(acc.at[pl.ds(z * SEATS, SEATS)], mine.at[k], out_sems.at[k]),
        ]
    for copy in done[1:]:
        copy.start()
    for copy in done:
        copy.wait()


def close_kernel(g0, g1, g2, g3, ec, es, out_one, out_two):
    owned = out_one.shape[0]
    for n in range(SEATS):
        t = spin((g0[n] + g1[n]) + (g2[n] + g3[n]), ec[n], es[n])
        if n < owned:
            out_one[n] = t
        else:
            out_two[n - owned] = t


def cone_places():
    nodes = cheb_nodes()
    rows = np.arange(8)[:, None]
    lanes = np.arange(128)[None, :]
    a = 2 * (rows // 2) + lanes // 64
    out = np.zeros((3, 4, 8, 128))
    out[0, 0], out[0, 1], out[0, 2] = child_axis(0)[a], child_axis(1)[a], -nodes[a]
    b, c = np.arange(128) % 64 // 8, np.arange(128) % 8
    for v in range(4):
        out[1, 3, v], out[2, 3, v] = child_axis(v // 2)[b], child_axis(v % 2)[c]
    out[1, 3, 4], out[2, 3, 4] = -nodes[b], -nodes[c]
    return out.astype(np.float32)


def to_nodes(tiles):
    count = tiles.shape[0]
    return tiles.reshape(count, 4, 2, 128).transpose(0, 2, 1, 3).reshape(count, 2, 512)


def cone_vectors(cone_angles):
    azimuth = cone_angles[:, 0]
    polar = cone_angles[:, 1]
    return jnp.stack(
        [jnp.cos(azimuth) * jnp.sin(polar), jnp.sin(azimuth) * jnp.sin(polar), jnp.cos(polar)],
        axis=1,
    )


def hop(x, shift, leg, groups):
    pairs = []
    for s in range(16):
        for g in range(groups):
            y, x0 = s // 4, s % 4
            if g % 2 == leg:
                x0 = (x0 + shift) % 4
            else:
                y = (y + shift) % 4
            pairs.append((s * groups + g, (4 * y + x0) * groups + g))
    return lax.ppermute(x, ("sfc", "grp"), pairs)


def around(x, shift, groups):
    pairs = [(g, (g + 2 * shift) % groups) for g in range(groups)]
    return lax.ppermute(x, "grp", pairs)


def after(value, *others):
    return lax.optimization_barrier((value, *others))[0]


def per_device(
    bin_points, bin_plan, bin_leaf, leaf_slots, box_slots, parent_cone, box_cone, cone_angles
):
    groups = lax.axis_size("grp")
    rank = lax.axis_index("grp")
    cap = bin_points.shape[0] // 8
    leaf_count = leaf_slots.shape[2] * 8
    first_owned = parent_cone.shape[1] // groups
    second_owned = box_cone.shape[1] // groups
    tile = jax.ShapeDtypeStruct((8, 128), f32)

    def tiles(*lead):
        return jax.ShapeDtypeStruct((*lead, *tile.shape), f32)

    me = lax.axis_index("sfc")
    here = jnp.stack([me % 4, me // 4, rank % 2, rank // 2]).astype(i32)
    bins, _, width = bin_points.shape
    pts = jnp.transpose(bin_points.reshape(bins // 8, 8, 5, width // 128, 128), (2, 0, 3, 1, 4))
    pts = pts.reshape(-1, 128)
    arrived = []
    routing = (here, bin_plan.reshape(bins // 128, 128), bin_leaf.reshape(bins // 128, 128))
    held = [None] * 4
    last = None

    def collect(c, last):
        got = [after(arrived[c][0], last)] + arrived[c][1:]
        sums = gather(got, leaf_count)
        for m, part in zip(CHUNKS[c], sums):
            held[m] = hop(part, m, 1, groups) if m else part
        return sums[0]

    for c in range(len(CHUNKS)):
        sent = expand(c, routing, pts, cap)
        if not c:
            *sent, table, labels = sent
            table = table.reshape(-1)
        last = sent[0]
        moved = [sent[0]]
        for k in (2, 1, 3):
            moved.append(hop(sent[k], k, 0, groups))
        arrived.append(moved)
        if c >= EARLY and c + 1 < len(CHUNKS):
            last = collect(c - EARLY, last)
        table = after(table, last)
        routing = (table, labels)

    cone_angles = after(cone_angles, sent[0])
    directions = cone_vectors(cone_angles)
    places = jnp.asarray(cone_places())
    angle = (
        directions[:, 0, None, None, None] * places[None, 0]
        + directions[:, 1, None, None, None] * places[None, 1]
        + directions[:, 2, None, None, None] * places[None, 2]
    ) * kappa_leaf
    make_phases = pl.pallas_call(
        phases_kernel,
        out_shape=(tiles(8, 32),) * 4 + (tiles(SEATS),) * 2 + (jax.ShapeDtypeStruct((256,), i32),),
        in_specs=[SMEM] * 5 + [VMEM] * 2,
        out_specs=(VMEM,) * 6 + (SMEM,),
        scratch_shapes=[pltpu.VMEM((n, 8, 128), f32) for n in (128, 128, 16, 16, 128, 128)],
        compiler_params=pltpu.CompilerParams(vmem_limit_bytes=16 << 20),
        name="phases",
    )
    slots, boxes = leaf_slots.reshape(-1), box_slots.reshape(-1)
    p0c, p0s, p1c, p1s, ec, es, goal = make_phases(
        here, slots, boxes, parent_cone[0], box_cone[0], jnp.cos(angle), jnp.sin(angle)
    )

    for c in range(len(CHUNKS) - 1 - EARLY, len(CHUNKS)):
        last = collect(c, last)

    leaves, mine, other = pl.pallas_call(
        levels_kernel,
        out_shape=(tiles(leaf_count), tiles(4, SEATS), tiles(4, SEATS)),
        in_specs=[SMEM] * 3 + [ANY] * 10,
        out_specs=(ANY,) * 3,
        scratch_shapes=[
            pltpu.VMEM((4, leaf_count, 8, 128), f32),
            pltpu.VMEM((4, 8, 32, 8, 128), f32),
            pltpu.VMEM((4, 256, 256), jnp.bfloat16),
            pltpu.VMEM((2, 8, 8, 128), f32),
            pltpu.VMEM((leaf_count, 8, 128), f32),
            pltpu.VMEM((8 * SEATS, 8, 128), f32),
            pltpu.VMEM((64, 8, 128), f32),
            pltpu.VMEM((2, 32, 8, 128), f32),
            pltpu.SemaphoreType.DMA((10,)),
            pltpu.SemaphoreType.DMA((9,)),
        ],
        compiler_params=pltpu.CompilerParams(vmem_limit_bytes=20 << 20),
        name="levels",
    )(
        here, goal, boxes, *held, p0c, p0s, p1c, p1s,
        jnp.asarray(lane_maps()), jnp.asarray(row_maps()),
    )
    swapped = lax.ppermute(other, "grp", [(g, g ^ 1) for g in range(groups)])
    blocks = [mine[k] + swapped[k] for k in range(4)]
    got = [blocks[0]] + [around(blocks[k], k, groups) for k in (1, 2, 3)]
    one, two = pl.pallas_call(
        close_kernel,
        out_shape=(tiles(first_owned), tiles(second_owned)),
        in_specs=[VMEM] * 6,
        out_specs=(VMEM, VMEM),
        compiler_params=pltpu.CompilerParams(vmem_limit_bytes=8 << 20),
        name="close",
    )(*got, ec, es)
    return (to_nodes(leaves), to_nodes(one), to_nodes(two))


def solution(mesh):
    placed = (
        P(("sfc", "grp"), None, None),
        P(("sfc", "grp"), None),
        P(("sfc", "grp")),
        P("sfc", None, "grp"),
        P("sfc", None, None),
        P("sfc", None),
        P("sfc", None),
        P(),
    )

    return jax.shard_map(
        per_device,
        mesh=mesh,
        in_specs=placed,
        out_specs=(
            P(("sfc", "grp"), None, None),
            P(("sfc", "grp"), None, None),
            P(("sfc", "grp"), None, None),
        ),
        check_vma=False,
    )
```
